32 devices in a mesh: groups: 2 (over x), seq: 16 (over z, y, core).
Axes of the slice: x: 2, y: 2, z: 4, core: 2. Of those that a mesh axis runs over, the one named last changes fastest.
Arguments:
- signal: bfloat16 [8192, 2048], P(('groups', 'seq')), parts along dimension 0, may hold values from -6 to 6
- input_gate: bfloat16 [8192, 2048], P(('groups', 'seq')), parts along dimension 0, may hold values from -6 to 6
- output_gate: bfloat16 [8192, 2048], P(('groups', 'seq')), parts along dimension 0, may hold values from -6 to 6
- filter_spectrum: float32 [2, 128, 64, 2048], P(None, 'seq'), may hold values from -6 to 6
- skip_gain: float32 [2048], replicated, may hold values from -1 to 1
Outputs:
- mixed_out: bfloat16 [8192, 2048], P(('groups', 'seq')), parts along dimension 0
The draws below stay inside these ranges and needn't reach their ends.
There are 2 independent parts, one for each index of `groups`. The reference program is written for one: setup_inputs(seed, part) draws one part's arguments, and reference() takes and returns one part's arrays. A program takes and returns all parts, laid end to end along the dimension named above; an argument that names none is the same for every part. Nothing has to cross between parts.
All inputs are finite; a program needn't handle non-finite values.
Results may differ from the reference program's by a relative error of at most 0.005.
Values may be sent and summed in bfloat16 or wider, within the bound.
No kernel may reach another device: no remote copies, remote signals or barrier semaphores. Data moves between devices by JAX's collectives and lax.ppermute only.
A program may use at most 128 MiB of HBM per device.

```python
import jax
import jax.numpy as jnp
from jax import lax

CHANNELS = 2048
SEQ_LEN = 4096
FFT_LEN = 8192
FREQ_LOW = 128
FREQ_HIGH = 64


def levels(stream_key, shape, pieces, least, high):
    def one(axis_at, parts):
        steps = jax.random.uniform(jax.random.fold_in(jax.random.fold_in(stream_key, 6), axis_at), (parts,), jnp.float32, least / len(pieces), high / len(pieces))
        return jnp.repeat(jnp.exp(steps), shape[axis_at] // parts).reshape((-1,) + (1,) * (len(shape) - axis_at - 1))

    loudness = one(*pieces[0])
    for cut in pieces[1:]:
        loudness = loudness * one(*cut)
    return loudness


def bell_draw(key, shape, width, bound, split=(), held_as=jnp.bfloat16):
    result = width * jax.random.normal(key, shape, jnp.float32)
    if split:
        result = result * levels(key, shape, split, -0.22, 0.18)
    return jnp.clip(result, -bound, bound).astype(held_as)


def setup_inputs(seed: int = 0, part: int = 0) -> dict:
    key_of = jax.random.split(jax.random.key(seed), 6)
    part_splits = jax.random.split(jax.random.fold_in(key_of[5], part), 6)
    return {
        "signal": bell_draw(part_splits[0], (SEQ_LEN, CHANNELS), 1.0, 6.0, ((0, 16),)),
        "input_gate": bell_draw(part_splits[1], (SEQ_LEN, CHANNELS), 1.0, 6.0, ((0, 16),)),
        "output_gate": bell_draw(part_splits[2], (SEQ_LEN, CHANNELS), 1.0, 6.0, ((0, 16),)),
        "filter_spectrum": bell_draw(key_of[3], (2, FREQ_LOW, FREQ_HIGH, CHANNELS), 1.0, 6.0, ((1, 16),), jnp.float32),
        "skip_gain": jnp.clip(jax.random.uniform(key_of[4], (CHANNELS,), jnp.float32, -1.0, 1.0), -1.0, 1.0),
    }


def reference(signal, input_gate, output_gate, filter_spectrum, skip_gain):
    gated_input = (input_gate.astype(jnp.float32) * signal.astype(jnp.float32)).astype(jnp.bfloat16)
    widened = gated_input.astype(jnp.float32)
    padded = jnp.concatenate([widened, jnp.zeros((SEQ_LEN, CHANNELS), widened.dtype)], axis=0)
    spectrum = jnp.fft.fft(padded, axis=0)
    response = lax.complex(filter_spectrum[0], filter_spectrum[1])
    response = jnp.transpose(response, (1, 0, 2)).reshape(FFT_LEN, CHANNELS)
    convolved = jnp.real(jnp.fft.ifft(spectrum * response, axis=0))[:SEQ_LEN]
    mixed_out = output_gate.astype(jnp.float32) * (convolved + skip_gain[None, :] * widened)
    return mixed_out.astype(jnp.bfloat16)
```

```python
import math

import jax
import jax.numpy as jnp
from jax import lax
from jax.sharding import PartitionSpec as P

EVERY = ("groups", "seq")


def angle_table(rows_count, cols_count, length):
    row_index = lax.iota(jnp.int32, rows_count)
    col_index = lax.iota(jnp.int32, cols_count)
    product = row_index[:, None] * col_index[None, :] % length
    angles = product.astype(jnp.float32) * (2.0 * math.pi / length)
    return (jnp.cos(angles), jnp.sin(angles))


def contract_first(matrix, values):
    return jnp.einsum("kn,nbc->kbc", matrix, values, precision=lax.Precision.HIGH)


def contract_second(matrix, values):
    return jnp.einsum("kn,anc->akc", matrix, values, precision=lax.Precision.HIGH)


def convolve(signal_rows, spectra_real, spectra_imag):
    half_rows, width, _ = signal_rows.shape
    full_rows = 2 * half_rows
    length = full_rows * width
    cos_one, sin_one = angle_table(full_rows, half_rows, full_rows)
    cos_two, sin_two = angle_table(width, width, width)
    turn_cos, turn_sin = angle_table(full_rows, width, length)
    turn_cos = turn_cos[:, :, None]
    turn_sin = turn_sin[:, :, None]
    first_real = contract_first(cos_one, signal_rows)
    first_imag = -contract_first(sin_one, signal_rows)
    twist_real = first_real * turn_cos + first_imag * turn_sin
    twist_imag = first_imag * turn_cos - first_real * turn_sin
    spec_real = contract_second(cos_two, twist_real) + contract_second(sin_two, twist_imag)
    spec_imag = contract_second(cos_two, twist_imag) - contract_second(sin_two, twist_real)
    prod_real = spec_real * spectra_real - spec_imag * spectra_imag
    prod_imag = spec_real * spectra_imag + spec_imag * spectra_real
    back_real = contract_second(cos_two, prod_real) - contract_second(sin_two, prod_imag)
    back_imag = contract_second(sin_two, prod_real) + contract_second(cos_two, prod_imag)
    rotated_real = back_real * turn_cos - back_imag * turn_sin
    rotated_imag = back_real * turn_sin + back_imag * turn_cos
    summed = contract_first(cos_one.T, rotated_real) - contract_first(sin_one.T, rotated_imag)
    return summed * (1.0 / length)


def exchange(values):
    return lax.all_to_all(values, EVERY, split_axis=0, concat_axis=0, tiled=True)


def on_device(signal, input_gate, output_gate, filter_spectrum, skip_gain):
    tok_rows, channels = signal.shape
    groups = lax.axis_size("groups")
    devices_seq = lax.axis_size("seq")
    parts = groups * devices_seq
    width = channels // parts
    low, high = filter_spectrum.shape[1:3]
    share = low // groups
    gated_input = (input_gate.astype(jnp.float32) * signal.astype(jnp.float32)).astype(jnp.bfloat16)

    sent = gated_input.reshape(tok_rows, parts, width).transpose(1, 0, 2).reshape(parts, -1, 128)
    got = exchange(sent).reshape(groups, devices_seq, tok_rows, width)
    rows = got.transpose(1, 2, 0, 3).reshape(-1, high, groups * width)

    mine = lax.dynamic_slice_in_dim(filter_spectrum, lax.axis_index("groups") * share, share, axis=1)
    mine = mine.astype(jnp.bfloat16).reshape(2, share, high, parts, width)
    mine = mine.transpose(3, 0, 1, 2, 4).reshape(parts, -1, 128)
    spectra = exchange(mine).reshape(groups, devices_seq, 2, share, high, width)
    spectra = spectra.transpose(2, 1, 0, 3, 4, 5).reshape(2, -1, high, 1, width)
    spectra = jnp.broadcast_to(spectra, spectra.shape[:3] + (groups, width))
    spectra = spectra.reshape(2, -1, high, groups * width).astype(jnp.float32)

    conv = convolve(rows.astype(jnp.float32), spectra[0], spectra[1]).astype(jnp.bfloat16)
    conv = conv.reshape(devices_seq, tok_rows, groups, width).transpose(2, 0, 1, 3)
    back = exchange(conv.reshape(parts, -1, 128)).reshape(parts, tok_rows, width)
    convolved = back.transpose(1, 0, 2).reshape(tok_rows, channels).astype(jnp.float32)
    mixed_out = output_gate.astype(jnp.float32) * (
        convolved + skip_gain[None, :] * gated_input.astype(jnp.float32)
    )
    return mixed_out.astype(jnp.bfloat16)


def solution(mesh):
    return jax.shard_map(
        on_device,
        mesh=mesh,
        in_specs=(P(EVERY, None), P(EVERY, None), P(EVERY, None), P(None, "seq", None, None), P()),
        out_specs=P(EVERY, None),
        check_vma=False,
    )
```

```python
import functools
import math

import jax
import jax.numpy as jnp
import ml_dtypes
import numpy as np
from jax import lax
from jax.experimental import pallas as pl
from jax.experimental.pallas import tpu as pltpu
from jax.sharding import PartitionSpec as P

EVERY = ("groups", "seq")
LANES = 128
HALF = LANES // 2
BF16 = jnp.bfloat16
F32 = jnp.float32


def exchange(values):
    return lax.all_to_all(values, EVERY, split_axis=0, concat_axis=0, tiled=True)


def left_lanes(rows):
    return lax.broadcasted_iota(jnp.int32, (rows, LANES), 1) < HALF


def swap_halves(first, second):
    left = left_lanes(first.shape[0])
    return (
        jnp.where(left, first, pltpu.roll(second, HALF, 1)),
        jnp.where(left, pltpu.roll(first, HALF, 1), second),
    )


def hi_lo(matrix):
    high = matrix.astype(ml_dtypes.bfloat16)
    low = (matrix - high.astype(np.float64)).astype(ml_dtypes.bfloat16)
    return high, low


@functools.lru_cache(None)
def tables(half_rows, width):
    full_rows = 2 * half_rows
    length = full_rows * width
    low_index = np.arange(half_rows)
    angle = 2 * np.pi * (np.outer(low_index, low_index) % full_rows) / full_rows
    real_part, imag_part = np.cos(angle), -np.sin(angle)
    imag_part[0] = 1.0 - 2.0 * (low_index % 2)
    first = np.concatenate([real_part, imag_part], 0)
    last = first.T / length
    inner = np.arange(width)
    angle = 2 * np.pi * (np.outer(inner, inner) % width) / width
    cosine, sine = np.cos(angle), np.sin(angle)
    second = np.block([[cosine, sine], [-sine, cosine]])
    third = np.block([[cosine, -sine], [sine, cosine]])
    first_hi, first_lo = hi_lo(first)
    second_hi, second_lo = hi_lo(second)
    third_hi, third_lo = hi_lo(third)
    last_hi, last_lo = hi_lo(last)
    turn = np.zeros((half_rows // 8 + 1, width, LANES), np.float32)
    for block in range(half_rows // 8 + 1):
        angle = 2 * np.pi * np.outer(inner, 8 * block + np.arange(8)) / length
        turn[block, :, :8] = np.cos(angle)
        turn[block, :, 8:16] = np.sin(angle)
    return (
        np.concatenate([first_hi, first_lo], 1),
        np.concatenate([second_hi, second_lo, second_hi], 1),
        np.concatenate([third_hi, third_lo], 1),
        np.concatenate([last_hi, last_lo], 1),
        turn,
    )


def pack_input_kernel(signal_ref, gate_ref, out_ref):
    rows = signal_ref.shape[0] // 2
    for block in range(signal_ref.shape[1] // LANES):
        lanes = pl.ds(block * LANES, LANES)
        gated = signal_ref[:, lanes].astype(F32) * gate_ref[:, lanes].astype(F32)
        first, second = swap_halves(gated[:rows], gated[rows:])
        out_ref[2 * block] = first.astype(BF16)
        out_ref[2 * block + 1] = second.astype(BF16)


def pack_input(signal, input_gate, parts):
    tok_rows, channels = signal.shape
    wide = 4 * LANES
    return pl.pallas_call(
        pack_input_kernel,
        out_shape=jax.ShapeDtypeStruct((parts, tok_rows // 2, LANES), BF16),
        grid=(channels // wide,),
        in_specs=[pl.BlockSpec((tok_rows, wide), lambda b: (0, b))] * 2,
        out_specs=pl.BlockSpec((8, tok_rows // 2, LANES), lambda b: (b, 0, 0)),
        cost_estimate=pl.CostEstimate(
            flops=signal.size, bytes_accessed=6 * signal.size, transcendentals=0
        ),
        name="pack_input",
    )(signal, input_gate)


def pack_filter_kernel(first_low_ref, filter_ref, out_ref, *, middle):
    share, width = filter_ref.shape[1:3]
    row = lax.broadcasted_iota(jnp.int32, (width, width), 0)
    col = lax.broadcasted_iota(jnp.int32, (width, width), 1)
    for low in range(share):
        mirrored = first_low_ref[1] + low > middle
        order = jnp.where(col == jnp.where(mirrored, width - 1 - row, row), 1.0, 0.0).astype(BF16)
        sign = jnp.where(mirrored, -1.0, 1.0).astype(F32)
        for block in range(filter_ref.shape[3] // LANES):
            lanes = pl.ds(block * LANES, LANES)
            both = jnp.concatenate(
                [filter_ref[0, low, :, lanes], filter_ref[1, low, :, lanes]], 1
            ).astype(BF16)
            both = jnp.dot(order, both, preferred_element_type=F32)
            first, second = swap_halves(both[:, :LANES], sign * both[:, LANES:])
            rows = pl.ds(low * width, width)
            out_ref[2 * block, rows, :] = first.astype(BF16)
            out_ref[2 * block + 1, rows, :] = second.astype(BF16)


def pack_filter(filter_spectrum, groups, devices_seq):
    _, low, width, channels = filter_spectrum.shape
    share = low // groups
    group = lax.axis_index("groups")
    first_low = lax.axis_index("seq") * low + group * share
    wide = 2 * LANES
    chunks = wide // HALF
    size = share * width * channels
    return pl.pallas_call(
        functools.partial(pack_filter_kernel, middle=low * devices_seq // 2),
        out_shape=jax.ShapeDtypeStruct((channels // HALF, share * width, LANES), BF16),
        grid_spec=pltpu.PrefetchScalarGridSpec(
            num_scalar_prefetch=1,
            grid=(channels // wide,),
            in_specs=[pl.BlockSpec((2, share, width, wide), lambda b, at: (0, at[0], 0, b))],
            out_specs=pl.BlockSpec((chunks, share * width, LANES), lambda b, at: (b, 0, 0)),
        ),
        cost_estimate=pl.CostEstimate(
            flops=4 * width * size, bytes_accessed=12 * size, transcendentals=0
        ),
        name="pack_filter",
    )(jnp.stack([group, first_low]), filter_spectrum)


def split_bf16(values):
    high = values.astype(BF16)
    return high, (values - high.astype(F32)).astype(BF16)


def forward_kernel(
    got_ref, first_ref, second_ref, turn_ref, out_ref, top_ref, rows_ref, stage_ref, *, devices_seq
):
    width = turn_ref.shape[1]
    half_rows = rows_ref.shape[0] // width
    full_rows = 2 * half_rows
    piece = got_ref.shape[1]
    for source in range(devices_seq):
        first, second = swap_halves(
            got_ref[source].astype(F32), got_ref[devices_seq + source].astype(F32)
        )
        rows_ref[pl.ds(2 * source * piece, piece), :] = first
        rows_ref[pl.ds((2 * source + 1) * piece, piece), :] = second
    first_matrix = first_ref[...]
    second_matrix = second_ref[...]

    def first_stage(step, carry):
        for u in range(0, 8, 2):
            pair = jnp.concatenate(
                [
                    rows_ref[pl.ds(8 * step + u + v, half_rows, stride=width), :].astype(BF16)
                    for v in range(2)
                ],
                1,
            )
            pair = jnp.concatenate([pair, pair], 0)
            done = jnp.dot(first_matrix, pair, preferred_element_type=F32)
            for v in range(2):
                at = pl.multiple_of((8 * step + u + v) * full_rows, full_rows)
                stage_ref[pl.ds(at, full_rows), :] = done[:, v * LANES : (v + 1) * LANES]
        return carry

    lax.fori_loop(0, width // 8, first_stage, 0)

    def turned(real, imag, block, u):
        cosine = turn_ref[block, :, u : u + 1]
        sine = turn_ref[block, :, 8 + u : 9 + u]
        if imag is None:
            return jnp.concatenate([real * cosine, -real * sine], 0)
        return jnp.concatenate([real * cosine + imag * sine, imag * cosine - real * sine], 0)

    def transform(values):
        high, low = split_bf16(values)
        return jnp.dot(
            second_matrix, jnp.concatenate([high, high, low], 0), preferred_element_type=F32
        )

    def second_stage(block, carry):
        for u in range(0, 8, 2):
            pair = []
            for v in range(u, u + 2):
                at = 8 * block + v
                real = stage_ref[pl.ds(at, width, stride=full_rows), :]
                imag = stage_ref[pl.ds(half_rows + at, width, stride=full_rows), :]
                if v == 0:
                    imag = imag * jnp.where(block == 0, 0.0, 1.0).astype(F32)
                pair.append(turned(real, imag, block, v))
            done = transform(jnp.concatenate(pair, 1))
            for v in range(2):
                out_ref[8 * block + u + v] = done[:, v * LANES : (v + 1) * LANES]
        return carry

    lax.fori_loop(0, half_rows // 8, second_stage, 0)
    real = stage_ref[pl.ds(half_rows, width, stride=full_rows), :]
    top_ref[...] = transform(turned(real, None, half_rows // 8, 0))


def forward(got, devices_seq, width):
    half_rows = got.shape[0] * got.shape[1] // width
    first, second, _, _, turn = tables(half_rows, width)
    return pl.pallas_call(
        functools.partial(forward_kernel, devices_seq=devices_seq),
        out_shape=(
            jax.ShapeDtypeStruct((half_rows, 2 * width, LANES), F32),
            jax.ShapeDtypeStruct((2 * width, LANES), F32),
        ),
        scratch_shapes=[
            pltpu.VMEM((half_rows * width, LANES), F32),
            pltpu.VMEM((2 * half_rows * width, LANES), F32),
        ],
        compiler_params=pltpu.CompilerParams(vmem_limit_bytes=32 << 20),
        cost_estimate=pl.CostEstimate(
            flops=2 * LANES * (first.size * width + second.size * half_rows),
            bytes_accessed=2 * got.size + 8 * half_rows * width * LANES,
            transcendentals=0,
        ),
        name="forward",
    )(got, first, second, turn)


def inverse_kernel(
    spec_ref, top_ref, filter_ref, third_ref, last_ref, turn_ref, out_ref,
    real_ref, imag_ref, rows_ref, *, devices_seq, share
):
    width = turn_ref.shape[1]
    half_rows = spec_ref.shape[0]
    third_matrix = third_ref[...]
    last_matrix = last_ref[...]
    per_source = 2 * share
    left = left_lanes(width)

    def place(source, at):
        return (at // share) * devices_seq * share + source * share + at % share

    def filtered(spec, response):
        turned = pltpu.roll(response, HALF, 1)
        real_part = jnp.where(left, response, turned)
        imag_part = jnp.where(left, turned, response)
        real, imag = spec[:width], spec[width:]
        return jnp.concatenate(
            [real * real_part - imag * imag_part, real * imag_part + imag * real_part], 0
        ).astype(BF16)

    def transform(values):
        return jnp.dot(
            third_matrix, jnp.concatenate([values, values], 0), preferred_element_type=F32
        )

    def turned_back(values, block, u):
        cosine = turn_ref[block, :, u : u + 1]
        sine = turn_ref[block, :, 8 + u : 9 + u]
        real, imag = values[:width], values[width:]
        return real * cosine - imag * sine, real * sine + imag * cosine

    def third_stage(block, carry):
        for u in range(0, per_source, 2):
            pair = []
            for v in range(u, u + 2):
                response = filter_ref[place(block, v)].astype(F32)
                if v == 0:
                    source = jnp.where(block == 0, 0, devices_seq - block)
                    mirror = filter_ref[place(source, 0)].astype(F32)
                    mirror = mirror * jnp.where(block == 0, 0.0, 1.0).astype(F32)
                else:
                    mirror = filter_ref[place(devices_seq - 1 - block, per_source - v)].astype(F32)
                pair.append(filtered(spec_ref[per_source * block + v], response + mirror))
            done = transform(jnp.concatenate(pair, 1))
            for v in range(2):
                real, imag = turned_back(done[:, v * LANES : (v + 1) * LANES], block, u + v)
                at = pl.multiple_of((per_source * block + u + v) * width, width)
                real_ref[pl.ds(at, width), :] = real
                imag_ref[pl.ds(at, width), :] = imag
        return carry

    lax.fori_loop(0, half_rows // per_source, third_stage, 0)
    top_block = half_rows // per_source
    response = filter_ref[place(top_block, 0)].astype(F32)
    done = transform(filtered(top_ref[...], response))
    imag_ref[pl.ds(0, width), :] = turned_back(done, top_block, 0)[0]

    def last_stage(step, carry):
        for u in range(0, 8, 2):
            pair = []
            for v in range(u, u + 2):
                rows = pl.ds(8 * step + v, half_rows, stride=width)
                pair.append(jnp.concatenate([real_ref[rows, :], imag_ref[rows, :]], 0).astype(BF16))
            pair = jnp.concatenate(pair, 1)
            done = jnp.dot(
                last_matrix, jnp.concatenate([pair, pair], 0), preferred_element_type=F32
            )
            for v in range(2):
                rows = pl.ds(8 * step + u + v, half_rows, stride=width)
                rows_ref[rows, :] = done[:, v * LANES : (v + 1) * LANES]
        return carry

    lax.fori_loop(0, width // 8, last_stage, 0)
    piece = out_ref.shape[1]
    for source in range(devices_seq):
        first, second = swap_halves(
            rows_ref[pl.ds(2 * source * piece, piece), :],
            rows_ref[pl.ds((2 * source + 1) * piece, piece), :],
        )
        out_ref[source] = first.astype(BF16)
        out_ref[devices_seq + source] = second.astype(BF16)


def inverse(spectrum, top, arrived, devices_seq, share, piece):
    half_rows, rows, _ = spectrum.shape
    width = rows // 2
    _, _, third, last, turn = tables(half_rows, width)
    return pl.pallas_call(
        functools.partial(inverse_kernel, devices_seq=devices_seq, share=share),
        out_shape=jax.ShapeDtypeStruct((2 * devices_seq, piece, LANES), BF16),
        scratch_shapes=[pltpu.VMEM((half_rows * width, LANES), F32)] * 3,
        compiler_params=pltpu.CompilerParams(vmem_limit_bytes=32 << 20),
        cost_estimate=pl.CostEstimate(
            flops=2 * LANES * (third.size * half_rows + last.size * width),
            bytes_accessed=4 * spectrum.size + 2 * arrived.size,
            transcendentals=0,
        ),
        name="inverse",
    )(spectrum, top, arrived, third, last, turn)


def mix_kernel(conv_ref, signal_ref, gate_ref, out_gate_ref, gain_ref, out_ref):
    rows = signal_ref.shape[0] // 2
    for block in range(signal_ref.shape[1] // LANES):
        lanes = pl.ds(block * LANES, LANES)
        gain = gain_ref[:, lanes]
        halves = swap_halves(
            conv_ref[2 * block].astype(F32), conv_ref[2 * block + 1].astype(F32)
        )
        for half, convolved in enumerate(halves):
            at = pl.ds(half * rows, rows)
            gated = signal_ref[at, lanes].astype(F32) * gate_ref[at, lanes].astype(F32)
            gated = gated.astype(BF16).astype(F32)
            mixed = out_gate_ref[at, lanes].astype(F32) * (convolved + gain * gated)
            out_ref[at, lanes] = mixed.astype(BF16)


def mix(conv, signal, input_gate, output_gate, skip_gain):
    tok_rows, channels = signal.shape
    wide = 4 * LANES
    block = pl.BlockSpec((tok_rows, wide), lambda b: (0, b))
    return pl.pallas_call(
        mix_kernel,
        out_shape=jax.ShapeDtypeStruct(signal.shape, BF16),
        grid=(channels // wide,),
        in_specs=[
            pl.BlockSpec((8, tok_rows // 2, LANES), lambda b: (b, 0, 0)),
            block,
            block,
            block,
            pl.BlockSpec((1, wide), lambda b: (0, b)),
        ],
        out_specs=block,
        cost_estimate=pl.CostEstimate(
            flops=4 * signal.size, bytes_accessed=10 * signal.size, transcendentals=0
        ),
        name="mix",
    )(conv, signal, input_gate, output_gate, skip_gain[None, :])


def spread_kernels(signal, input_gate, output_gate, filter_spectrum, skip_gain):
    groups = lax.axis_size("groups")
    devices_seq = lax.axis_size("seq")
    low, high = filter_spectrum.shape[1:3]
    share = low // groups
    piece = signal.shape[0] // 2
    got = exchange(pack_input(signal, input_gate, groups * devices_seq))
    arrived = exchange(pack_filter(filter_spectrum, groups, devices_seq))
    spectrum, top = forward(got, devices_seq, high)
    conv = inverse(
        spectrum, top, arrived.reshape(-1, high, LANES), devices_seq, share, piece
    )
    return mix(exchange(conv), signal, input_gate, output_gate, skip_gain)


def angle_table(rows_count, cols_count, length):
    row_index = lax.iota(jnp.int32, rows_count)
    col_index = lax.iota(jnp.int32, cols_count)
    product = row_index[:, None] * col_index[None, :] % length
    angles = product.astype(jnp.float32) * (2.0 * math.pi / length)
    return (jnp.cos(angles), jnp.sin(angles))


def contract_first(matrix, values):
    return jnp.einsum("kn,nbc->kbc", matrix, values, precision=lax.Precision.HIGH)


def contract_second(matrix, values):
    return jnp.einsum("kn,anc->akc", matrix, values, precision=lax.Precision.HIGH)


def convolve(signal_rows, spectra_real, spectra_imag):
    half_rows, width, _ = signal_rows.shape
    full_rows = 2 * half_rows
    length = full_rows * width
    cos_one, sin_one = angle_table(full_rows, half_rows, full_rows)
    cos_two, sin_two = angle_table(width, width, width)
    turn_cos, turn_sin = angle_table(full_rows, width, length)
    turn_cos = turn_cos[:, :, None]
    turn_sin = turn_sin[:, :, None]
    first_real = contract_first(cos_one, signal_rows)
    first_imag = -contract_first(sin_one, signal_rows)
    twist_real = first_real * turn_cos + first_imag * turn_sin
    twist_imag = first_imag * turn_cos - first_real * turn_sin
    spec_real = contract_second(cos_two, twist_real) + contract_second(sin_two, twist_imag)
    spec_imag = contract_second(cos_two, twist_imag) - contract_second(sin_two, twist_real)
    prod_real = spec_real * spectra_real - spec_imag * spectra_imag
    prod_imag = spec_real * spectra_imag + spec_imag * spectra_real
    back_real = contract_second(cos_two, prod_real) - contract_second(sin_two, prod_imag)
    back_imag = contract_second(sin_two, prod_real) + contract_second(cos_two, prod_imag)
    rotated_real = back_real * turn_cos - back_imag * turn_sin
    rotated_imag = back_real * turn_sin + back_imag * turn_cos
    summed = contract_first(cos_one.T, rotated_real) - contract_first(sin_one.T, rotated_imag)
    return summed * (1.0 / length)


def spread_plain(signal, input_gate, output_gate, filter_spectrum, skip_gain):
    tok_rows, channels = signal.shape
    groups = lax.axis_size("groups")
    devices_seq = lax.axis_size("seq")
    parts = groups * devices_seq
    width = channels // parts
    low, high = filter_spectrum.shape[1:3]
    share = low // groups
    gated_input = (input_gate.astype(jnp.float32) * signal.astype(jnp.float32)).astype(jnp.bfloat16)

    sent = gated_input.reshape(tok_rows, parts, width).transpose(1, 0, 2).reshape(parts, -1, 128)
    got = exchange(sent).reshape(groups, devices_seq, tok_rows, width)
    rows = got.transpose(1, 2, 0, 3).reshape(-1, high, groups * width)

    mine = lax.dynamic_slice_in_dim(filter_spectrum, lax.axis_index("groups") * share, share, axis=1)
    mine = mine.astype(jnp.bfloat16).reshape(2, share, high, parts, width)
    mine = mine.transpose(3, 0, 1, 2, 4).reshape(parts, -1, 128)
    spectra = exchange(mine).reshape(groups, devices_seq, 2, share, high, width)
    spectra = spectra.transpose(2, 1, 0, 3, 4, 5).reshape(2, -1, high, 1, width)
    spectra = jnp.broadcast_to(spectra, spectra.shape[:3] + (groups, width))
    spectra = spectra.reshape(2, -1, high, groups * width).astype(jnp.float32)

    conv = convolve(rows.astype(jnp.float32), spectra[0], spectra[1]).astype(jnp.bfloat16)
    conv = conv.reshape(devices_seq, tok_rows, groups, width).transpose(2, 0, 1, 3)
    back = exchange(conv.reshape(parts, -1, 128)).reshape(parts, tok_rows, width)
    convolved = back.transpose(1, 0, 2).reshape(tok_rows, channels).astype(jnp.float32)
    mixed_out = output_gate.astype(jnp.float32) * (
        convolved + skip_gain[None, :] * gated_input.astype(jnp.float32)
    )
    return mixed_out.astype(jnp.bfloat16)


def on_device(signal, input_gate, output_gate, filter_spectrum, skip_gain):
    groups = lax.axis_size("groups")
    devices_seq = lax.axis_size("seq")
    tok_rows, channels = signal.shape
    low, high = filter_spectrum.shape[1:3]
    fits = (
        groups == 2
        and channels == groups * devices_seq * HALF
        and low == 8
        and tok_rows == low * high // 2
        and tok_rows % 32 == 0
        and devices_seq % 2 == 0
    )
    plan = spread_kernels if fits else spread_plain
    return plan(signal, input_gate, output_gate, filter_spectrum, skip_gain)


def solution(mesh):
    return jax.shard_map(
        on_device,
        mesh=mesh,
        in_specs=(P(EVERY, None), P(EVERY, None), P(EVERY, None), P(None, "seq", None, None), P()),
        out_specs=P(EVERY, None),
        check_vma=False,
    )
```

```python
import functools
import math

import jax
import jax.numpy as jnp
import ml_dtypes
import numpy as np
from jax import lax
from jax.experimental import pallas as pl
from jax.experimental.pallas import tpu as pltpu
from jax.sharding import PartitionSpec as P

EVERY = ("groups", "seq")
LANES = 128
HALF = LANES // 2
PAD = 8
BF16 = jnp.bfloat16
F32 = jnp.float32


def exchange(values):
    return lax.all_to_all(values, EVERY, split_axis=0, concat_axis=0, tiled=True)


def left_lanes(rows):
    return lax.broadcasted_iota(jnp.int32, (rows, LANES), 1) < HALF


def swap_halves(first, second):
    left = left_lanes(first.shape[0])
    return (
        jnp.where(left, first, pltpu.roll(second, HALF, 1)),
        jnp.where(left, pltpu.roll(first, HALF, 1), second),
    )


def hi_lo(matrix):
    high = matrix.astype(ml_dtypes.bfloat16)
    low = (matrix - high.astype(np.float64)).astype(ml_dtypes.bfloat16)
    return high, low


@functools.lru_cache(None)
def tables(half_rows, width):
    full_rows = 2 * half_rows
    length = full_rows * width
    low_index = np.arange(half_rows)
    angle = 2 * np.pi * (np.outer(low_index, low_index) % full_rows) / full_rows
    real_part, imag_part = np.cos(angle), -np.sin(angle)
    imag_part[0] = 1.0 - 2.0 * (low_index % 2)
    first = np.concatenate([real_part, imag_part], 0)
    last = first.T / length
    inner = np.arange(width)
    angle = 2 * np.pi * (np.outer(inner, inner) % width) / width
    cosine, sine = np.cos(angle), np.sin(angle)
    second = np.block([[cosine, sine], [-sine, cosine]])
    third = np.block([[cosine, -sine], [sine, cosine]])
    first_hi, first_lo = hi_lo(first)
    second_hi, second_lo = hi_lo(second)
    third_hi, third_lo = hi_lo(third)
    last_hi, last_lo = hi_lo(last)
    turn = np.zeros((half_rows // 8 + 1, width, LANES), np.float32)
    for block in range(half_rows // 8 + 1):
        angle = 2 * np.pi * np.outer(inner, 8 * block + np.arange(8)) / length
        turn[block, :, :8] = np.cos(angle)
        turn[block, :, 8:16] = np.sin(angle)
    return (
        np.concatenate([first_hi, first_lo], 1),
        np.concatenate([second_hi, second_lo, second_hi], 1),
        np.concatenate([third_hi, third_lo], 1),
        np.concatenate([last_hi, last_lo], 1),
        turn,
    )


def pack_input_kernel(signal_ref, gate_ref, out_ref):
    rows = signal_ref.shape[0] // 2
    for block in range(signal_ref.shape[1] // LANES):
        lanes = pl.ds(block * LANES, LANES)
        gated = signal_ref[:, lanes].astype(F32) * gate_ref[:, lanes].astype(F32)
        first, second = swap_halves(gated[:rows], gated[rows:])
        out_ref[2 * block] = first.astype(BF16)
        out_ref[2 * block + 1] = second.astype(BF16)


def pack_input(signal, input_gate, parts):
    tok_rows, channels = signal.shape
    wide = 8 * LANES
    return pl.pallas_call(
        pack_input_kernel,
        out_shape=jax.ShapeDtypeStruct((parts, tok_rows // 2, LANES), BF16),
        grid=(channels // wide,),
        in_specs=[pl.BlockSpec((tok_rows, wide), lambda b: (0, b))] * 2,
        out_specs=pl.BlockSpec((16, tok_rows // 2, LANES), lambda b: (b, 0, 0)),
        cost_estimate=pl.CostEstimate(
            flops=signal.size, bytes_accessed=6 * signal.size, transcendentals=0
        ),
        name="pack_input",
    )(signal, input_gate)


def pack_filter_kernel(first_low_ref, filter_ref, out_ref, *, middle):
    share, width = filter_ref.shape[1:3]
    row = lax.broadcasted_iota(jnp.int32, (width, width), 0)
    col = lax.broadcasted_iota(jnp.int32, (width, width), 1)
    for low in range(share):
        mirrored = first_low_ref[1] + low > middle
        order = jnp.where(col == jnp.where(mirrored, width - 1 - row, row), 1.0, 0.0).astype(BF16)
        sign = jnp.where(mirrored, -1.0, 1.0).astype(F32)
        for block in range(filter_ref.shape[3] // LANES):
            lanes = pl.ds(block * LANES, LANES)
            both = jnp.concatenate(
                [filter_ref[0, low, :, lanes], filter_ref[1, low, :, lanes]], 1
            ).astype(BF16)
            both = jnp.dot(order, both, preferred_element_type=F32)
            first, second = swap_halves(both[:, :LANES], sign * both[:, LANES:])
            rows = pl.ds(low * width, width)
            out_ref[2 * block, rows, :] = first.astype(BF16)
            out_ref[2 * block + 1, rows, :] = second.astype(BF16)


def pack_filter(filter_spectrum, groups, devices_seq):
    _, low, width, channels = filter_spectrum.shape
    share = low // groups
    group = lax.axis_index("groups")
    first_low = lax.axis_index("seq") * low + group * share
    wide = 8 * LANES
    chunks = wide // HALF
    size = share * width * channels
    return pl.pallas_call(
        functools.partial(pack_filter_kernel, middle=low * devices_seq // 2),
        out_shape=jax.ShapeDtypeStruct((channels // HALF, share * width, LANES), BF16),
        grid_spec=pltpu.PrefetchScalarGridSpec(
            num_scalar_prefetch=1,
            grid=(channels // wide,),
            in_specs=[pl.BlockSpec((2, share, width, wide), lambda b, at: (0, at[0], 0, b))],
            out_specs=pl.BlockSpec((chunks, share * width, LANES), lambda b, at: (b, 0, 0)),
        ),
        cost_estimate=pl.CostEstimate(
            flops=4 * width * size, bytes_accessed=12 * size, transcendentals=0
        ),
        name="pack_filter",
    )(jnp.stack([group, first_low]), filter_spectrum)


def split_bf16(values):
    high = values.astype(BF16)
    return high, (values - high.astype(F32)).astype(BF16)


def forward_kernel(
    got_ref, first_ref, second_ref, turn_ref, out_ref, top_ref, rows_ref, stage_ref, *, devices_seq
):
    width = turn_ref.shape[1]
    half_rows = out_ref.shape[0]
    full_rows = 2 * half_rows
    pitch = width + PAD
    tall = full_rows + PAD
    lines = got_ref.shape[1] // width
    for source in range(devices_seq):
        for line in range(lines):
            at = pl.ds(line * width, width)
            halves = swap_halves(
                got_ref[source, at, :].astype(F32),
                got_ref[devices_seq + source, at, :].astype(F32),
            )
            for half in range(2):
                row = (2 * source + half) * lines + line
                rows_ref[pl.ds(row * pitch, width), :] = halves[half]
    first_matrix = first_ref[...]
    second_matrix = second_ref[...]

    def first_stage(step, carry):
        for u in range(0, 8, 2):
            pair = jnp.concatenate(
                [
                    rows_ref[pl.ds(8 * step + u + v, half_rows, stride=pitch), :].astype(BF16)
                    for v in range(2)
                ],
                1,
            )
            pair = jnp.concatenate([pair, pair], 0)
            done = jnp.dot(first_matrix, pair, preferred_element_type=F32)
            for v in range(2):
                at = pl.multiple_of((8 * step + u + v) * tall, PAD)
                stage_ref[pl.ds(at, full_rows), :] = done[:, v * LANES : (v + 1) * LANES]
        return carry

    lax.fori_loop(0, width // 8, first_stage, 0)

    def turned(real, imag, block, u):
        cosine = turn_ref[block, :, u : u + 1]
        sine = turn_ref[block, :, 8 + u : 9 + u]
        if imag is None:
            return jnp.concatenate([real * cosine, -real * sine], 0)
        return jnp.concatenate([real * cosine + imag * sine, imag * cosine - real * sine], 0)

    def transform(values):
        high, low = split_bf16(values)
        return jnp.dot(
            second_matrix, jnp.concatenate([high, high, low], 0), preferred_element_type=F32
        )

    def second_stage(block, carry):
        for u in range(0, 8, 2):
            pair = []
            for v in range(u, u + 2):
                at = 8 * block + v
                real = stage_ref[pl.ds(at, width, stride=tall), :]
                imag = stage_ref[pl.ds(half_rows + at, width, stride=tall), :]
                if v == 0:
                    imag = imag * jnp.where(block == 0, 0.0, 1.0).astype(F32)
                pair.append(turned(real, imag, block, v))
            done = transform(jnp.concatenate(pair, 1))
            for v in range(2):
                out_ref[8 * block + u + v] = done[:, v * LANES : (v + 1) * LANES]
        return carry

    lax.fori_loop(0, half_rows // 8, second_stage, 0)
    real = stage_ref[pl.ds(half_rows, width, stride=tall), :]
    top_ref[...] = transform(turned(real, None, half_rows // 8, 0))


def forward(got, devices_seq, width):
    half_rows = got.shape[0] * got.shape[1] // width
    first, second, _, _, turn = tables(half_rows, width)
    return pl.pallas_call(
        functools.partial(forward_kernel, devices_seq=devices_seq),
        out_shape=(
            jax.ShapeDtypeStruct((half_rows, 2 * width, LANES), F32),
            jax.ShapeDtypeStruct((2 * width, LANES), F32),
        ),
        scratch_shapes=[
            pltpu.VMEM((half_rows * (width + PAD), LANES), F32),
            pltpu.VMEM((width * (2 * half_rows + PAD), LANES), F32),
        ],
        compiler_params=pltpu.CompilerParams(vmem_limit_bytes=16 << 20),
        cost_estimate=pl.CostEstimate(
            flops=2 * LANES * (first.size * width + second.size * half_rows),
            bytes_accessed=2 * got.size + 8 * half_rows * width * LANES,
            transcendentals=0,
        ),
        name="forward",
    )(got, first, second, turn)


def inverse_kernel(
    spec_hbm, top_ref, filter_ref, third_ref, last_ref, turn_ref, out_ref,
    spec_ref, real_ref, imag_ref, rows_ref, sems, *, devices_seq, share
):
    width = turn_ref.shape[1]
    half_rows = spec_ref.shape[0]
    pitch = width + PAD
    third_matrix = third_ref[...]
    last_matrix = last_ref[...]
    per_source = 2 * share
    left = left_lanes(width)

    def fetch(block):
        at = pl.ds(per_source * block, per_source)
        return pltpu.make_async_copy(spec_hbm.at[at], spec_ref.at[at], sems.at[block])

    for block in range(half_rows // per_source):
        fetch(block).start()

    def place(source, at):
        return (at // share) * devices_seq * share + source * share + at % share

    def filtered(spec, response):
        turned = pltpu.roll(response, HALF, 1)
        real_part = jnp.where(left, response, turned)
        imag_part = jnp.where(left, turned, response)
        real, imag = spec[:width], spec[width:]
        return jnp.concatenate(
            [real * real_part - imag * imag_part, real * imag_part + imag * real_part], 0
        ).astype(BF16)

    def transform(values):
        return jnp.dot(
            third_matrix, jnp.concatenate([values, values], 0), preferred_element_type=F32
        )

    def turned_back(values, block, u):
        cosine = turn_ref[block, :, u : u + 1]
        sine = turn_ref[block, :, 8 + u : 9 + u]
        real, imag = values[:width], values[width:]
        return real * cosine - imag * sine, real * sine + imag * cosine

    def third_stage(block, carry):
        fetch(block).wait()
        for u in range(0, per_source, 2):
            pair = []
            for v in range(u, u + 2):
                response = filter_ref[place(block, v)].astype(F32)
                if v == 0:
                    source = jnp.where(block == 0, 0, devices_seq - block)
                    mirror = filter_ref[place(source, 0)].astype(F32)
                    mirror = mirror * jnp.where(block == 0, 0.0, 1.0).astype(F32)
                else:
                    mirror = filter_ref[place(devices_seq - 1 - block, per_source - v)].astype(F32)
                pair.append(filtered(spec_ref[per_source * block + v], response + mirror))
            done = transform(jnp.concatenate(pair, 1))
            for v in range(2):
                real, imag = turned_back(done[:, v * LANES : (v + 1) * LANES], block, u + v)
                at = pl.multiple_of((per_source * block + u + v) * pitch, PAD)
                real_ref[pl.ds(at, width), :] = real
                imag_ref[pl.ds(at, width), :] = imag
        return carry

    lax.fori_loop(0, half_rows // per_source, third_stage, 0, unroll=True)
    top_block = half_rows // per_source
    response = filter_ref[place(top_block, 0)].astype(F32)
    done = transform(filtered(top_ref[...], response))
    imag_ref[pl.ds(0, width), :] = turned_back(done, top_block, 0)[0]

    def last_stage(step, carry):
        for u in range(0, 8, 2):
            pair = []
            for v in range(u, u + 2):
                rows = pl.ds(8 * step + v, half_rows, stride=pitch)
                pair.append(jnp.concatenate([real_ref[rows, :], imag_ref[rows, :]], 0).astype(BF16))
            pair = jnp.concatenate(pair, 1)
            done = jnp.dot(
                last_matrix, jnp.concatenate([pair, pair], 0), preferred_element_type=F32
            )
            for v in range(2):
                rows = pl.ds(8 * step + u + v, half_rows, stride=pitch)
                rows_ref[rows, :] = done[:, v * LANES : (v + 1) * LANES]
        return carry

    lax.fori_loop(0, width // 8, last_stage, 0, unroll=True)
    lines = out_ref.shape[1] // width
    for source in range(devices_seq):
        for line in range(lines):
            first, second = swap_halves(
                *(
                    rows_ref[pl.ds(((2 * source + half) * lines + line) * pitch, width), :]
                    for half in range(2)
                )
            )
            at = pl.ds(line * width, width)
            out_ref[source, at, :] = first.astype(BF16)
            out_ref[devices_seq + source, at, :] = second.astype(BF16)


def inverse(spectrum, top, arrived, devices_seq, share, piece):
    half_rows, rows, _ = spectrum.shape
    width = rows // 2
    _, _, third, last, turn = tables(half_rows, width)
    return pl.pallas_call(
        functools.partial(inverse_kernel, devices_seq=devices_seq, share=share),
        out_shape=jax.ShapeDtypeStruct((2 * devices_seq, piece, LANES), BF16),
        in_specs=[pl.BlockSpec(memory_space=pl.ANY)]
        + [pl.BlockSpec(memory_space=pltpu.VMEM)] * 5,
        scratch_shapes=[pltpu.VMEM(spectrum.shape, F32)]
        + [pltpu.VMEM((half_rows * (width + PAD), LANES), F32)] * 3
        + [pltpu.SemaphoreType.DMA((half_rows // (2 * share),))],
        compiler_params=pltpu.CompilerParams(vmem_limit_bytes=16 << 20),
        cost_estimate=pl.CostEstimate(
            flops=2 * LANES * (third.size * half_rows + last.size * width),
            bytes_accessed=4 * spectrum.size + 2 * arrived.size,
            transcendentals=0,
        ),
        name="inverse",
    )(spectrum, top, arrived, third, last, turn)


def mix_kernel(conv_ref, signal_ref, gate_ref, out_gate_ref, gain_ref, out_ref):
    rows = signal_ref.shape[0] // 2
    for block in range(signal_ref.shape[1] // LANES):
        lanes = pl.ds(block * LANES, LANES)
        gain = gain_ref[:, lanes]
        halves = swap_halves(
            conv_ref[2 * block].astype(F32), conv_ref[2 * block + 1].astype(F32)
        )
        for half, convolved in enumerate(halves):
            at = pl.ds(half * rows, rows)
            gated = signal_ref[at, lanes].astype(F32) * gate_ref[at, lanes].astype(F32)
            gated = gated.astype(BF16).astype(F32)
            mixed = out_gate_ref[at, lanes].astype(F32) * (convolved + gain * gated)
            out_ref[at, lanes] = mixed.astype(BF16)


def mix(conv, signal, input_gate, output_gate, skip_gain):
    tok_rows, channels = signal.shape
    wide = 8 * LANES
    block = pl.BlockSpec((tok_rows, wide), lambda b: (0, b))
    return pl.pallas_call(
        mix_kernel,
        out_shape=jax.ShapeDtypeStruct(signal.shape, BF16),
        grid=(channels // wide,),
        in_specs=[
            pl.BlockSpec((16, tok_rows // 2, LANES), lambda b: (b, 0, 0)),
            block,
            block,
            block,
            pl.BlockSpec((1, wide), lambda b: (0, b)),
        ],
        out_specs=block,
        cost_estimate=pl.CostEstimate(
            flops=4 * signal.size, bytes_accessed=10 * signal.size, transcendentals=0
        ),
        name="mix",
    )(conv, signal, input_gate, output_gate, skip_gain[None, :])


def spread_kernels(signal, input_gate, output_gate, filter_spectrum, skip_gain):
    groups = lax.axis_size("groups")
    devices_seq = lax.axis_size("seq")
    low, high = filter_spectrum.shape[1:3]
    share = low // groups
    piece = signal.shape[0] // 2
    got = exchange(pack_input(signal, input_gate, groups * devices_seq))
    arrived = exchange(pack_filter(filter_spectrum, groups, devices_seq))
    spectrum, top = forward(got, devices_seq, high)
    conv = inverse(
        spectrum, top, arrived.reshape(-1, high, LANES), devices_seq, share, piece
    )
    return mix(exchange(conv), signal, input_gate, output_gate, skip_gain)


def angle_table(rows_count, cols_count, length):
    row_index = lax.iota(jnp.int32, rows_count)
    col_index = lax.iota(jnp.int32, cols_count)
    product = row_index[:, None] * col_index[None, :] % length
    angles = product.astype(jnp.float32) * (2.0 * math.pi / length)
    return (jnp.cos(angles), jnp.sin(angles))


def contract_first(matrix, values):
    return jnp.einsum("kn,nbc->kbc", matrix, values, precision=lax.Precision.HIGH)


def contract_second(matrix, values):
    return jnp.einsum("kn,anc->akc", matrix, values, precision=lax.Precision.HIGH)


def convolve(signal_rows, spectra_real, spectra_imag):
    half_rows, width, _ = signal_rows.shape
    full_rows = 2 * half_rows
    length = full_rows * width
    cos_one, sin_one = angle_table(full_rows, half_rows, full_rows)
    cos_two, sin_two = angle_table(width, width, width)
    turn_cos, turn_sin = angle_table(full_rows, width, length)
    turn_cos = turn_cos[:, :, None]
    turn_sin = turn_sin[:, :, None]
    first_real = contract_first(cos_one, signal_rows)
    first_imag = -contract_first(sin_one, signal_rows)
    twist_real = first_real * turn_cos + first_imag * turn_sin
    twist_imag = first_imag * turn_cos - first_real * turn_sin
    spec_real = contract_second(cos_two, twist_real) + contract_second(sin_two, twist_imag)
    spec_imag = contract_second(cos_two, twist_imag) - contract_second(sin_two, twist_real)
    prod_real = spec_real * spectra_real - spec_imag * spectra_imag
    prod_imag = spec_real * spectra_imag + spec_imag * spectra_real
    back_real = contract_second(cos_two, prod_real) - contract_second(sin_two, prod_imag)
    back_imag = contract_second(sin_two, prod_real) + contract_second(cos_two, prod_imag)
    rotated_real = back_real * turn_cos - back_imag * turn_sin
    rotated_imag = back_real * turn_sin + back_imag * turn_cos
    summed = contract_first(cos_one.T, rotated_real) - contract_first(sin_one.T, rotated_imag)
    return summed * (1.0 / length)


def spread_plain(signal, input_gate, output_gate, filter_spectrum, skip_gain):
    tok_rows, channels = signal.shape
    groups = lax.axis_size("groups")
    devices_seq = lax.axis_size("seq")
    parts = groups * devices_seq
    width = channels // parts
    low, high = filter_spectrum.shape[1:3]
    share = low // groups
    gated_input = (input_gate.astype(jnp.float32) * signal.astype(jnp.float32)).astype(jnp.bfloat16)

    sent = gated_input.reshape(tok_rows, parts, width).transpose(1, 0, 2).reshape(parts, -1, 128)
    got = exchange(sent).reshape(groups, devices_seq, tok_rows, width)
    rows = got.transpose(1, 2, 0, 3).reshape(-1, high, groups * width)

    mine = lax.dynamic_slice_in_dim(filter_spectrum, lax.axis_index("groups") * share, share, axis=1)
    mine = mine.astype(jnp.bfloat16).reshape(2, share, high, parts, width)
    mine = mine.transpose(3, 0, 1, 2, 4).reshape(parts, -1, 128)
    spectra = exchange(mine).reshape(groups, devices_seq, 2, share, high, width)
    spectra = spectra.transpose(2, 1, 0, 3, 4, 5).reshape(2, -1, high, 1, width)
    spectra = jnp.broadcast_to(spectra, spectra.shape[:3] + (groups, width))
    spectra = spectra.reshape(2, -1, high, groups * width).astype(jnp.float32)

    conv = convolve(rows.astype(jnp.float32), spectra[0], spectra[1]).astype(jnp.bfloat16)
    conv = conv.reshape(devices_seq, tok_rows, groups, width).transpose(2, 0, 1, 3)
    back = exchange(conv.reshape(parts, -1, 128)).reshape(parts, tok_rows, width)
    convolved = back.transpose(1, 0, 2).reshape(tok_rows, channels).astype(jnp.float32)
    mixed_out = output_gate.astype(jnp.float32) * (
        convolved + skip_gain[None, :] * gated_input.astype(jnp.float32)
    )
    return mixed_out.astype(jnp.bfloat16)


def on_device(signal, input_gate, output_gate, filter_spectrum, skip_gain):
    groups = lax.axis_size("groups")
    devices_seq = lax.axis_size("seq")
    tok_rows, channels = signal.shape
    low, high = filter_spectrum.shape[1:3]
    fits = (
        groups == 2
        and channels == groups * devices_seq * HALF
        and low == 8
        and tok_rows == low * high // 2
        and tok_rows % 32 == 0
        and devices_seq % 2 == 0
    )
    plan = spread_kernels if fits else spread_plain
    return plan(signal, input_gate, output_gate, filter_spectrum, skip_gain)


def solution(mesh):
    return jax.shard_map(
        on_device,
        mesh=mesh,
        in_specs=(P(EVERY, None), P(EVERY, None), P(EVERY, None), P(None, "seq", None, None), P()),
        out_specs=P(EVERY, None),
        check_vma=False,
    )
```

```python
import functools
import math

import jax
import jax.numpy as jnp
import ml_dtypes
import numpy as np
from jax import lax
from jax.experimental import pallas as pl
from jax.experimental.pallas import tpu as pltpu
from jax.sharding import PartitionSpec as P

EVERY = ("groups", "seq")
PAIRS = ("seq", "groups")
LANES = 128
HALF = LANES // 2
PAD = 8
BF16 = jnp.bfloat16
F32 = jnp.float32


def exchange(values, axes=EVERY):
    return lax.all_to_all(values, axes, split_axis=0, concat_axis=0, tiled=True)


def left_lanes(rows):
    return lax.broadcasted_iota(jnp.int32, (rows, LANES), 1) < HALF


def swap_halves(first, second):
    left = left_lanes(first.shape[0])
    return (
        jnp.where(left, first, pltpu.roll(second, HALF, 1)),
        jnp.where(left, pltpu.roll(first, HALF, 1), second),
    )


def hi_lo(matrix):
    high = matrix.astype(ml_dtypes.bfloat16)
    low = (matrix - high.astype(np.float64)).astype(ml_dtypes.bfloat16)
    return high, low


@functools.lru_cache(None)
def tables(half_rows, width):
    full_rows = 2 * half_rows
    length = full_rows * width
    low_index = np.arange(half_rows)
    angle = 2 * np.pi * (np.outer(low_index, low_index) % full_rows) / full_rows
    real_part, imag_part = np.cos(angle), -np.sin(angle)
    imag_part[0] = 1.0 - 2.0 * (low_index % 2)
    first = np.concatenate([real_part, imag_part], 0)
    last = first.T / length
    inner = np.arange(width)
    angle = 2 * np.pi * (np.outer(inner, inner) % width) / width
    cosine, sine = np.cos(angle), np.sin(angle)
    second = np.block([[cosine, sine], [-sine, cosine]])
    third = np.block([[cosine, -sine], [sine, cosine]])
    first_hi, first_lo = hi_lo(first)
    second_hi, second_lo = hi_lo(second)
    third_hi, third_lo = hi_lo(third)
    last_hi, last_lo = hi_lo(last)
    turn = np.zeros((half_rows // 8 + 1, width, LANES), np.float32)
    for block in range(half_rows // 8 + 1):
        angle = 2 * np.pi * np.outer(inner, 8 * block + np.arange(8)) / length
        turn[block, :, :8] = np.cos(angle)
        turn[block, :, 8:16] = np.sin(angle)
    return (
        np.concatenate([first_hi, first_lo], 1),
        np.concatenate([second_hi, second_lo, second_hi], 1),
        np.block([[third_hi, third_lo], [last_hi, last_lo]]),
        turn,
    )


def pack_input_kernel(signal_ref, gate_ref, out_ref):
    rows = signal_ref.shape[0] // 2
    for block in range(signal_ref.shape[1] // LANES):
        lanes = pl.ds(block * LANES, LANES)
        gated = signal_ref[:, lanes].astype(F32) * gate_ref[:, lanes].astype(F32)
        first, second = swap_halves(gated[:rows], gated[rows:])
        out_ref[2 * block, 0] = first.astype(BF16)
        out_ref[2 * block + 1, 0] = second.astype(BF16)


def pack_input(signal, input_gate, devices_seq):
    tok_rows, channels = signal.shape
    wide = channels // 2
    return pl.pallas_call(
        pack_input_kernel,
        out_shape=jax.ShapeDtypeStruct((devices_seq, 2, tok_rows // 2, LANES), BF16),
        grid=(2,),
        in_specs=[pl.BlockSpec((tok_rows, wide), lambda b: (0, b))] * 2,
        out_specs=pl.BlockSpec((devices_seq, 1, tok_rows // 2, LANES), lambda b: (0, b, 0, 0)),
        cost_estimate=pl.CostEstimate(
            flops=signal.size, bytes_accessed=6 * signal.size, transcendentals=0
        ),
        name="pack_input",
    )(signal, input_gate)


def pack_filter_kernel(first_low_ref, filter_ref, out_ref, *, middle):
    share, width = filter_ref.shape[1:3]
    row = lax.broadcasted_iota(jnp.int32, (width, width), 0)
    col = lax.broadcasted_iota(jnp.int32, (width, width), 1)
    for low in range(share):
        mirrored = first_low_ref[1] + low > middle
        order = jnp.where(col == jnp.where(mirrored, width - 1 - row, row), 1.0, 0.0).astype(BF16)
        sign = jnp.where(mirrored, -1.0, 1.0).astype(F32)
        for block in range(filter_ref.shape[3] // LANES):
            lanes = pl.ds(block * LANES, LANES)
            both = jnp.concatenate(
                [filter_ref[0, low, :, lanes], filter_ref[1, low, :, lanes]], 1
            ).astype(BF16)
            both = jnp.dot(order, both, preferred_element_type=F32)
            first, second = swap_halves(both[:, :LANES], sign * both[:, LANES:])
            rows = pl.ds(low * width, width)
            out_ref[2 * block, rows, :] = first.astype(BF16)
            out_ref[2 * block + 1, rows, :] = second.astype(BF16)


def pack_filter(filter_spectrum, devices_seq):
    _, low, width, channels = filter_spectrum.shape
    group = lax.axis_index("groups")
    wide = 4 * LANES
    steps = channels // 2 // wide
    size = low * width * channels // 2
    return pl.pallas_call(
        functools.partial(pack_filter_kernel, middle=low * devices_seq // 2),
        out_shape=jax.ShapeDtypeStruct((devices_seq, low * width, LANES), BF16),
        grid_spec=pltpu.PrefetchScalarGridSpec(
            num_scalar_prefetch=1,
            grid=(steps,),
            in_specs=[
                pl.BlockSpec(
                    (2, low, width, wide), lambda b, at: (0, 0, 0, at[0] * steps + b)
                )
            ],
            out_specs=pl.BlockSpec((wide // HALF, low * width, LANES), lambda b, at: (b, 0, 0)),
        ),
        compiler_params=pltpu.CompilerParams(vmem_limit_bytes=16 << 20),
        cost_estimate=pl.CostEstimate(
            flops=4 * width * size, bytes_accessed=12 * size, transcendentals=0
        ),
        name="pack_filter",
    )(
        jnp.stack([group, lax.axis_index("seq") * low]),
        pltpu.with_memory_space_constraint(filter_spectrum, pltpu.HBM),
    )


def split_bf16(values):
    high = values.astype(BF16)
    return high, (values - high.astype(F32)).astype(BF16)


def forward_kernel(
    got_ref, first_ref, second_ref, turn_ref, out_ref, rows_ref, stage_ref, *, devices_seq
):
    width = turn_ref.shape[1]
    half_rows = out_ref.shape[0] - 1
    full_rows = 2 * half_rows
    pitch = width + PAD
    tall = full_rows + PAD
    lines = got_ref.shape[2] // width
    for source in range(devices_seq):
        for line in range(lines):
            at = pl.ds(line * width, width)
            halves = swap_halves(
                got_ref[source, 0, at, :].astype(F32), got_ref[source, 1, at, :].astype(F32)
            )
            for half in range(2):
                row = (2 * source + half) * lines + line
                rows_ref[pl.ds(row * pitch, width), :] = halves[half]
    first_matrix = first_ref[...]
    second_matrix = second_ref[...]

    def first_stage(step, carry):
        for u in range(0, 8, 2):
            pair = jnp.concatenate(
                [
                    rows_ref[pl.ds(8 * step + u + v, half_rows, stride=pitch), :].astype(BF16)
                    for v in range(2)
                ],
                1,
            )
            pair = jnp.concatenate([pair, pair], 0)
            done = jnp.dot(first_matrix, pair, preferred_element_type=F32)
            for v in range(2):
                at = pl.multiple_of((8 * step + u + v) * tall, PAD)
                stage_ref[pl.ds(at, full_rows), :] = done[:, v * LANES : (v + 1) * LANES]
        return carry

    lax.fori_loop(0, width // 8, first_stage, 0)

    def turned(real, imag, block, u):
        cosine = turn_ref[block, :, u : u + 1]
        sine = turn_ref[block, :, 8 + u : 9 + u]
        if imag is None:
            return jnp.concatenate([real * cosine, -real * sine], 0)
        return jnp.concatenate([real * cosine + imag * sine, imag * cosine - real * sine], 0)

    def transform(values):
        high, low = split_bf16(values)
        return jnp.dot(
            second_matrix, jnp.concatenate([high, high, low], 0), preferred_element_type=F32
        )

    def second_stage(block, carry):
        for u in range(0, 8, 2):
            pair = []
            for v in range(u, u + 2):
                at = 8 * block + v
                real = stage_ref[pl.ds(at, width, stride=tall), :]
                imag = stage_ref[pl.ds(half_rows + at, width, stride=tall), :]
                if v == 0:
                    imag = imag * jnp.where(block == 0, 0.0, 1.0).astype(F32)
                pair.append(turned(real, imag, block, v))
            done = transform(jnp.concatenate(pair, 1))
            for v in range(2):
                out_ref[8 * block + u + v] = done[:, v * LANES : (v + 1) * LANES]
        return carry

    lax.fori_loop(0, half_rows // 8, second_stage, 0)
    real = stage_ref[pl.ds(half_rows, width, stride=tall), :]
    out_ref[half_rows] = transform(turned(real, None, half_rows // 8, 0))


def forward(got, devices_seq, width):
    half_rows = got.size // (LANES * width)
    first, second, _, turn = tables(half_rows, width)
    return pl.pallas_call(
        functools.partial(forward_kernel, devices_seq=devices_seq),
        out_shape=jax.ShapeDtypeStruct((half_rows + 1, 2 * width, LANES), F32),
        scratch_shapes=[
            pltpu.VMEM((half_rows * (width + PAD), LANES), F32),
            pltpu.VMEM((width * (2 * half_rows + PAD), LANES), F32),
        ],
        compiler_params=pltpu.CompilerParams(vmem_limit_bytes=16 << 20),
        cost_estimate=pl.CostEstimate(
            flops=2 * LANES * (first.size * width + second.size * half_rows),
            bytes_accessed=2 * got.size + 8 * half_rows * width * LANES,
            transcendentals=0,
        ),
        name="forward",
    )(got, first, second, turn)


def inverse_kernel(
    spec_hbm, matrices_hbm, filter_ref, turn_ref, out_ref,
    spec_ref, matrices_ref, real_ref, imag_ref, rows_ref, sems, *, devices_seq
):
    width = turn_ref.shape[1]
    half_rows = spec_ref.shape[0] - 1
    pitch = width + PAD
    per_source = 8
    left = left_lanes(width)

    top_block = half_rows // per_source

    def fetch(block, count=per_source):
        at = pl.ds(per_source * block, count)
        return pltpu.make_async_copy(spec_hbm.at[at], spec_ref.at[at], sems.at[block])

    matrices = pltpu.make_async_copy(matrices_hbm, matrices_ref, sems.at[top_block + 1])
    matrices.start()
    for block in range(top_block):
        fetch(block).start()
    fetch(top_block, 1).start()
    matrices.wait()
    third_matrix = matrices_ref[: 2 * width]
    last_matrix = matrices_ref[2 * width :]

    def filtered(spec, response):
        turned = pltpu.roll(response, HALF, 1)
        real_part = jnp.where(left, response, turned)
        imag_part = jnp.where(left, turned, response)
        real, imag = spec[:width], spec[width:]
        return jnp.concatenate(
            [real * real_part - imag * imag_part, real * imag_part + imag * real_part], 0
        ).astype(BF16)

    def transform(values):
        return jnp.dot(
            third_matrix, jnp.concatenate([values, values], 0), preferred_element_type=F32
        )

    def turned_back(values, block, u):
        cosine = turn_ref[block, :, u : u + 1]
        sine = turn_ref[block, :, 8 + u : 9 + u]
        real, imag = values[:width], values[width:]
        return real * cosine - imag * sine, real * sine + imag * cosine

    def third_stage(block, carry):
        fetch(block).wait()
        for u in range(0, per_source, 2):
            pair = []
            for v in range(u, u + 2):
                response = filter_ref[per_source * block + v].astype(F32)
                if v == 0:
                    at = jnp.where(block == 0, 0, 2 * half_rows - per_source * block)
                    mirror = filter_ref[at].astype(F32)
                    mirror = mirror * jnp.where(block == 0, 0.0, 1.0).astype(F32)
                else:
                    mirror = filter_ref[2 * half_rows - per_source * block - v].astype(F32)
                pair.append(filtered(spec_ref[per_source * block + v], response + mirror))
            done = transform(jnp.concatenate(pair, 1))
            for v in range(2):
                real, imag = turned_back(done[:, v * LANES : (v + 1) * LANES], block, u + v)
                at = pl.multiple_of((per_source * block + u + v) * pitch, PAD)
                real_ref[pl.ds(at, width), :] = real
                imag_ref[pl.ds(at, width), :] = imag
        return carry

    lax.fori_loop(0, half_rows // per_source, third_stage, 0, unroll=True)
    fetch(top_block, 1).wait()
    response = filter_ref[half_rows].astype(F32)
    done = transform(filtered(spec_ref[half_rows], response))
    imag_ref[pl.ds(0, width), :] = turned_back(done, top_block, 0)[0]

    def last_stage(step, carry):
        for u in range(0, 8, 2):
            pair = []
            for v in range(u, u + 2):
                rows = pl.ds(8 * step + v, half_rows, stride=pitch)
                pair.append(jnp.concatenate([real_ref[rows, :], imag_ref[rows, :]], 0).astype(BF16))
            pair = jnp.concatenate(pair, 1)
            done = jnp.dot(
                last_matrix, jnp.concatenate([pair, pair], 0), preferred_element_type=F32
            )
            for v in range(2):
                rows = pl.ds(8 * step + u + v, half_rows, stride=pitch)
                rows_ref[rows, :] = done[:, v * LANES : (v + 1) * LANES]
        return carry

    lax.fori_loop(0, width // 8, last_stage, 0, unroll=True)
    lines = out_ref.shape[2] // width
    for source in range(devices_seq):
        for line in range(lines):
            first, second = swap_halves(
                *(
                    rows_ref[pl.ds(((2 * source + half) * lines + line) * pitch, width), :]
                    for half in range(2)
                )
            )
            at = pl.ds(line * width, width)
            out_ref[source, 0, at, :] = first.astype(BF16)
            out_ref[source, 1, at, :] = second.astype(BF16)


def inverse(spectrum, arrived, devices_seq, piece):
    width = spectrum.shape[1] // 2
    half_rows = spectrum.shape[0] - 1
    _, _, matrices, turn = tables(half_rows, width)
    return pl.pallas_call(
        functools.partial(inverse_kernel, devices_seq=devices_seq),
        out_shape=jax.ShapeDtypeStruct((devices_seq, 2, piece, LANES), BF16),
        in_specs=[pl.BlockSpec(memory_space=pltpu.HBM)] * 2
        + [pl.BlockSpec(memory_space=pltpu.VMEM)] * 2,
        scratch_shapes=[pltpu.VMEM(spectrum.shape, F32), pltpu.VMEM(matrices.shape, BF16)]
        + [pltpu.VMEM((half_rows * (width + PAD), LANES), F32)] * 3
        + [pltpu.SemaphoreType.DMA((half_rows // 8 + 2,))],
        compiler_params=pltpu.CompilerParams(vmem_limit_bytes=20 << 20),
        cost_estimate=pl.CostEstimate(
            flops=2 * LANES * matrices.size * width,
            bytes_accessed=4 * spectrum.size + 2 * arrived.size,
            transcendentals=0,
        ),
        name="inverse",
    )(
        pltpu.with_memory_space_constraint(spectrum, pltpu.HBM),
        pltpu.with_memory_space_constraint(jnp.asarray(matrices), pltpu.HBM),
        arrived,
        turn,
    )


def mix_kernel(conv_ref, signal_ref, gate_ref, out_gate_ref, gain_ref, out_ref):
    rows = signal_ref.shape[0] // 2
    for block in range(signal_ref.shape[1] // LANES):
        lanes = pl.ds(block * LANES, LANES)
        gain = gain_ref[:, lanes]
        place = divmod(2 * block, conv_ref.shape[0])
        halves = swap_halves(
            conv_ref[place[1], place[0]].astype(F32), conv_ref[place[1] + 1, place[0]].astype(F32)
        )
        for half, convolved in enumerate(halves):
            at = pl.ds(half * rows, rows)
            gated = signal_ref[at, lanes].astype(F32) * gate_ref[at, lanes].astype(F32)
            gated = gated.astype(BF16).astype(F32)
            mixed = out_gate_ref[at, lanes].astype(F32) * (convolved + gain * gated)
            out_ref[at, lanes] = mixed.astype(BF16)


def mix(conv, signal, input_gate, output_gate, skip_gain):
    return pl.pallas_call(
        mix_kernel,
        out_shape=jax.ShapeDtypeStruct(signal.shape, BF16),
        in_specs=[pl.BlockSpec(memory_space=pltpu.VMEM)] * 5,
        compiler_params=pltpu.CompilerParams(vmem_limit_bytes=16 << 20),
        cost_estimate=pl.CostEstimate(
            flops=4 * signal.size, bytes_accessed=10 * signal.size, transcendentals=0
        ),
        name="mix",
    )(conv, signal, input_gate, output_gate, skip_gain[None, :])


def spread_kernels(signal, input_gate, output_gate, filter_spectrum, skip_gain):
    devices_seq = lax.axis_size("seq")
    width = filter_spectrum.shape[2]

    def pairs(values):
        return exchange(values.reshape(-1, *values.shape[2:]), PAIRS).reshape(values.shape)

    got = pairs(pack_input(signal, input_gate, devices_seq))
    arrived = exchange(pack_filter(filter_spectrum, devices_seq), "seq")
    spectrum = forward(got, devices_seq, width)
    conv = inverse(
        spectrum, arrived.reshape(-1, width, LANES), devices_seq, signal.shape[0] // 2
    )
    return mix(pairs(conv), signal, input_gate, output_gate, skip_gain)


def angle_table(rows_count, cols_count, length):
    row_index = lax.iota(jnp.int32, rows_count)
    col_index = lax.iota(jnp.int32, cols_count)
    product = row_index[:, None] * col_index[None, :] % length
    angles = product.astype(jnp.float32) * (2.0 * math.pi / length)
    return (jnp.cos(angles), jnp.sin(angles))


def contract_first(matrix, values):
    return jnp.einsum("kn,nbc->kbc", matrix, values, precision=lax.Precision.HIGH)


def contract_second(matrix, values):
    return jnp.einsum("kn,anc->akc", matrix, values, precision=lax.Precision.HIGH)


def convolve(signal_rows, spectra_real, spectra_imag):
    half_rows, width, _ = signal_rows.shape
    full_rows = 2 * half_rows
    length = full_rows * width
    cos_one, sin_one = angle_table(full_rows, half_rows, full_rows)
    cos_two, sin_two = angle_table(width, width, width)
    turn_cos, turn_sin = angle_table(full_rows, width, length)
    turn_cos = turn_cos[:, :, None]
    turn_sin = turn_sin[:, :, None]
    first_real = contract_first(cos_one, signal_rows)
    first_imag = -contract_first(sin_one, signal_rows)
    twist_real = first_real * turn_cos + first_imag * turn_sin
    twist_imag = first_imag * turn_cos - first_real * turn_sin
    spec_real = contract_second(cos_two, twist_real) + contract_second(sin_two, twist_imag)
    spec_imag = contract_second(cos_two, twist_imag) - contract_second(sin_two, twist_real)
    prod_real = spec_real * spectra_real - spec_imag * spectra_imag
    prod_imag = spec_real * spectra_imag + spec_imag * spectra_real
    back_real = contract_second(cos_two, prod_real) - contract_second(sin_two, prod_imag)
    back_imag = contract_second(sin_two, prod_real) + contract_second(cos_two, prod_imag)
    rotated_real = back_real * turn_cos - back_imag * turn_sin
    rotated_imag = back_real * turn_sin + back_imag * turn_cos
    summed = contract_first(cos_one.T, rotated_real) - contract_first(sin_one.T, rotated_imag)
    return summed * (1.0 / length)


def spread_plain(signal, input_gate, output_gate, filter_spectrum, skip_gain):
    tok_rows, channels = signal.shape
    groups = lax.axis_size("groups")
    devices_seq = lax.axis_size("seq")
    parts = groups * devices_seq
    width = channels // parts
    low, high = filter_spectrum.shape[1:3]
    share = low // groups
    gated_input = (input_gate.astype(jnp.float32) * signal.astype(jnp.float32)).astype(jnp.bfloat16)

    sent = gated_input.reshape(tok_rows, parts, width).transpose(1, 0, 2).reshape(parts, -1, 128)
    got = exchange(sent).reshape(groups, devices_seq, tok_rows, width)
    rows = got.transpose(1, 2, 0, 3).reshape(-1, high, groups * width)

    mine = lax.dynamic_slice_in_dim(filter_spectrum, lax.axis_index("groups") * share, share, axis=1)
    mine = mine.astype(jnp.bfloat16).reshape(2, share, high, parts, width)
    mine = mine.transpose(3, 0, 1, 2, 4).reshape(parts, -1, 128)
    spectra = exchange(mine).reshape(groups, devices_seq, 2, share, high, width)
    spectra = spectra.transpose(2, 1, 0, 3, 4, 5).reshape(2, -1, high, 1, width)
    spectra = jnp.broadcast_to(spectra, spectra.shape[:3] + (groups, width))
    spectra = spectra.reshape(2, -1, high, groups * width).astype(jnp.float32)

    conv = convolve(rows.astype(jnp.float32), spectra[0], spectra[1]).astype(jnp.bfloat16)
    conv = conv.reshape(devices_seq, tok_rows, groups, width).transpose(2, 0, 1, 3)
    back = exchange(conv.reshape(parts, -1, 128)).reshape(parts, tok_rows, width)
    convolved = back.transpose(1, 0, 2).reshape(tok_rows, channels).astype(jnp.float32)
    mixed_out = output_gate.astype(jnp.float32) * (
        convolved + skip_gain[None, :] * gated_input.astype(jnp.float32)
    )
    return mixed_out.astype(jnp.bfloat16)


def on_device(signal, input_gate, output_gate, filter_spectrum, skip_gain):
    groups = lax.axis_size("groups")
    devices_seq = lax.axis_size("seq")
    tok_rows, channels = signal.shape
    low, high = filter_spectrum.shape[1:3]
    fits = (
        groups == 2
        and channels == groups * devices_seq * HALF
        and low == 8
        and tok_rows == low * high // 2
        and tok_rows % 32 == 0
        and devices_seq % 2 == 0
    )
    plan = spread_kernels if fits else spread_plain
    return plan(signal, input_gate, output_gate, filter_spectrum, skip_gain)


def solution(mesh):
    return jax.shard_map(
        on_device,
        mesh=mesh,
        in_specs=(P(EVERY, None), P(EVERY, None), P(EVERY, None), P(None, "seq", None, None), P()),
        out_specs=P(EVERY, None),
        check_vma=False,
    )
```

```python
import functools
import math

import jax
import jax.numpy as jnp
import ml_dtypes
import numpy as np
from jax import lax
from jax.experimental import pallas as pl
from jax.experimental.pallas import tpu as pltpu
from jax.sharding import PartitionSpec as P

EVERY = ("groups", "seq")
PAIRS = ("seq", "groups")
LANES = 128
HALF = LANES // 2
PAD = 8
BF16 = jnp.bfloat16
F32 = jnp.float32


def exchange(values, axes=EVERY):
    return lax.all_to_all(values, axes, split_axis=0, concat_axis=0, tiled=True)


def left_lanes(rows):
    return lax.broadcasted_iota(jnp.int32, (rows, LANES), 1) < HALF


def swap_halves(first, second):
    left = left_lanes(first.shape[0])
    return (
        jnp.where(left, first, pltpu.roll(second, HALF, 1)),
        jnp.where(left, pltpu.roll(first, HALF, 1), second),
    )


def hi_lo(matrix):
    high = matrix.astype(ml_dtypes.bfloat16)
    low = (matrix - high.astype(np.float64)).astype(ml_dtypes.bfloat16)
    return high, low


@functools.lru_cache(None)
def tables(half_rows, width):
    full_rows = 2 * half_rows
    length = full_rows * width
    low_index = np.arange(half_rows)
    angle = 2 * np.pi * (np.outer(low_index, low_index) % full_rows) / full_rows
    real_part, imag_part = np.cos(angle), -np.sin(angle)
    imag_part[0] = 1.0 - 2.0 * (low_index % 2)
    first = np.concatenate([real_part, imag_part], 0)
    last = first.T / length
    inner = np.arange(width)
    angle = 2 * np.pi * (np.outer(inner, inner) % width) / width
    cosine, sine = np.cos(angle), np.sin(angle)
    second = np.block([[cosine, sine], [-sine, cosine]])
    third = np.block([[cosine, -sine], [sine, cosine]])
    first_hi, first_lo = hi_lo(first)
    second_hi, second_lo = hi_lo(second)
    third_hi, third_lo = hi_lo(third)
    last_hi, last_lo = hi_lo(last)
    turn = np.zeros((half_rows // 8 + 1, width, LANES), np.float32)
    for block in range(half_rows // 8 + 1):
        angle = 2 * np.pi * np.outer(inner, 8 * block + np.arange(8)) / length
        turn[block, :, :8] = np.cos(angle)
        turn[block, :, 8:16] = np.sin(angle)
    return (
        np.concatenate([first_hi, first_lo], 1),
        np.concatenate([second_hi, second_lo, second_hi], 1),
        np.block([[third_hi, third_lo], [last_hi, last_lo]]),
        turn,
    )


def pack_input_kernel(signal_ref, gate_ref, out_ref):
    rows = signal_ref.shape[0] // 2
    for block in range(signal_ref.shape[1] // LANES):
        lanes = pl.ds(block * LANES, LANES)
        gated = signal_ref[:, lanes].astype(F32) * gate_ref[:, lanes].astype(F32)
        first, second = swap_halves(gated[:rows], gated[rows:])
        out_ref[2 * block, 0] = first.astype(BF16)
        out_ref[2 * block + 1, 0] = second.astype(BF16)


def pack_input(signal, input_gate, devices_seq):
    tok_rows, channels = signal.shape
    wide = channels // 2
    return pl.pallas_call(
        pack_input_kernel,
        out_shape=jax.ShapeDtypeStruct((devices_seq, 2, tok_rows // 2, LANES), BF16),
        grid=(2,),
        in_specs=[pl.BlockSpec((tok_rows, wide), lambda b: (0, b))] * 2,
        out_specs=pl.BlockSpec((devices_seq, 1, tok_rows // 2, LANES), lambda b: (0, b, 0, 0)),
        cost_estimate=pl.CostEstimate(
            flops=signal.size, bytes_accessed=6 * signal.size, transcendentals=0
        ),
        name="pack_input",
    )(signal, input_gate)


def pack_filter_kernel(place_ref, filter_ref, *refs, middle):
    out_refs, chunks_ref = refs[:-1], refs[-1]
    low_count, width = filter_ref.shape[1:3]
    chunks = chunks_ref.shape[0]
    seq = place_ref[1]
    row = lax.broadcasted_iota(jnp.int32, (width, width), 0)
    col = lax.broadcasted_iota(jnp.int32, (width, width), 1)
    for low in range(low_count):
        mirrored = seq * low_count + low > middle
        order = jnp.where(col == jnp.where(mirrored, width - 1 - row, row), 1.0, 0.0).astype(BF16)
        sign = jnp.where(mirrored, -1.0, 1.0).astype(F32)
        for block in range(chunks // 2):
            lanes = pl.ds(block * LANES, LANES)
            both = jnp.concatenate(
                [filter_ref[0, low, :, lanes], filter_ref[1, low, :, lanes]], 1
            ).astype(BF16)
            both = jnp.dot(order, both, preferred_element_type=F32)
            halves = swap_halves(both[:, :LANES], sign * both[:, LANES:])
            rows = pl.ds(low * width, width)
            for half in range(2):
                near = (2 * block + half) ^ (seq % chunks)
                chunks_ref[near, rows, :] = halves[half].astype(BF16)
    for step in range(len(out_refs) // chunks):

        @pl.when(pl.program_id(0) == step)
        def _():
            for near in range(chunks):
                out_refs[chunks * step + near][...] = chunks_ref[near]


def pack_filter(filter_spectrum, devices_seq):
    _, low, width, channels = filter_spectrum.shape
    chunks = 4
    wide = chunks * HALF
    steps = devices_seq // chunks
    size = low * width * channels // 2
    block = (low * width, LANES)

    def lanes_of(step, place):
        return (0, 0, 0, place[0] * steps + ((place[1] // chunks) ^ step))

    return pl.pallas_call(
        functools.partial(pack_filter_kernel, middle=low * devices_seq // 2),
        out_shape=[jax.ShapeDtypeStruct(block, BF16)] * devices_seq,
        grid_spec=pltpu.PrefetchScalarGridSpec(
            num_scalar_prefetch=1,
            grid=(steps,),
            in_specs=[pl.BlockSpec((2, low, width, wide), lanes_of)],
            out_specs=[pl.BlockSpec(block, lambda step, place: (0, 0))] * devices_seq,
            scratch_shapes=[pltpu.VMEM((chunks, *block), BF16)],
        ),
        compiler_params=pltpu.CompilerParams(vmem_limit_bytes=16 << 20),
        cost_estimate=pl.CostEstimate(
            flops=4 * width * size, bytes_accessed=12 * size, transcendentals=0
        ),
        name="pack_filter",
    )(
        jnp.stack([lax.axis_index("groups"), lax.axis_index("seq")]),
        pltpu.with_memory_space_constraint(filter_spectrum, pltpu.HBM),
    )


def swap_with(values, distance):
    count = lax.axis_size("seq")
    return lax.ppermute(values, "seq", [(i, i ^ distance) for i in range(count)])


def split_bf16(values):
    high = values.astype(BF16)
    return high, (values - high.astype(F32)).astype(BF16)


def forward_kernel(
    got_ref, first_ref, second_ref, turn_ref, out_ref, rows_ref, stage_ref, *, devices_seq
):
    width = turn_ref.shape[1]
    half_rows = out_ref.shape[0] - 1
    full_rows = 2 * half_rows
    pitch = width + PAD
    tall = full_rows + PAD
    lines = got_ref.shape[2] // width
    for source in range(devices_seq):
        for line in range(lines):
            at = pl.ds(line * width, width)
            halves = swap_halves(
                got_ref[source, 0, at, :].astype(F32), got_ref[source, 1, at, :].astype(F32)
            )
            for half in range(2):
                row = (2 * source + half) * lines + line
                rows_ref[pl.ds(row * pitch, width), :] = halves[half]
    first_matrix = first_ref[...]
    second_matrix = second_ref[...]

    def first_stage(step, carry):
        for u in range(0, 8, 2):
            pair = jnp.concatenate(
                [
                    rows_ref[pl.ds(8 * step + u + v, half_rows, stride=pitch), :].astype(BF16)
                    for v in range(2)
                ],
                1,
            )
            pair = jnp.concatenate([pair, pair], 0)
            done = jnp.dot(first_matrix, pair, preferred_element_type=F32)
            for v in range(2):
                at = pl.multiple_of((8 * step + u + v) * tall, PAD)
                stage_ref[pl.ds(at, full_rows), :] = done[:, v * LANES : (v + 1) * LANES]
        return carry

    lax.fori_loop(0, width // 8, first_stage, 0)

    def turned(real, imag, block, u):
        cosine = turn_ref[block, :, u : u + 1]
        sine = turn_ref[block, :, 8 + u : 9 + u]
        if imag is None:
            return jnp.concatenate([real * cosine, -real * sine], 0)
        return jnp.concatenate([real * cosine + imag * sine, imag * cosine - real * sine], 0)

    def transform(values):
        high, low = split_bf16(values)
        return jnp.dot(
            second_matrix, jnp.concatenate([high, high, low], 0), preferred_element_type=F32
        )

    def second_stage(block, carry):
        for u in range(0, 8, 2):
            pair = []
            for v in range(u, u + 2):
                at = 8 * block + v
                real = stage_ref[pl.ds(at, width, stride=tall), :]
                imag = stage_ref[pl.ds(half_rows + at, width, stride=tall), :]
                if v == 0:
                    imag = imag * jnp.where(block == 0, 0.0, 1.0).astype(F32)
                pair.append(turned(real, imag, block, v))
            done = transform(jnp.concatenate(pair, 1))
            for v in range(2):
                out_ref[8 * block + u + v] = done[:, v * LANES : (v + 1) * LANES]
        return carry

    lax.fori_loop(0, half_rows // 8, second_stage, 0)
    real = stage_ref[pl.ds(half_rows, width, stride=tall), :]
    out_ref[half_rows] = transform(turned(real, None, half_rows // 8, 0))


def forward(got, devices_seq, width):
    half_rows = got.size // (LANES * width)
    first, second, _, turn = tables(half_rows, width)
    return pl.pallas_call(
        functools.partial(forward_kernel, devices_seq=devices_seq),
        out_shape=jax.ShapeDtypeStruct((half_rows + 1, 2 * width, LANES), F32),
        scratch_shapes=[
            pltpu.VMEM((half_rows * (width + PAD), LANES), F32),
            pltpu.VMEM((width * (2 * half_rows + PAD), LANES), F32),
        ],
        compiler_params=pltpu.CompilerParams(vmem_limit_bytes=16 << 20),
        cost_estimate=pl.CostEstimate(
            flops=2 * LANES * (first.size * width + second.size * half_rows),
            bytes_accessed=2 * got.size + 8 * half_rows * width * LANES,
            transcendentals=0,
        ),
        name="forward",
    )(got, first, second, turn)


def inverse_kernel(
    place_ref, spec_hbm, matrices_hbm, *refs, devices_seq
):
    filter_hbm = refs[:devices_seq]
    turn_ref, out_ref, spec_ref, filter_ref, matrices_ref = refs[devices_seq : devices_seq + 5]
    real_ref, imag_ref, rows_ref, sems, filter_sems = refs[devices_seq + 5 :]
    width = turn_ref.shape[1]
    half_rows = spec_ref.shape[0] - 1
    pitch = width + PAD
    per_source = 8
    left = left_lanes(width)

    top_block = half_rows // per_source

    def fetch(block, count=per_source):
        at = pl.ds(per_source * block, count)
        return pltpu.make_async_copy(spec_hbm.at[at], spec_ref.at[at], sems.at[block])

    matrices = pltpu.make_async_copy(matrices_hbm, matrices_ref, sems.at[top_block + 1])
    matrices.start()
    fetch(0).start()
    for distance in range(devices_seq):
        source = place_ref[0] ^ distance
        pltpu.make_async_copy(
            filter_hbm[distance], filter_ref.at[source], filter_sems.at[source]
        ).start()
    for block in range(1, top_block):
        fetch(block).start()
    fetch(top_block, 1).start()
    matrices.wait()

    def arrival(source):
        return pltpu.make_async_copy(
            filter_hbm[0], filter_ref.at[source], filter_sems.at[source]
        )

    def response_of(low):
        return filter_ref[low // per_source, pl.ds(low % per_source * width, width), :].astype(F32)
    third_matrix = matrices_ref[: 2 * width]
    last_matrix = matrices_ref[2 * width :]

    def filtered(spec, response):
        turned = pltpu.roll(response, HALF, 1)
        real_part = jnp.where(left, response, turned)
        imag_part = jnp.where(left, turned, response)
        real, imag = spec[:width], spec[width:]
        return jnp.concatenate(
            [real * real_part - imag * imag_part, real * imag_part + imag * real_part], 0
        ).astype(BF16)

    def transform(values):
        return jnp.dot(
            third_matrix, jnp.concatenate([values, values], 0), preferred_element_type=F32
        )

    def turned_back(values, block, u):
        cosine = turn_ref[block, :, u : u + 1]
        sine = turn_ref[block, :, 8 + u : 9 + u]
        real, imag = values[:width], values[width:]
        return real * cosine - imag * sine, real * sine + imag * cosine

    for block in range(top_block):
        fetch(block).wait()
        arrival(block).wait()
        arrival(devices_seq - 1 - block).wait()
        for u in range(0, per_source, 2):
            pair = []
            for v in range(u, u + 2):
                low = per_source * block + v
                response = response_of(low)
                if low:
                    response = response + response_of(2 * half_rows - low)
                pair.append(filtered(spec_ref[low], response))
            done = transform(jnp.concatenate(pair, 1))
            for v in range(2):
                real, imag = turned_back(done[:, v * LANES : (v + 1) * LANES], block, u + v)
                at = pl.ds((per_source * block + u + v) * pitch, width)
                real_ref[at, :] = real
                imag_ref[at, :] = imag
    fetch(top_block, 1).wait()
    done = transform(filtered(spec_ref[half_rows], response_of(half_rows)))
    imag_ref[pl.ds(0, width), :] = turned_back(done, top_block, 0)[0]

    def last_stage(step, carry):
        for u in range(0, 8, 2):
            pair = []
            for v in range(u, u + 2):
                rows = pl.ds(8 * step + v, half_rows, stride=pitch)
                pair.append(jnp.concatenate([real_ref[rows, :], imag_ref[rows, :]], 0).astype(BF16))
            pair = jnp.concatenate(pair, 1)
            done = jnp.dot(
                last_matrix, jnp.concatenate([pair, pair], 0), preferred_element_type=F32
            )
            for v in range(2):
                rows = pl.ds(8 * step + u + v, half_rows, stride=pitch)
                rows_ref[rows, :] = done[:, v * LANES : (v + 1) * LANES]
        return carry

    lax.fori_loop(0, width // 8, last_stage, 0, unroll=True)
    lines = out_ref.shape[2] // width
    for source in range(devices_seq):
        for line in range(lines):
            first, second = swap_halves(
                *(
                    rows_ref[pl.ds(((2 * source + half) * lines + line) * pitch, width), :]
                    for half in range(2)
                )
            )
            at = pl.ds(line * width, width)
            out_ref[source, 0, at, :] = first.astype(BF16)
            out_ref[source, 1, at, :] = second.astype(BF16)


def inverse(spectrum, arrived, devices_seq, piece):
    width = spectrum.shape[1] // 2
    half_rows = spectrum.shape[0] - 1
    _, _, matrices, turn = tables(half_rows, width)
    return pl.pallas_call(
        functools.partial(inverse_kernel, devices_seq=devices_seq),
        out_shape=jax.ShapeDtypeStruct((devices_seq, 2, piece, LANES), BF16),
        in_specs=[pl.BlockSpec(memory_space=pltpu.SMEM)]
        + [pl.BlockSpec(memory_space=pltpu.HBM)] * (2 + devices_seq)
        + [pl.BlockSpec(memory_space=pltpu.VMEM)],
        scratch_shapes=[
            pltpu.VMEM(spectrum.shape, F32),
            pltpu.VMEM((devices_seq, *arrived[0].shape), BF16),
            pltpu.VMEM(matrices.shape, BF16),
        ]
        + [pltpu.VMEM((half_rows * (width + PAD), LANES), F32)] * 3
        + [pltpu.SemaphoreType.DMA((half_rows // 8 + 2,)), pltpu.SemaphoreType.DMA((devices_seq,))],
        compiler_params=pltpu.CompilerParams(vmem_limit_bytes=20 << 20),
        cost_estimate=pl.CostEstimate(
            flops=2 * LANES * matrices.size * width,
            bytes_accessed=4 * spectrum.size + 2 * devices_seq * arrived[0].size,
            transcendentals=0,
        ),
        name="inverse",
    )(
        lax.axis_index("seq").reshape(1),
        *(
            pltpu.with_memory_space_constraint(operand, pltpu.HBM)
            for operand in (spectrum, jnp.asarray(matrices), *arrived)
        ),
        turn,
    )


def mix_kernel(conv_ref, signal_ref, gate_ref, out_gate_ref, gain_ref, out_ref):
    rows = signal_ref.shape[0] // 2
    for block in range(signal_ref.shape[1] // LANES):
        lanes = pl.ds(block * LANES, LANES)
        gain = gain_ref[:, lanes]
        place = divmod(2 * block, conv_ref.shape[0])
        halves = swap_halves(
            conv_ref[place[1], place[0]].astype(F32), conv_ref[place[1] + 1, place[0]].astype(F32)
        )
        for half, convolved in enumerate(halves):
            at = pl.ds(half * rows, rows)
            gated = signal_ref[at, lanes].astype(F32) * gate_ref[at, lanes].astype(F32)
            gated = gated.astype(BF16).astype(F32)
            mixed = out_gate_ref[at, lanes].astype(F32) * (convolved + gain * gated)
            out_ref[at, lanes] = mixed.astype(BF16)


def mix(conv, signal, input_gate, output_gate, skip_gain):
    return pl.pallas_call(
        mix_kernel,
        out_shape=jax.ShapeDtypeStruct(signal.shape, BF16),
        in_specs=[pl.BlockSpec(memory_space=pltpu.VMEM)] * 5,
        compiler_params=pltpu.CompilerParams(vmem_limit_bytes=16 << 20),
        cost_estimate=pl.CostEstimate(
            flops=4 * signal.size, bytes_accessed=10 * signal.size, transcendentals=0
        ),
        name="mix",
    )(conv, signal, input_gate, output_gate, skip_gain[None, :])


def spread_kernels(signal, input_gate, output_gate, filter_spectrum, skip_gain):
    devices_seq = lax.axis_size("seq")
    width = filter_spectrum.shape[2]

    def pairs(values):
        return exchange(values.reshape(-1, *values.shape[2:]), PAIRS).reshape(values.shape)

    got = pairs(pack_input(signal, input_gate, devices_seq))
    packed = pack_filter(filter_spectrum, devices_seq)
    arrived = [packed[0]] + [swap_with(packed[d], d) for d in range(1, devices_seq)]
    spectrum = forward(got, devices_seq, width)
    conv = inverse(spectrum, arrived, devices_seq, signal.shape[0] // 2)
    return mix(pairs(conv), signal, input_gate, output_gate, skip_gain)


def angle_table(rows_count, cols_count, length):
    row_index = lax.iota(jnp.int32, rows_count)
    col_index = lax.iota(jnp.int32, cols_count)
    product = row_index[:, None] * col_index[None, :] % length
    angles = product.astype(jnp.float32) * (2.0 * math.pi / length)
    return (jnp.cos(angles), jnp.sin(angles))


def contract_first(matrix, values):
    return jnp.einsum("kn,nbc->kbc", matrix, values, precision=lax.Precision.HIGH)


def contract_second(matrix, values):
    return jnp.einsum("kn,anc->akc", matrix, values, precision=lax.Precision.HIGH)


def convolve(signal_rows, spectra_real, spectra_imag):
    half_rows, width, _ = signal_rows.shape
    full_rows = 2 * half_rows
    length = full_rows * width
    cos_one, sin_one = angle_table(full_rows, half_rows, full_rows)
    cos_two, sin_two = angle_table(width, width, width)
    turn_cos, turn_sin = angle_table(full_rows, width, length)
    turn_cos = turn_cos[:, :, None]
    turn_sin = turn_sin[:, :, None]
    first_real = contract_first(cos_one, signal_rows)
    first_imag = -contract_first(sin_one, signal_rows)
    twist_real = first_real * turn_cos + first_imag * turn_sin
    twist_imag = first_imag * turn_cos - first_real * turn_sin
    spec_real = contract_second(cos_two, twist_real) + contract_second(sin_two, twist_imag)
    spec_imag = contract_second(cos_two, twist_imag) - contract_second(sin_two, twist_real)
    prod_real = spec_real * spectra_real - spec_imag * spectra_imag
    prod_imag = spec_real * spectra_imag + spec_imag * spectra_real
    back_real = contract_second(cos_two, prod_real) - contract_second(sin_two, prod_imag)
    back_imag = contract_second(sin_two, prod_real) + contract_second(cos_two, prod_imag)
    rotated_real = back_real * turn_cos - back_imag * turn_sin
    rotated_imag = back_real * turn_sin + back_imag * turn_cos
    summed = contract_first(cos_one.T, rotated_real) - contract_first(sin_one.T, rotated_imag)
    return summed * (1.0 / length)


def spread_plain(signal, input_gate, output_gate, filter_spectrum, skip_gain):
    tok_rows, channels = signal.shape
    groups = lax.axis_size("groups")
    devices_seq = lax.axis_size("seq")
    parts = groups * devices_seq
    width = channels // parts
    low, high = filter_spectrum.shape[1:3]
    share = low // groups
    gated_input = (input_gate.astype(jnp.float32) * signal.astype(jnp.float32)).astype(jnp.bfloat16)

    sent = gated_input.reshape(tok_rows, parts, width).transpose(1, 0, 2).reshape(parts, -1, 128)
    got = exchange(sent).reshape(groups, devices_seq, tok_rows, width)
    rows = got.transpose(1, 2, 0, 3).reshape(-1, high, groups * width)

    mine = lax.dynamic_slice_in_dim(filter_spectrum, lax.axis_index("groups") * share, share, axis=1)
    mine = mine.astype(jnp.bfloat16).reshape(2, share, high, parts, width)
    mine = mine.transpose(3, 0, 1, 2, 4).reshape(parts, -1, 128)
    spectra = exchange(mine).reshape(groups, devices_seq, 2, share, high, width)
    spectra = spectra.transpose(2, 1, 0, 3, 4, 5).reshape(2, -1, high, 1, width)
    spectra = jnp.broadcast_to(spectra, spectra.shape[:3] + (groups, width))
    spectra = spectra.reshape(2, -1, high, groups * width).astype(jnp.float32)

    conv = convolve(rows.astype(jnp.float32), spectra[0], spectra[1]).astype(jnp.bfloat16)
    conv = conv.reshape(devices_seq, tok_rows, groups, width).transpose(2, 0, 1, 3)
    back = exchange(conv.reshape(parts, -1, 128)).reshape(parts, tok_rows, width)
    convolved = back.transpose(1, 0, 2).reshape(tok_rows, channels).astype(jnp.float32)
    mixed_out = output_gate.astype(jnp.float32) * (
        convolved + skip_gain[None, :] * gated_input.astype(jnp.float32)
    )
    return mixed_out.astype(jnp.bfloat16)


def on_device(signal, input_gate, output_gate, filter_spectrum, skip_gain):
    groups = lax.axis_size("groups")
    devices_seq = lax.axis_size("seq")
    tok_rows, channels = signal.shape
    low, high = filter_spectrum.shape[1:3]
    fits = (
        groups == 2
        and channels == groups * devices_seq * HALF
        and low == 8
        and tok_rows == low * high // 2
        and tok_rows % 32 == 0
        and devices_seq >= 4
        and devices_seq & (devices_seq - 1) == 0
    )
    plan = spread_kernels if fits else spread_plain
    return plan(signal, input_gate, output_gate, filter_spectrum, skip_gain)


def solution(mesh):
    return jax.shard_map(
        on_device,
        mesh=mesh,
        in_specs=(P(EVERY, None), P(EVERY, None), P(EVERY, None), P(None, "seq", None, None), P()),
        out_specs=P(EVERY, None),
        check_vma=False,
    )
```

```python
import functools
import math

import jax
import jax.numpy as jnp
import ml_dtypes
import numpy as np
from jax import lax
from jax.experimental import pallas as pl
from jax.experimental.pallas import tpu as pltpu
from jax.sharding import PartitionSpec as P

EVERY = ("groups", "seq")
PAIRS = ("seq", "groups")
LANES = 128
HALF = LANES // 2
PAD = 8
BF16 = jnp.bfloat16
F32 = jnp.float32


def exchange(values, axes=EVERY):
    return lax.all_to_all(values, axes, split_axis=0, concat_axis=0, tiled=True)


def left_lanes(rows):
    return lax.broadcasted_iota(jnp.int32, (rows, LANES), 1) < HALF


def swap_halves(first, second):
    left = left_lanes(first.shape[0])
    return (
        jnp.where(left, first, pltpu.roll(second, HALF, 1)),
        jnp.where(left, pltpu.roll(first, HALF, 1), second),
    )


def hi_lo(matrix):
    high = matrix.astype(ml_dtypes.bfloat16)
    low = (matrix - high.astype(np.float64)).astype(ml_dtypes.bfloat16)
    return high, low


@functools.lru_cache(None)
def tables(half_rows, width):
    full_rows = 2 * half_rows
    length = full_rows * width
    low_index = np.arange(half_rows)
    angle = 2 * np.pi * (np.outer(low_index, low_index) % full_rows) / full_rows
    real_part, imag_part = np.cos(angle), -np.sin(angle)
    imag_part[0] = 1.0 - 2.0 * (low_index % 2)
    first = np.concatenate([real_part, imag_part], 0)
    last = first.T / length
    inner = np.arange(width)
    angle = 2 * np.pi * (np.outer(inner, inner) % width) / width
    cosine, sine = np.cos(angle), np.sin(angle)
    second = np.block([[cosine, sine], [-sine, cosine]])
    third = np.block([[cosine, -sine], [sine, cosine]])
    first_hi, first_lo = hi_lo(first)
    second_hi, second_lo = hi_lo(second)
    third_hi, third_lo = hi_lo(third)
    last_hi, last_lo = hi_lo(last)
    turn = np.zeros((half_rows // 8 + 1, width, LANES), np.float32)
    for block in range(half_rows // 8 + 1):
        angle = 2 * np.pi * np.outer(inner, 8 * block + np.arange(8)) / length
        turn[block, :, :8] = np.cos(angle)
        turn[block, :, 8:16] = np.sin(angle)
    return (
        np.concatenate([first_hi, first_lo], 1),
        np.concatenate([second_hi, second_lo, second_hi], 1),
        np.block([[third_hi, third_lo], [last_hi, last_lo]]),
        turn,
    )


def pack_input_kernel(signal_ref, gate_ref, out_ref):
    rows = signal_ref.shape[0] // 2
    for block in range(signal_ref.shape[1] // LANES):
        lanes = pl.ds(block * LANES, LANES)
        gated = signal_ref[:, lanes].astype(F32) * gate_ref[:, lanes].astype(F32)
        first, second = swap_halves(gated[:rows], gated[rows:])
        out_ref[2 * block, 0] = first.astype(BF16)
        out_ref[2 * block + 1, 0] = second.astype(BF16)


def pack_input(signal, input_gate, devices_seq):
    tok_rows, channels = signal.shape
    wide = channels // 2
    return pl.pallas_call(
        pack_input_kernel,
        out_shape=jax.ShapeDtypeStruct((devices_seq, 2, tok_rows // 2, LANES), BF16),
        grid=(2,),
        in_specs=[pl.BlockSpec((tok_rows, wide), lambda b: (0, b))] * 2,
        out_specs=pl.BlockSpec((devices_seq, 1, tok_rows // 2, LANES), lambda b: (0, b, 0, 0)),
        cost_estimate=pl.CostEstimate(
            flops=signal.size, bytes_accessed=6 * signal.size, transcendentals=0
        ),
        name="pack_input",
    )(signal, input_gate)


def pack_filter_kernel(place_ref, filter_ref, *refs, middle):
    out_refs, chunks_ref = refs[:-1], refs[-1]
    low_count, width = filter_ref.shape[1:3]
    chunks = chunks_ref.shape[0]
    seq = place_ref[1]
    row = lax.broadcasted_iota(jnp.int32, (width, width), 0)
    col = lax.broadcasted_iota(jnp.int32, (width, width), 1)
    for low in range(low_count):
        mirrored = seq * low_count + low > middle
        order = jnp.where(col == jnp.where(mirrored, width - 1 - row, row), 1.0, 0.0).astype(BF16)
        sign = jnp.where(mirrored, -1.0, 1.0).astype(F32)
        for block in range(chunks // 2):
            lanes = pl.ds(block * LANES, LANES)
            both = jnp.concatenate(
                [filter_ref[0, low, :, lanes], filter_ref[1, low, :, lanes]], 1
            ).astype(BF16)
            both = jnp.dot(order, both, preferred_element_type=F32)
            halves = swap_halves(both[:, :LANES], sign * both[:, LANES:])
            rows = pl.ds(low * width, width)
            for half in range(2):
                near = (2 * block + half) ^ (seq % chunks)
                chunks_ref[near, rows, :] = halves[half].astype(BF16)
    for step in range(len(out_refs) // chunks):

        @pl.when(pl.program_id(0) == step)
        def _():
            for near in range(chunks):
                out_refs[chunks * step + near][...] = chunks_ref[near]


def pack_filter(filter_spectrum, devices_seq):
    _, low, width, channels = filter_spectrum.shape
    chunks = 4
    wide = chunks * HALF
    steps = devices_seq // chunks
    size = low * width * channels // 2
    block = (low * width, LANES)

    def lanes_of(step, place):
        return (0, 0, 0, place[0] * steps + ((place[1] // chunks) ^ step))

    return pl.pallas_call(
        functools.partial(pack_filter_kernel, middle=low * devices_seq // 2),
        out_shape=[pltpu.HBM(block, BF16)] * devices_seq,
        grid_spec=pltpu.PrefetchScalarGridSpec(
            num_scalar_prefetch=1,
            grid=(steps,),
            in_specs=[pl.BlockSpec((2, low, width, wide), lanes_of)],
            out_specs=[pl.BlockSpec(block, lambda step, place: (0, 0))] * devices_seq,
            scratch_shapes=[pltpu.VMEM((chunks, *block), BF16)],
        ),
        compiler_params=pltpu.CompilerParams(vmem_limit_bytes=16 << 20),
        cost_estimate=pl.CostEstimate(
            flops=4 * width * size, bytes_accessed=12 * size, transcendentals=0
        ),
        name="pack_filter",
    )(
        jnp.stack([lax.axis_index("groups"), lax.axis_index("seq")]),
        pltpu.with_memory_space_constraint(filter_spectrum, pltpu.HBM),
    )


def swap_with(values, distance):
    count = lax.axis_size("seq")
    return lax.ppermute(values, "seq", [(i, i ^ distance) for i in range(count)])


def split_bf16(values):
    high = values.astype(BF16)
    return high, (values - high.astype(F32)).astype(BF16)


def forward_kernel(
    got_ref, first_ref, second_ref, turn_ref, out_ref, rows_ref, stage_ref, *, devices_seq
):
    width = turn_ref.shape[1]
    half_rows = out_ref.shape[0] - 1
    full_rows = 2 * half_rows
    pitch = width + PAD
    tall = full_rows + PAD
    lines = got_ref.shape[2] // width
    for source in range(devices_seq):
        for line in range(lines):
            at = pl.ds(line * width, width)
            halves = swap_halves(
                got_ref[source, 0, at, :].astype(F32), got_ref[source, 1, at, :].astype(F32)
            )
            for half in range(2):
                row = (2 * source + half) * lines + line
                rows_ref[pl.ds(row * pitch, width), :] = halves[half]
    first_matrix = first_ref[...]
    second_matrix = second_ref[...]

    def first_stage(step, carry):
        for u in range(0, 8, 2):
            pair = jnp.concatenate(
                [
                    rows_ref[pl.ds(8 * step + u + v, half_rows, stride=pitch), :].astype(BF16)
                    for v in range(2)
                ],
                1,
            )
            pair = jnp.concatenate([pair, pair], 0)
            done = jnp.dot(first_matrix, pair, preferred_element_type=F32)
            for v in range(2):
                at = pl.multiple_of((8 * step + u + v) * tall, PAD)
                stage_ref[pl.ds(at, full_rows), :] = done[:, v * LANES : (v + 1) * LANES]
        return carry

    lax.fori_loop(0, width // 8, first_stage, 0)

    def turned(real, imag, block, u):
        cosine = turn_ref[block, :, u : u + 1]
        sine = turn_ref[block, :, 8 + u : 9 + u]
        if imag is None:
            return jnp.concatenate([real * cosine, -real * sine], 0)
        return jnp.concatenate([real * cosine + imag * sine, imag * cosine - real * sine], 0)

    def transform(values):
        high, low = split_bf16(values)
        return jnp.dot(
            second_matrix, jnp.concatenate([high, high, low], 0), preferred_element_type=F32
        )

    def second_stage(block, carry):
        for u in range(0, 8, 2):
            pair = []
            for v in range(u, u + 2):
                at = 8 * block + v
                real = stage_ref[pl.ds(at, width, stride=tall), :]
                imag = stage_ref[pl.ds(half_rows + at, width, stride=tall), :]
                if v == 0:
                    imag = imag * jnp.where(block == 0, 0.0, 1.0).astype(F32)
                pair.append(turned(real, imag, block, v))
            done = transform(jnp.concatenate(pair, 1))
            for v in range(2):
                out_ref[8 * block + u + v] = done[:, v * LANES : (v + 1) * LANES]
        return carry

    lax.fori_loop(0, half_rows // 8, second_stage, 0)
    real = stage_ref[pl.ds(half_rows, width, stride=tall), :]
    out_ref[half_rows] = transform(turned(real, None, half_rows // 8, 0))


def forward(got, devices_seq, width):
    half_rows = got.size // (LANES * width)
    first, second, _, turn = tables(half_rows, width)
    return pl.pallas_call(
        functools.partial(forward_kernel, devices_seq=devices_seq),
        out_shape=pltpu.HBM((half_rows + 1, 2 * width, LANES), F32),
        scratch_shapes=[
            pltpu.VMEM((half_rows * (width + PAD), LANES), F32),
            pltpu.VMEM((width * (2 * half_rows + PAD), LANES), F32),
        ],
        compiler_params=pltpu.CompilerParams(vmem_limit_bytes=16 << 20),
        cost_estimate=pl.CostEstimate(
            flops=2 * LANES * (first.size * width + second.size * half_rows),
            bytes_accessed=2 * got.size + 8 * half_rows * width * LANES,
            transcendentals=0,
        ),
        name="forward",
    )(got, first, second, turn)


def inverse_kernel(
    place_ref, spec_hbm, matrices_hbm, *refs, devices_seq
):
    filter_hbm = refs[:devices_seq]
    turn_ref, out_ref, spec_ref, filter_ref, lead_ref, matrices_ref = refs[
        devices_seq : devices_seq + 6
    ]
    real_ref, imag_ref, rows_ref, sems, filter_sems = refs[devices_seq + 6 :]
    width = turn_ref.shape[1]
    half_rows = spec_ref.shape[0] - 1
    pitch = width + PAD
    per_source = 8
    left = left_lanes(width)

    top_block = half_rows // per_source

    place = place_ref[0]
    upper = place >= top_block

    def block_of(distance):
        source = place ^ distance
        return jnp.where(upper, devices_seq - 1 - source, source)

    def fetch(distance):
        at = pl.ds(per_source * block_of(distance), per_source)
        return pltpu.make_async_copy(spec_hbm.at[at], spec_ref.at[at], sems.at[distance])

    def arrival(distance):
        return pltpu.make_async_copy(
            filter_hbm[distance], filter_ref.at[distance], filter_sems.at[distance]
        )

    top_rows = pl.ds(half_rows, 1)
    top = pltpu.make_async_copy(
        spec_hbm.at[top_rows], spec_ref.at[top_rows], sems.at[top_block]
    )
    matrices = pltpu.make_async_copy(matrices_hbm, matrices_ref, sems.at[top_block + 1])
    matrices.start()
    for distance in range(top_block):
        fetch(distance).start()
        arrival(distance).start()
        arrival(devices_seq - 1 - distance).start()
    top.start()
    matrices.wait()
    third_matrix = matrices_ref[: 2 * width]
    last_matrix = matrices_ref[2 * width :]

    def response_of(distance, at):
        far = devices_seq - 1 - distance
        row = pl.ds(at * width, width)
        mirror = pl.ds((per_source - at) * width, width)
        lower = jnp.where(upper, filter_ref[far, row], filter_ref[distance, row])
        higher = jnp.where(upper, filter_ref[distance, mirror], filter_ref[far, mirror])
        return lower.astype(F32) + higher.astype(F32)

    def filtered(spec, response):
        turned = pltpu.roll(response, HALF, 1)
        real_part = jnp.where(left, response, turned)
        imag_part = jnp.where(left, turned, response)
        real, imag = spec[:width], spec[width:]
        return jnp.concatenate(
            [real * real_part - imag * imag_part, real * imag_part + imag * real_part], 0
        ).astype(BF16)

    def transform(values):
        return jnp.dot(
            third_matrix, jnp.concatenate([values, values], 0), preferred_element_type=F32
        )

    def turned_back(values, block, u):
        cosine = turn_ref[block, :, u : u + 1]
        sine = turn_ref[block, :, 8 + u : 9 + u]
        real, imag = values[:width], values[width:]
        return real * cosine - imag * sine, real * sine + imag * cosine

    def third_stage(slots):
        values = jnp.concatenate(
            [filtered(spec_ref[low], response) for low, response, _, _ in slots], 1
        )
        done = transform(values)
        results = []
        for v, (_, _, block, u) in enumerate(slots):
            results.append(turned_back(done[:, v * LANES : (v + 1) * LANES], block, u))
        return results

    def keep(low, values):
        at = low * pitch if isinstance(low, int) else pl.multiple_of(low * pitch, PAD)
        real_ref[pl.ds(at, width), :] = values[0]
        imag_ref[pl.ds(at, width), :] = values[1]

    for distance in range(top_block):
        block = block_of(distance)
        far = devices_seq - 1 - distance
        fetch(distance).wait()
        arrival(distance).wait()
        arrival(far).wait()
        for near in (distance, far):
            lead_ref[place ^ near] = filter_ref[near, :width].astype(F32)
        slots = [
            (per_source * block + v, response_of(distance, v), block, v)
            for v in range(1, per_source)
        ]
        for at in range(0, len(slots), 2):
            pair = slots[at : at + 2]
            for slot, values in zip(pair, third_stage(pair)):
                keep(slot[0], values)
    top.wait()
    slots = [(0, lead_ref[0], 0, 0), (half_rows, lead_ref[top_block], top_block, 0)]
    first, middle = third_stage(slots)
    keep(0, (first[0], middle[0]))
    slots = [
        (per_source * block, lead_ref[block] + lead_ref[devices_seq - block], block, 0)
        for block in range(1, top_block)
    ]
    for at in range(0, len(slots), 2):
        pair = slots[at : at + 2]
        for slot, values in zip(pair, third_stage(pair)):
            keep(slot[0], values)

    def last_stage(step, carry):
        for u in range(0, 8, 2):
            pair = []
            for v in range(u, u + 2):
                rows = pl.ds(8 * step + v, half_rows, stride=pitch)
                pair.append(jnp.concatenate([real_ref[rows, :], imag_ref[rows, :]], 0).astype(BF16))
            pair = jnp.concatenate(pair, 1)
            done = jnp.dot(
                last_matrix, jnp.concatenate([pair, pair], 0), preferred_element_type=F32
            )
            for v in range(2):
                rows = pl.ds(8 * step + u + v, half_rows, stride=pitch)
                rows_ref[rows, :] = done[:, v * LANES : (v + 1) * LANES]
        return carry

    lax.fori_loop(0, width // 8, last_stage, 0, unroll=True)
    lines = out_ref.shape[2] // width
    for source in range(devices_seq):
        for line in range(lines):
            first, second = swap_halves(
                *(
                    rows_ref[pl.ds(((2 * source + half) * lines + line) * pitch, width), :]
                    for half in range(2)
                )
            )
            at = pl.ds(line * width, width)
            out_ref[source, 0, at, :] = first.astype(BF16)
            out_ref[source, 1, at, :] = second.astype(BF16)


def inverse(spectrum, arrived, devices_seq, piece):
    width = spectrum.shape[1] // 2
    half_rows = spectrum.shape[0] - 1
    _, _, matrices, turn = tables(half_rows, width)
    return pl.pallas_call(
        functools.partial(inverse_kernel, devices_seq=devices_seq),
        out_shape=jax.ShapeDtypeStruct((devices_seq, 2, piece, LANES), BF16),
        in_specs=[pl.BlockSpec(memory_space=pltpu.SMEM)]
        + [pl.BlockSpec(memory_space=pltpu.HBM)] * (2 + devices_seq)
        + [pl.BlockSpec(memory_space=pltpu.VMEM)],
        scratch_shapes=[
            pltpu.VMEM(spectrum.shape, F32),
            pltpu.VMEM((devices_seq, *arrived[0].shape), BF16),
            pltpu.VMEM((devices_seq, width, LANES), F32),
            pltpu.VMEM(matrices.shape, BF16),
        ]
        + [pltpu.VMEM((half_rows * (width + PAD), LANES), F32)] * 3
        + [pltpu.SemaphoreType.DMA((half_rows // 8 + 2,)), pltpu.SemaphoreType.DMA((devices_seq,))],
        compiler_params=pltpu.CompilerParams(vmem_limit_bytes=20 << 20),
        cost_estimate=pl.CostEstimate(
            flops=2 * LANES * matrices.size * width,
            bytes_accessed=4 * spectrum.size + 2 * devices_seq * arrived[0].size,
            transcendentals=0,
        ),
        name="inverse",
    )(
        lax.axis_index("seq").reshape(1),
        *(
            pltpu.with_memory_space_constraint(operand, pltpu.HBM)
            for operand in (spectrum, jnp.asarray(matrices), *arrived)
        ),
        turn,
    )


def mix_kernel(conv_ref, signal_ref, gate_ref, out_gate_ref, gain_ref, out_ref):
    rows = signal_ref.shape[0] // 2
    for block in range(signal_ref.shape[1] // LANES):
        lanes = pl.ds(block * LANES, LANES)
        gain = gain_ref[:, lanes]
        place = divmod(2 * block, conv_ref.shape[0])
        halves = swap_halves(
            conv_ref[place[1], place[0]].astype(F32), conv_ref[place[1] + 1, place[0]].astype(F32)
        )
        for half, convolved in enumerate(halves):
            at = pl.ds(half * rows, rows)
            gated = signal_ref[at, lanes].astype(F32) * gate_ref[at, lanes].astype(F32)
            gated = gated.astype(BF16).astype(F32)
            mixed = out_gate_ref[at, lanes].astype(F32) * (convolved + gain * gated)
            out_ref[at, lanes] = mixed.astype(BF16)


def mix(conv, signal, input_gate, output_gate, skip_gain):
    return pl.pallas_call(
        mix_kernel,
        out_shape=jax.ShapeDtypeStruct(signal.shape, BF16),
        in_specs=[pl.BlockSpec(memory_space=pltpu.VMEM)] * 5,
        compiler_params=pltpu.CompilerParams(vmem_limit_bytes=16 << 20),
        cost_estimate=pl.CostEstimate(
            flops=4 * signal.size, bytes_accessed=10 * signal.size, transcendentals=0
        ),
        name="mix",
    )(conv, signal, input_gate, output_gate, skip_gain[None, :])


def spread_kernels(signal, input_gate, output_gate, filter_spectrum, skip_gain):
    devices_seq = lax.axis_size("seq")
    width = filter_spectrum.shape[2]

    def pairs(values):
        return exchange(values.reshape(-1, *values.shape[2:]), PAIRS).reshape(values.shape)

    got = pairs(pack_input(signal, input_gate, devices_seq))
    packed = pack_filter(filter_spectrum, devices_seq)
    arrived = [packed[0]] + [swap_with(packed[d], d) for d in range(1, devices_seq)]
    spectrum = forward(got, devices_seq, width)
    conv = inverse(spectrum, arrived, devices_seq, signal.shape[0] // 2)
    return mix(pairs(conv), signal, input_gate, output_gate, skip_gain)


def angle_table(rows_count, cols_count, length):
    row_index = lax.iota(jnp.int32, rows_count)
    col_index = lax.iota(jnp.int32, cols_count)
    product = row_index[:, None] * col_index[None, :] % length
    angles = product.astype(jnp.float32) * (2.0 * math.pi / length)
    return (jnp.cos(angles), jnp.sin(angles))


def contract_first(matrix, values):
    return jnp.einsum("kn,nbc->kbc", matrix, values, precision=lax.Precision.HIGH)


def contract_second(matrix, values):
    return jnp.einsum("kn,anc->akc", matrix, values, precision=lax.Precision.HIGH)


def convolve(signal_rows, spectra_real, spectra_imag):
    half_rows, width, _ = signal_rows.shape
    full_rows = 2 * half_rows
    length = full_rows * width
    cos_one, sin_one = angle_table(full_rows, half_rows, full_rows)
    cos_two, sin_two = angle_table(width, width, width)
    turn_cos, turn_sin = angle_table(full_rows, width, length)
    turn_cos = turn_cos[:, :, None]
    turn_sin = turn_sin[:, :, None]
    first_real = contract_first(cos_one, signal_rows)
    first_imag = -contract_first(sin_one, signal_rows)
    twist_real = first_real * turn_cos + first_imag * turn_sin
    twist_imag = first_imag * turn_cos - first_real * turn_sin
    spec_real = contract_second(cos_two, twist_real) + contract_second(sin_two, twist_imag)
    spec_imag = contract_second(cos_two, twist_imag) - contract_second(sin_two, twist_real)
    prod_real = spec_real * spectra_real - spec_imag * spectra_imag
    prod_imag = spec_real * spectra_imag + spec_imag * spectra_real
    back_real = contract_second(cos_two, prod_real) - contract_second(sin_two, prod_imag)
    back_imag = contract_second(sin_two, prod_real) + contract_second(cos_two, prod_imag)
    rotated_real = back_real * turn_cos - back_imag * turn_sin
    rotated_imag = back_real * turn_sin + back_imag * turn_cos
    summed = contract_first(cos_one.T, rotated_real) - contract_first(sin_one.T, rotated_imag)
    return summed * (1.0 / length)


def spread_plain(signal, input_gate, output_gate, filter_spectrum, skip_gain):
    tok_rows, channels = signal.shape
    groups = lax.axis_size("groups")
    devices_seq = lax.axis_size("seq")
    parts = groups * devices_seq
    width = channels // parts
    low, high = filter_spectrum.shape[1:3]
    share = low // groups
    gated_input = (input_gate.astype(jnp.float32) * signal.astype(jnp.float32)).astype(jnp.bfloat16)

    sent = gated_input.reshape(tok_rows, parts, width).transpose(1, 0, 2).reshape(parts, -1, 128)
    got = exchange(sent).reshape(groups, devices_seq, tok_rows, width)
    rows = got.transpose(1, 2, 0, 3).reshape(-1, high, groups * width)

    mine = lax.dynamic_slice_in_dim(filter_spectrum, lax.axis_index("groups") * share, share, axis=1)
    mine = mine.astype(jnp.bfloat16).reshape(2, share, high, parts, width)
    mine = mine.transpose(3, 0, 1, 2, 4).reshape(parts, -1, 128)
    spectra = exchange(mine).reshape(groups, devices_seq, 2, share, high, width)
    spectra = spectra.transpose(2, 1, 0, 3, 4, 5).reshape(2, -1, high, 1, width)
    spectra = jnp.broadcast_to(spectra, spectra.shape[:3] + (groups, width))
    spectra = spectra.reshape(2, -1, high, groups * width).astype(jnp.float32)

    conv = convolve(rows.astype(jnp.float32), spectra[0], spectra[1]).astype(jnp.bfloat16)
    conv = conv.reshape(devices_seq, tok_rows, groups, width).transpose(2, 0, 1, 3)
    back = exchange(conv.reshape(parts, -1, 128)).reshape(parts, tok_rows, width)
    convolved = back.transpose(1, 0, 2).reshape(tok_rows, channels).astype(jnp.float32)
    mixed_out = output_gate.astype(jnp.float32) * (
        convolved + skip_gain[None, :] * gated_input.astype(jnp.float32)
    )
    return mixed_out.astype(jnp.bfloat16)


def on_device(signal, input_gate, output_gate, filter_spectrum, skip_gain):
    groups = lax.axis_size("groups")
    devices_seq = lax.axis_size("seq")
    tok_rows, channels = signal.shape
    low, high = filter_spectrum.shape[1:3]
    fits = (
        groups == 2
        and channels == groups * devices_seq * HALF
        and low == 8
        and tok_rows == low * high // 2
        and tok_rows % 32 == 0
        and devices_seq >= 4
        and devices_seq & (devices_seq - 1) == 0
    )
    plan = spread_kernels if fits else spread_plain
    return plan(signal, input_gate, output_gate, filter_spectrum, skip_gain)


def solution(mesh):
    return jax.shard_map(
        on_device,
        mesh=mesh,
        in_specs=(P(EVERY, None), P(EVERY, None), P(EVERY, None), P(None, "seq", None, None), P()),
        out_specs=P(EVERY, None),
        check_vma=False,
    )
```

```python
import functools
import math

import jax
import jax.numpy as jnp
import ml_dtypes
import numpy as np
from jax import lax
from jax.experimental import pallas as pl
from jax.experimental.pallas import tpu as pltpu
from jax.sharding import PartitionSpec as P

EVERY = ("groups", "seq")
PAIRS = ("seq", "groups")
LANES = 128
HALF = LANES // 2
PAD = 8
PIECES = 4
JOINED = (8, 10)
BF16 = jnp.bfloat16
F32 = jnp.float32


def exchange(values, axes=EVERY):
    return lax.all_to_all(values, axes, split_axis=0, concat_axis=0, tiled=True)


def left_lanes(rows):
    return lax.broadcasted_iota(jnp.int32, (rows, LANES), 1) < HALF


def swap_halves(first, second):
    left = left_lanes(first.shape[0])
    return (
        jnp.where(left, first, pltpu.roll(second, HALF, 1)),
        jnp.where(left, pltpu.roll(first, HALF, 1), second),
    )


def hi_lo(matrix):
    high = matrix.astype(ml_dtypes.bfloat16)
    low = (matrix - high.astype(np.float64)).astype(ml_dtypes.bfloat16)
    return high, low


@functools.lru_cache(None)
def tables(half_rows, width):
    full_rows = 2 * half_rows
    length = full_rows * width
    low_index = np.arange(half_rows)
    angle = 2 * np.pi * (np.outer(low_index, low_index) % full_rows) / full_rows
    real_part, imag_part = np.cos(angle), -np.sin(angle)
    imag_part[0] = 1.0 - 2.0 * (low_index % 2)
    first = np.concatenate([real_part, imag_part], 0)
    last = first.T / length
    inner = np.arange(width)
    angle = 2 * np.pi * (np.outer(inner, inner) % width) / width
    cosine, sine = np.cos(angle), np.sin(angle)
    second = np.block([[cosine, sine], [-sine, cosine]])
    third = np.block([[cosine, -sine], [sine, cosine]])
    first_hi, first_lo = hi_lo(first)
    second_hi, second_lo = hi_lo(second)
    third_hi, third_lo = hi_lo(third)
    last_hi, last_lo = hi_lo(last)
    turn = np.zeros((half_rows // 8 + 1, width, LANES), np.float32)
    for block in range(half_rows // 8 + 1):
        angle = 2 * np.pi * np.outer(inner, 8 * block + np.arange(8)) / length
        turn[block, :, :8] = np.cos(angle)
        turn[block, :, 8:16] = np.sin(angle)
    return (
        np.concatenate([first_hi, first_lo], 1),
        np.concatenate([second_hi, second_lo, second_hi], 1),
        np.block([[third_hi, third_lo], [last_hi, last_lo]]),
        turn,
    )


def pack_input_kernel(signal_ref, gate_ref, out_ref):
    rows = signal_ref.shape[0] // 2
    for block in range(signal_ref.shape[1] // LANES):
        lanes = pl.ds(block * LANES, LANES)
        gated = signal_ref[:, lanes].astype(F32) * gate_ref[:, lanes].astype(F32)
        first, second = swap_halves(gated[:rows], gated[rows:])
        out_ref[2 * block, 0] = first.astype(BF16)
        out_ref[2 * block + 1, 0] = second.astype(BF16)


def pack_input(signal, input_gate, devices_seq):
    tok_rows, channels = signal.shape
    wide = channels // 2
    return pl.pallas_call(
        pack_input_kernel,
        out_shape=jax.ShapeDtypeStruct((devices_seq, 2, tok_rows // 2, LANES), BF16),
        grid=(2,),
        in_specs=[pl.BlockSpec((tok_rows, wide), lambda b: (0, b))] * 2,
        out_specs=pl.BlockSpec((devices_seq, 1, tok_rows // 2, LANES), lambda b: (0, b, 0, 0)),
        cost_estimate=pl.CostEstimate(
            flops=signal.size, bytes_accessed=6 * signal.size, transcendentals=0
        ),
        name="pack_input",
    )(signal, input_gate)


def pack_filter_kernel(place_ref, filter_ref, *refs, middle):
    out_refs, chunks_ref = refs[:-1], refs[-1]
    low_count, width = filter_ref.shape[1:3]
    chunks = chunks_ref.shape[0]
    seq = place_ref[1]
    row = lax.broadcasted_iota(jnp.int32, (width, width), 0)
    col = lax.broadcasted_iota(jnp.int32, (width, width), 1)
    for low in range(low_count):
        mirrored = seq * low_count + low > middle
        order = jnp.where(col == jnp.where(mirrored, width - 1 - row, row), 1.0, 0.0).astype(BF16)
        sign = jnp.where(mirrored, -1.0, 1.0).astype(F32)
        for block in range(chunks // 2):
            lanes = pl.ds(block * LANES, LANES)
            both = jnp.concatenate(
                [filter_ref[0, low, :, lanes], filter_ref[1, low, :, lanes]], 1
            ).astype(BF16)
            both = jnp.dot(order, both, preferred_element_type=F32)
            halves = swap_halves(both[:, :LANES], sign * both[:, LANES:])
            rows = pl.ds(low * width, width)
            for half in range(2):
                near = (2 * block + half) ^ (seq % chunks)
                chunks_ref[near, rows, :] = halves[half].astype(BF16)
    views = [ref.at[at] for ref in out_refs for at in range(ref.shape[0])]
    for step in range(len(views) // chunks):

        @pl.when(pl.program_id(0) == step)
        def _():
            for near in range(chunks):
                views[chunks * step + near][...] = chunks_ref[near]


def pack_filter(filter_spectrum, devices_seq):
    _, low, width, channels = filter_spectrum.shape
    chunks = 4
    wide = chunks * HALF
    steps = devices_seq // chunks
    size = low * width * channels // 2
    block = (low * width, LANES)
    shapes = [
        (1 + (d in JOINED), *block) for d in range(devices_seq) if d - 1 not in JOINED
    ]

    def lanes_of(step, place):
        return (0, 0, 0, place[0] * steps + ((place[1] // chunks) ^ step))

    return pl.pallas_call(
        functools.partial(pack_filter_kernel, middle=low * devices_seq // 2),
        out_shape=[pltpu.HBM(shape, BF16) for shape in shapes],
        grid_spec=pltpu.PrefetchScalarGridSpec(
            num_scalar_prefetch=1,
            grid=(steps,),
            in_specs=[pl.BlockSpec((2, low, width, wide), lanes_of)],
            out_specs=[pl.BlockSpec(shape, lambda step, place: (0, 0, 0)) for shape in shapes],
            scratch_shapes=[pltpu.VMEM((chunks, *block), BF16)],
        ),
        compiler_params=pltpu.CompilerParams(vmem_limit_bytes=16 << 20),
        cost_estimate=pl.CostEstimate(
            flops=4 * width * size, bytes_accessed=12 * size, transcendentals=0
        ),
        name="pack_filter",
    )(
        jnp.stack([lax.axis_index("groups"), lax.axis_index("seq")]),
        pltpu.with_memory_space_constraint(filter_spectrum, pltpu.HBM),
    )


def swap_with(values, distance):
    count = lax.axis_size("seq")
    return lax.ppermute(values, "seq", [(i, i ^ distance) for i in range(count)])


def split_bf16(values):
    high = values.astype(BF16)
    return high, (values - high.astype(F32)).astype(BF16)


def forward_kernel(
    got_ref, first_ref, second_ref, turn_ref, out_ref, rows_ref, stage_ref, *, devices_seq
):
    width = turn_ref.shape[1]
    half_rows = out_ref.shape[0] - 1
    full_rows = 2 * half_rows
    pitch = width + PAD
    tall = full_rows + PAD
    lines = got_ref.shape[2] // width
    for source in range(devices_seq):
        for line in range(lines):
            at = pl.ds(line * width, width)
            halves = swap_halves(
                got_ref[source, 0, at, :].astype(F32), got_ref[source, 1, at, :].astype(F32)
            )
            for half in range(2):
                row = (2 * source + half) * lines + line
                rows_ref[pl.ds(row * pitch, width), :] = halves[half]
    first_matrix = first_ref[...]
    second_matrix = second_ref[...]

    def first_stage(step, carry):
        for u in range(0, 8, 2):
            pair = jnp.concatenate(
                [
                    rows_ref[pl.ds(8 * step + u + v, half_rows, stride=pitch), :].astype(BF16)
                    for v in range(2)
                ],
                1,
            )
            pair = jnp.concatenate([pair, pair], 0)
            done = jnp.dot(first_matrix, pair, preferred_element_type=F32)
            for v in range(2):
                at = pl.multiple_of((8 * step + u + v) * tall, PAD)
                stage_ref[pl.ds(at, full_rows), :] = done[:, v * LANES : (v + 1) * LANES]
        return carry

    lax.fori_loop(0, width // 8, first_stage, 0)

    def turned(real, imag, block, u):
        cosine = turn_ref[block, :, u : u + 1]
        sine = turn_ref[block, :, 8 + u : 9 + u]
        if imag is None:
            return jnp.concatenate([real * cosine, -real * sine], 0)
        return jnp.concatenate([real * cosine + imag * sine, imag * cosine - real * sine], 0)

    def transform(values):
        high, low = split_bf16(values)
        return jnp.dot(
            second_matrix, jnp.concatenate([high, high, low], 0), preferred_element_type=F32
        )

    def second_stage(block, carry):
        for u in range(0, 8, 2):
            pair = []
            for v in range(u, u + 2):
                at = 8 * block + v
                real = stage_ref[pl.ds(at, width, stride=tall), :]
                imag = stage_ref[pl.ds(half_rows + at, width, stride=tall), :]
                if v == 0:
                    imag = imag * jnp.where(block == 0, 0.0, 1.0).astype(F32)
                pair.append(turned(real, imag, block, v))
            done = transform(jnp.concatenate(pair, 1))
            for v in range(2):
                out_ref[8 * block + u + v] = done[:, v * LANES : (v + 1) * LANES]
        return carry

    lax.fori_loop(0, half_rows // 8, second_stage, 0)
    real = stage_ref[pl.ds(half_rows, width, stride=tall), :]
    out_ref[half_rows] = transform(turned(real, None, half_rows // 8, 0))


def forward(got, devices_seq, width):
    half_rows = got.size // (LANES * width)
    first, second, _, turn = tables(half_rows, width)
    return pl.pallas_call(
        functools.partial(forward_kernel, devices_seq=devices_seq),
        out_shape=pltpu.VMEM((half_rows + 1, 2 * width, LANES), F32),
        scratch_shapes=[
            pltpu.VMEM((half_rows * (width + PAD), LANES), F32),
            pltpu.VMEM((width * (2 * half_rows + PAD), LANES), F32),
        ],
        compiler_params=pltpu.CompilerParams(vmem_limit_bytes=16 << 20),
        cost_estimate=pl.CostEstimate(
            flops=2 * LANES * (first.size * width + second.size * half_rows),
            bytes_accessed=2 * got.size + 8 * half_rows * width * LANES,
            transcendentals=0,
        ),
        name="forward",
    )(got, first, second, turn)


def inverse_kernel(
    place_ref, spec_ref, matrices_hbm, *refs, devices_seq
):
    filter_hbm = refs[:devices_seq]
    turn_ref, out_ref, filter_ref, lead_ref, matrices_ref = refs[devices_seq : devices_seq + 5]
    real_ref, imag_ref, rows_ref, matrices_sem, filter_sems = refs[devices_seq + 5 :]
    width = turn_ref.shape[1]
    half_rows = spec_ref.shape[0] - 1
    pitch = width + PAD
    per_source = 8
    left = left_lanes(width)

    top_block = half_rows // per_source

    place = place_ref[0]
    upper = place >= top_block

    def block_of(distance):
        source = place ^ distance
        return jnp.where(upper, devices_seq - 1 - source, source)

    def arrival(distance):
        return pltpu.make_async_copy(
            filter_hbm[distance].at[int(distance - 1 in JOINED)],
            filter_ref.at[distance],
            filter_sems.at[distance],
        )

    matrices = pltpu.make_async_copy(matrices_hbm, matrices_ref, matrices_sem)
    matrices.start()
    for distance in range(top_block):
        arrival(distance).start()
        arrival(devices_seq - 1 - distance).start()
    matrices.wait()
    third_matrix = matrices_ref[: 2 * width]
    last_matrix = matrices_ref[2 * width :]

    def response_of(distance, at):
        far = devices_seq - 1 - distance
        row = pl.ds(at * width, width)
        mirror = pl.ds((per_source - at) * width, width)
        lower = jnp.where(upper, filter_ref[far, row], filter_ref[distance, row])
        higher = jnp.where(upper, filter_ref[distance, mirror], filter_ref[far, mirror])
        return lower.astype(F32) + higher.astype(F32)

    def filtered(spec, response):
        turned = pltpu.roll(response, HALF, 1)
        real_part = jnp.where(left, response, turned)
        imag_part = jnp.where(left, turned, response)
        real, imag = spec[:width], spec[width:]
        return jnp.concatenate(
            [real * real_part - imag * imag_part, real * imag_part + imag * real_part], 0
        ).astype(BF16)

    def transform(values):
        return jnp.dot(
            third_matrix, jnp.concatenate([values, values], 0), preferred_element_type=F32
        )

    def turned_back(values, block, u):
        cosine = turn_ref[block, :, u : u + 1]
        sine = turn_ref[block, :, 8 + u : 9 + u]
        real, imag = values[:width], values[width:]
        return real * cosine - imag * sine, real * sine + imag * cosine

    def third_stage(slots):
        values = jnp.concatenate(
            [filtered(spec_ref[low], response) for low, response, _, _ in slots], 1
        )
        done = transform(values)
        results = []
        for v, (_, _, block, u) in enumerate(slots):
            results.append(turned_back(done[:, v * LANES : (v + 1) * LANES], block, u))
        return results

    def keep(low, values):
        at = low * pitch if isinstance(low, int) else pl.multiple_of(low * pitch, PAD)
        real_ref[pl.ds(at, width), :] = values[0]
        imag_ref[pl.ds(at, width), :] = values[1]

    for distance in range(top_block):
        block = block_of(distance)
        far = devices_seq - 1 - distance
        arrival(distance).wait()
        arrival(far).wait()
        for near in (distance, far):
            lead_ref[place ^ near] = filter_ref[near, :width].astype(F32)
        slots = [
            (per_source * block + v, response_of(distance, v), block, v)
            for v in range(1, per_source)
        ]
        for at in range(0, len(slots), 2):
            pair = slots[at : at + 2]
            for slot, values in zip(pair, third_stage(pair)):
                keep(slot[0], values)
    slots = [(0, lead_ref[0], 0, 0), (half_rows, lead_ref[top_block], top_block, 0)]
    first, middle = third_stage(slots)
    keep(0, (first[0], middle[0]))
    slots = [
        (per_source * block, lead_ref[block] + lead_ref[devices_seq - block], block, 0)
        for block in range(1, top_block)
    ]
    for at in range(0, len(slots), 2):
        pair = slots[at : at + 2]
        for slot, values in zip(pair, third_stage(pair)):
            keep(slot[0], values)

    def last_stage(step, carry):
        for u in range(0, 8, 2):
            pair = []
            for v in range(u, u + 2):
                rows = pl.ds(8 * step + v, half_rows, stride=pitch)
                pair.append(jnp.concatenate([real_ref[rows, :], imag_ref[rows, :]], 0).astype(BF16))
            pair = jnp.concatenate(pair, 1)
            done = jnp.dot(
                last_matrix, jnp.concatenate([pair, pair], 0), preferred_element_type=F32
            )
            for v in range(2):
                rows = pl.ds(8 * step + u + v, half_rows, stride=pitch)
                rows_ref[rows, :] = done[:, v * LANES : (v + 1) * LANES]
        return carry

    lax.fori_loop(0, width // 8, last_stage, 0, unroll=True)
    lines = out_ref.shape[2] // width
    for source in range(devices_seq):
        for line in range(lines):
            first, second = swap_halves(
                *(
                    rows_ref[pl.ds(((2 * source + half) * lines + line) * pitch, width), :]
                    for half in range(2)
                )
            )
            at = pl.ds(line * width, width)
            out_ref[source, 0, at, :] = first.astype(BF16)
            out_ref[source, 1, at, :] = second.astype(BF16)


def inverse(spectrum, arrived, devices_seq, piece):
    width = spectrum.shape[1] // 2
    half_rows = spectrum.shape[0] - 1
    _, _, matrices, turn = tables(half_rows, width)
    return pl.pallas_call(
        functools.partial(inverse_kernel, devices_seq=devices_seq),
        out_shape=jax.ShapeDtypeStruct((devices_seq, 2, piece, LANES), BF16),
        in_specs=[pl.BlockSpec(memory_space=pltpu.SMEM), pl.BlockSpec(memory_space=pltpu.VMEM)]
        + [pl.BlockSpec(memory_space=pltpu.HBM)] * (1 + devices_seq)
        + [pl.BlockSpec(memory_space=pltpu.VMEM)],
        scratch_shapes=[
            pltpu.VMEM((devices_seq, *arrived[0].shape[1:]), BF16),
            pltpu.VMEM((devices_seq, width, LANES), F32),
            pltpu.VMEM(matrices.shape, BF16),
        ]
        + [pltpu.VMEM((half_rows * (width + PAD), LANES), F32)] * 3
        + [pltpu.SemaphoreType.DMA, pltpu.SemaphoreType.DMA((devices_seq,))],
        compiler_params=pltpu.CompilerParams(vmem_limit_bytes=20 << 20),
        cost_estimate=pl.CostEstimate(
            flops=2 * LANES * matrices.size * width,
            bytes_accessed=4 * spectrum.size + 2 * devices_seq * arrived[0].size,
            transcendentals=0,
        ),
        name="inverse",
    )(
        lax.axis_index("seq").reshape(1),
        pltpu.with_memory_space_constraint(spectrum, pltpu.VMEM),
        *(
            pltpu.with_memory_space_constraint(operand, pltpu.HBM)
            for operand in (jnp.asarray(matrices), *arrived)
        ),
        turn,
    )


def mix_kernel(conv_ref, signal_ref, gate_ref, out_gate_ref, gain_ref, out_hbm, out_ref, sems):
    rows = signal_ref.shape[0] // 2
    pieces = sems.shape[0]
    wide = signal_ref.shape[1] // pieces

    def leave(piece):
        lanes = pl.ds(piece * wide, wide)
        return pltpu.make_async_copy(out_ref.at[:, lanes], out_hbm.at[:, lanes], sems.at[piece])

    for piece in range(pieces):
        for start in range(piece * wide, (piece + 1) * wide, LANES):
            lanes = pl.ds(start, LANES)
            gain = gain_ref[:, lanes]
            group, seq = divmod(start // HALF, conv_ref.shape[0])
            halves = swap_halves(
                conv_ref[seq, group].astype(F32), conv_ref[seq + 1, group].astype(F32)
            )
            for half, convolved in enumerate(halves):
                at = pl.ds(half * rows, rows)
                gated = signal_ref[at, lanes].astype(F32) * gate_ref[at, lanes].astype(F32)
                gated = gated.astype(BF16).astype(F32)
                mixed = out_gate_ref[at, lanes].astype(F32) * (convolved + gain * gated)
                out_ref[at, lanes] = mixed.astype(BF16)
        leave(piece).start()
    for piece in range(pieces):
        leave(piece).wait()


def mix(conv, signal, input_gate, output_gate, skip_gain):
    return pl.pallas_call(
        mix_kernel,
        out_shape=jax.ShapeDtypeStruct(signal.shape, BF16),
        in_specs=[pl.BlockSpec(memory_space=pltpu.VMEM)] * 5,
        out_specs=pl.BlockSpec(memory_space=pltpu.HBM),
        scratch_shapes=[pltpu.VMEM(signal.shape, BF16), pltpu.SemaphoreType.DMA((PIECES,))],
        compiler_params=pltpu.CompilerParams(vmem_limit_bytes=16 << 20),
        cost_estimate=pl.CostEstimate(
            flops=4 * signal.size, bytes_accessed=10 * signal.size, transcendentals=0
        ),
        name="mix",
    )(conv, signal, input_gate, output_gate, skip_gain[None, :])


def spread_kernels(signal, input_gate, output_gate, filter_spectrum, skip_gain):
    devices_seq = lax.axis_size("seq")
    width = filter_spectrum.shape[2]

    def pairs(values):
        return exchange(values.reshape(-1, *values.shape[2:]), PAIRS).reshape(values.shape)

    got = pairs(pack_input(signal, input_gate, devices_seq))
    packed = pack_filter(filter_spectrum, devices_seq)
    packed = iter(packed)
    arrived = [next(packed)]
    for distance in range(1, devices_seq):
        if distance - 1 in JOINED:
            arrived.append(swap_with(arrived[-1], 1))
        else:
            arrived.append(swap_with(next(packed), distance))
    spectrum = forward(got, devices_seq, width)
    conv = inverse(spectrum, arrived, devices_seq, signal.shape[0] // 2)
    return mix(pairs(conv), signal, input_gate, output_gate, skip_gain)


def angle_table(rows_count, cols_count, length):
    row_index = lax.iota(jnp.int32, rows_count)
    col_index = lax.iota(jnp.int32, cols_count)
    product = row_index[:, None] * col_index[None, :] % length
    angles = product.astype(jnp.float32) * (2.0 * math.pi / length)
    return (jnp.cos(angles), jnp.sin(angles))


def contract_first(matrix, values):
    return jnp.einsum("kn,nbc->kbc", matrix, values, precision=lax.Precision.HIGH)


def contract_second(matrix, values):
    return jnp.einsum("kn,anc->akc", matrix, values, precision=lax.Precision.HIGH)


def convolve(signal_rows, spectra_real, spectra_imag):
    half_rows, width, _ = signal_rows.shape
    full_rows = 2 * half_rows
    length = full_rows * width
    cos_one, sin_one = angle_table(full_rows, half_rows, full_rows)
    cos_two, sin_two = angle_table(width, width, width)
    turn_cos, turn_sin = angle_table(full_rows, width, length)
    turn_cos = turn_cos[:, :, None]
    turn_sin = turn_sin[:, :, None]
    first_real = contract_first(cos_one, signal_rows)
    first_imag = -contract_first(sin_one, signal_rows)
    twist_real = first_real * turn_cos + first_imag * turn_sin
    twist_imag = first_imag * turn_cos - first_real * turn_sin
    spec_real = contract_second(cos_two, twist_real) + contract_second(sin_two, twist_imag)
    spec_imag = contract_second(cos_two, twist_imag) - contract_second(sin_two, twist_real)
    prod_real = spec_real * spectra_real - spec_imag * spectra_imag
    prod_imag = spec_real * spectra_imag + spec_imag * spectra_real
    back_real = contract_second(cos_two, prod_real) - contract_second(sin_two, prod_imag)
    back_imag = contract_second(sin_two, prod_real) + contract_second(cos_two, prod_imag)
    rotated_real = back_real * turn_cos - back_imag * turn_sin
    rotated_imag = back_real * turn_sin + back_imag * turn_cos
    summed = contract_first(cos_one.T, rotated_real) - contract_first(sin_one.T, rotated_imag)
    return summed * (1.0 / length)


def spread_plain(signal, input_gate, output_gate, filter_spectrum, skip_gain):
    tok_rows, channels = signal.shape
    groups = lax.axis_size("groups")
    devices_seq = lax.axis_size("seq")
    parts = groups * devices_seq
    width = channels // parts
    low, high = filter_spectrum.shape[1:3]
    share = low // groups
    gated_input = (input_gate.astype(jnp.float32) * signal.astype(jnp.float32)).astype(jnp.bfloat16)

    sent = gated_input.reshape(tok_rows, parts, width).transpose(1, 0, 2).reshape(parts, -1, 128)
    got = exchange(sent).reshape(groups, devices_seq, tok_rows, width)
    rows = got.transpose(1, 2, 0, 3).reshape(-1, high, groups * width)

    mine = lax.dynamic_slice_in_dim(filter_spectrum, lax.axis_index("groups") * share, share, axis=1)
    mine = mine.astype(jnp.bfloat16).reshape(2, share, high, parts, width)
    mine = mine.transpose(3, 0, 1, 2, 4).reshape(parts, -1, 128)
    spectra = exchange(mine).reshape(groups, devices_seq, 2, share, high, width)
    spectra = spectra.transpose(2, 1, 0, 3, 4, 5).reshape(2, -1, high, 1, width)
    spectra = jnp.broadcast_to(spectra, spectra.shape[:3] + (groups, width))
    spectra = spectra.reshape(2, -1, high, groups * width).astype(jnp.float32)

    conv = convolve(rows.astype(jnp.float32), spectra[0], spectra[1]).astype(jnp.bfloat16)
    conv = conv.reshape(devices_seq, tok_rows, groups, width).transpose(2, 0, 1, 3)
    back = exchange(conv.reshape(parts, -1, 128)).reshape(parts, tok_rows, width)
    convolved = back.transpose(1, 0, 2).reshape(tok_rows, channels).astype(jnp.float32)
    mixed_out = output_gate.astype(jnp.float32) * (
        convolved + skip_gain[None, :] * gated_input.astype(jnp.float32)
    )
    return mixed_out.astype(jnp.bfloat16)


def on_device(signal, input_gate, output_gate, filter_spectrum, skip_gain):
    groups = lax.axis_size("groups")
    devices_seq = lax.axis_size("seq")
    tok_rows, channels = signal.shape
    low, high = filter_spectrum.shape[1:3]
    fits = (
        groups == 2
        and channels == groups * devices_seq * HALF
        and low == 8
        and tok_rows == low * high // 2
        and tok_rows % 32 == 0
        and devices_seq >= 4
        and devices_seq & (devices_seq - 1) == 0
    )
    plan = spread_kernels if fits else spread_plain
    return plan(signal, input_gate, output_gate, filter_spectrum, skip_gain)


def solution(mesh):
    return jax.shard_map(
        on_device,
        mesh=mesh,
        in_specs=(P(EVERY, None), P(EVERY, None), P(EVERY, None), P(None, "seq", None, None), P()),
        out_specs=P(EVERY, None),
        check_vma=False,
    )
```

```python
import functools
import math

import jax
import jax.numpy as jnp
import ml_dtypes
import numpy as np
from jax import lax
from jax.experimental import pallas as pl
from jax.experimental.pallas import tpu as pltpu
from jax.sharding import PartitionSpec as P

EVERY = ("groups", "seq")
PAIRS = ("seq", "groups")
LANES = 128
HALF = LANES // 2
PAD = 8
PIECES = 4
JOINED = ()
EARLY = (7, 6, 5, 4)
BF16 = jnp.bfloat16
F32 = jnp.float32


def exchange(values, axes=EVERY):
    return lax.all_to_all(values, axes, split_axis=0, concat_axis=0, tiled=True)


def left_lanes(rows):
    return lax.broadcasted_iota(jnp.int32, (rows, LANES), 1) < HALF


def swap_halves(first, second):
    left = left_lanes(first.shape[0])
    return (
        jnp.where(left, first, pltpu.roll(second, HALF, 1)),
        jnp.where(left, pltpu.roll(first, HALF, 1), second),
    )


def hi_lo(matrix):
    high = matrix.astype(ml_dtypes.bfloat16)
    low = (matrix - high.astype(np.float64)).astype(ml_dtypes.bfloat16)
    return high, low


@functools.lru_cache(None)
def tables(half_rows, width):
    full_rows = 2 * half_rows
    length = full_rows * width
    low_index = np.arange(half_rows)
    angle = 2 * np.pi * (np.outer(low_index, low_index) % full_rows) / full_rows
    real_part, imag_part = np.cos(angle), -np.sin(angle)
    imag_part[0] = 1.0 - 2.0 * (low_index % 2)
    first = np.concatenate([real_part, imag_part], 0)
    last = first.T / length
    inner = np.arange(width)
    angle = 2 * np.pi * (np.outer(inner, inner) % width) / width
    cosine, sine = np.cos(angle), np.sin(angle)
    second = np.block([[cosine, sine], [-sine, cosine]])
    third = np.block([[cosine, -sine], [sine, cosine]])
    first_hi, first_lo = hi_lo(first)
    second_hi, second_lo = hi_lo(second)
    third_hi, third_lo = hi_lo(third)
    last_hi, last_lo = hi_lo(last)
    turn = np.zeros((half_rows // 8 + 1, width, LANES), np.float32)
    for block in range(half_rows // 8 + 1):
        angle = 2 * np.pi * np.outer(inner, 8 * block + np.arange(8)) / length
        turn[block, :, :8] = np.cos(angle)
        turn[block, :, 8:16] = np.sin(angle)
    return (
        np.concatenate([first_hi, first_lo], 1),
        np.concatenate([second_hi, second_lo, second_hi], 1),
        np.block([[third_hi, third_lo], [last_hi, last_lo]]),
        turn,
    )


def pack_input_kernel(signal_ref, gate_ref, out_ref):
    rows = signal_ref.shape[0] // 2
    for block in range(signal_ref.shape[1] // LANES):
        lanes = pl.ds(block * LANES, LANES)
        gated = signal_ref[:, lanes].astype(F32) * gate_ref[:, lanes].astype(F32)
        first, second = swap_halves(gated[:rows], gated[rows:])
        out_ref[2 * block, 0] = first.astype(BF16)
        out_ref[2 * block + 1, 0] = second.astype(BF16)


def pack_input(signal, input_gate, devices_seq):
    tok_rows, channels = signal.shape
    wide = channels // 2
    return pl.pallas_call(
        pack_input_kernel,
        out_shape=jax.ShapeDtypeStruct((devices_seq, 2, tok_rows // 2, LANES), BF16),
        grid=(2,),
        in_specs=[pl.BlockSpec((tok_rows, wide), lambda b: (0, b))] * 2,
        out_specs=pl.BlockSpec((devices_seq, 1, tok_rows // 2, LANES), lambda b: (0, b, 0, 0)),
        cost_estimate=pl.CostEstimate(
            flops=signal.size, bytes_accessed=6 * signal.size, transcendentals=0
        ),
        name="pack_input",
    )(signal, input_gate)


def pack_filter_kernel(place_ref, filter_ref, *refs, middle):
    out_refs, chunks_ref = refs[:-1], refs[-1]
    low_count, width = filter_ref.shape[1:3]
    chunks = chunks_ref.shape[0]
    seq = place_ref[1]
    row = lax.broadcasted_iota(jnp.int32, (width, width), 0)
    col = lax.broadcasted_iota(jnp.int32, (width, width), 1)
    for low in range(low_count):
        mirrored = seq * low_count + low > middle
        order = jnp.where(col == jnp.where(mirrored, width - 1 - row, row), 1.0, 0.0).astype(BF16)
        sign = jnp.where(mirrored, -1.0, 1.0).astype(F32)
        for block in range(chunks // 2):
            lanes = pl.ds(block * LANES, LANES)
            both = jnp.concatenate(
                [filter_ref[0, low, :, lanes], filter_ref[1, low, :, lanes]], 1
            ).astype(BF16)
            both = jnp.dot(order, both, preferred_element_type=F32)
            halves = swap_halves(both[:, :LANES], sign * both[:, LANES:])
            rows = pl.ds(low * width, width)
            for half in range(2):
                near = (2 * block + half) ^ (seq % chunks)
                chunks_ref[near, rows, :] = halves[half].astype(BF16)
    views = [ref.at[at] for ref in out_refs for at in range(ref.shape[0])]
    for step in range(len(views) // chunks):

        @pl.when(pl.program_id(0) == step)
        def _():
            for near in range(chunks):
                views[chunks * step + near][...] = chunks_ref[near]


def pack_filter(filter_spectrum, devices_seq):
    _, low, width, channels = filter_spectrum.shape
    chunks = 4
    wide = chunks * HALF
    steps = devices_seq // chunks
    size = low * width * channels // 2
    block = (low * width, LANES)
    shapes = [
        (1 + (d in JOINED), *block) for d in range(devices_seq) if d - 1 not in JOINED
    ]

    def lanes_of(step, place):
        return (0, 0, 0, place[0] * steps + ((place[1] // chunks) ^ step))

    return pl.pallas_call(
        functools.partial(pack_filter_kernel, middle=low * devices_seq // 2),
        out_shape=[pltpu.HBM(shape, BF16) for shape in shapes],
        grid_spec=pltpu.PrefetchScalarGridSpec(
            num_scalar_prefetch=1,
            grid=(steps,),
            in_specs=[pl.BlockSpec((2, low, width, wide), lanes_of)],
            out_specs=[pl.BlockSpec(shape, lambda step, place: (0, 0, 0)) for shape in shapes],
            scratch_shapes=[pltpu.VMEM((chunks, *block), BF16)],
        ),
        compiler_params=pltpu.CompilerParams(vmem_limit_bytes=16 << 20),
        cost_estimate=pl.CostEstimate(
            flops=4 * width * size, bytes_accessed=12 * size, transcendentals=0
        ),
        name="pack_filter",
    )(
        jnp.stack([lax.axis_index("groups"), lax.axis_index("seq")]),
        pltpu.with_memory_space_constraint(filter_spectrum, pltpu.HBM),
    )


def swap_with(values, distance):
    count = lax.axis_size("seq")
    return lax.ppermute(values, "seq", [(i, i ^ distance) for i in range(count)])


def split_bf16(values):
    high = values.astype(BF16)
    return high, (values - high.astype(F32)).astype(BF16)


def forward_kernel(
    got_ref, first_ref, second_ref, turn_ref, out_ref, rows_ref, stage_ref, *, devices_seq
):
    width = turn_ref.shape[1]
    half_rows = out_ref.shape[0] - 1
    full_rows = 2 * half_rows
    pitch = width + PAD
    tall = full_rows + PAD
    lines = got_ref.shape[2] // width
    for source in range(devices_seq):
        for line in range(lines):
            at = pl.ds(line * width, width)
            halves = swap_halves(
                got_ref[source, 0, at, :].astype(F32), got_ref[source, 1, at, :].astype(F32)
            )
            for half in range(2):
                row = (2 * source + half) * lines + line
                rows_ref[pl.ds(row * pitch, width), :] = halves[half]
    first_matrix = first_ref[...]
    second_matrix = second_ref[...]

    def first_stage(step, carry):
        for u in range(0, 8, 2):
            pair = jnp.concatenate(
                [
                    rows_ref[pl.ds(8 * step + u + v, half_rows, stride=pitch), :].astype(BF16)
                    for v in range(2)
                ],
                1,
            )
            pair = jnp.concatenate([pair, pair], 0)
            done = jnp.dot(first_matrix, pair, preferred_element_type=F32)
            for v in range(2):
                at = pl.multiple_of((8 * step + u + v) * tall, PAD)
                stage_ref[pl.ds(at, full_rows), :] = done[:, v * LANES : (v + 1) * LANES]
        return carry

    lax.fori_loop(0, width // 8, first_stage, 0)

    def turned(real, imag, block, u):
        cosine = turn_ref[block, :, u : u + 1]
        sine = turn_ref[block, :, 8 + u : 9 + u]
        if imag is None:
            return jnp.concatenate([real * cosine, -real * sine], 0)
        return jnp.concatenate([real * cosine + imag * sine, imag * cosine - real * sine], 0)

    def transform(values):
        high, low = split_bf16(values)
        return jnp.dot(
            second_matrix, jnp.concatenate([high, high, low], 0), preferred_element_type=F32
        )

    def second_stage(block, carry):
        for u in range(0, 8, 2):
            pair = []
            for v in range(u, u + 2):
                at = 8 * block + v
                real = stage_ref[pl.ds(at, width, stride=tall), :]
                imag = stage_ref[pl.ds(half_rows + at, width, stride=tall), :]
                if v == 0:
                    imag = imag * jnp.where(block == 0, 0.0, 1.0).astype(F32)
                pair.append(turned(real, imag, block, v))
            done = transform(jnp.concatenate(pair, 1))
            for v in range(2):
                out_ref[8 * block + u + v] = done[:, v * LANES : (v + 1) * LANES]
        return carry

    lax.fori_loop(0, half_rows // 8, second_stage, 0)
    real = stage_ref[pl.ds(half_rows, width, stride=tall), :]
    out_ref[half_rows] = transform(turned(real, None, half_rows // 8, 0))


def forward(got, devices_seq, width):
    half_rows = got.size // (LANES * width)
    first, second, _, turn = tables(half_rows, width)
    return pl.pallas_call(
        functools.partial(forward_kernel, devices_seq=devices_seq),
        out_shape=pltpu.VMEM((half_rows + 1, 2 * width, LANES), F32),
        scratch_shapes=[
            pltpu.VMEM((half_rows * (width + PAD), LANES), F32),
            pltpu.VMEM((width * (2 * half_rows + PAD), LANES), F32),
        ],
        compiler_params=pltpu.CompilerParams(vmem_limit_bytes=16 << 20),
        cost_estimate=pl.CostEstimate(
            flops=2 * LANES * (first.size * width + second.size * half_rows),
            bytes_accessed=2 * got.size + 8 * half_rows * width * LANES,
            transcendentals=0,
        ),
        name="forward",
    )(got, first, second, turn)


def inverse_kernel(place_ref, spec_ref, turn_ref, matrices_hbm, *refs, devices_seq, early):
    distances = EARLY if early else [d for d in range(devices_seq // 2) if d not in EARLY]
    filter_hbm, refs = refs[:devices_seq], refs[devices_seq:]
    if early:
        real_ref, imag_ref, filter_ref, matrices_ref, matrices_sem, filter_sems = refs
    else:
        (_, _, out_ref, real_ref, imag_ref) = refs[:5]
        filter_ref, matrices_ref, matrices_sem, filter_sems, lead_ref, rows_ref = refs[5:]
    width = turn_ref.shape[1]
    half_rows = spec_ref.shape[0] - 1
    pitch = width + PAD
    per_source = 8
    left = left_lanes(width)
    top_block = half_rows // per_source

    place = place_ref[0]
    upper = place >= top_block

    def block_of(distance):
        source = place ^ distance
        return jnp.where(upper, devices_seq - 1 - source, source)

    def arrival(distance, count=None):
        rows = pl.ds(0, count or filter_ref.shape[1])
        return pltpu.make_async_copy(
            filter_hbm[distance].at[int(distance - 1 in JOINED), rows],
            filter_ref.at[distance, rows],
            filter_sems.at[distance],
        )

    def pair_of(distance):
        return distance, devices_seq - 1 - distance

    matrices = pltpu.make_async_copy(matrices_hbm, matrices_ref, matrices_sem)
    matrices.start()
    for distance in distances:
        for near in pair_of(distance):
            arrival(near).start()
    if not early:
        for distance in EARLY:
            for near in pair_of(distance):
                arrival(near, width).start()
    matrices.wait()
    third_matrix = matrices_ref[: 2 * width]
    last_matrix = matrices_ref[2 * width :]

    def response_of(distance, at):
        far = devices_seq - 1 - distance
        row = pl.ds(at * width, width)
        mirror = pl.ds((per_source - at) * width, width)
        lower = jnp.where(upper, filter_ref[far, row], filter_ref[distance, row])
        higher = jnp.where(upper, filter_ref[distance, mirror], filter_ref[far, mirror])
        return lower.astype(F32) + higher.astype(F32)

    def filtered(spec, response):
        turned = pltpu.roll(response, HALF, 1)
        real_part = jnp.where(left, response, turned)
        imag_part = jnp.where(left, turned, response)
        real, imag = spec[:width], spec[width:]
        return jnp.concatenate(
            [real * real_part - imag * imag_part, real * imag_part + imag * real_part], 0
        ).astype(BF16)

    def transform(values):
        return jnp.dot(
            third_matrix, jnp.concatenate([values, values], 0), preferred_element_type=F32
        )

    def turned_back(values, block, u):
        cosine = turn_ref[block, :, u : u + 1]
        sine = turn_ref[block, :, 8 + u : 9 + u]
        real, imag = values[:width], values[width:]
        return real * cosine - imag * sine, real * sine + imag * cosine

    def third_stage(slots):
        values = jnp.concatenate(
            [filtered(spec_ref[low], response) for low, response, _, _ in slots], 1
        )
        done = transform(values)
        results = []
        for v, (_, _, block, u) in enumerate(slots):
            results.append(turned_back(done[:, v * LANES : (v + 1) * LANES], block, u))
        return results

    def keep(low, values):
        at = low * pitch if isinstance(low, int) else pl.multiple_of(low * pitch, PAD)
        real_ref[pl.ds(at, width), :] = values[0]
        imag_ref[pl.ds(at, width), :] = values[1]

    for distance in distances:
        block = block_of(distance)
        for near in pair_of(distance):
            arrival(near).wait()
        slots = [
            (per_source * block + v, response_of(distance, v), block, v)
            for v in range(1, per_source)
        ]
        for at in range(0, len(slots), 2):
            pair = slots[at : at + 2]
            for slot, values in zip(pair, third_stage(pair)):
                keep(slot[0], values)
    if early:
        return
    for distance in EARLY:
        for near in pair_of(distance):
            arrival(near, width).wait()
    for distance in range(devices_seq):
        lead_ref[place ^ distance] = filter_ref[distance, :width].astype(F32)
    slots = [(0, lead_ref[0], 0, 0), (half_rows, lead_ref[top_block], top_block, 0)]
    first, middle = third_stage(slots)
    keep(0, (first[0], middle[0]))
    slots = [
        (per_source * block, lead_ref[block] + lead_ref[devices_seq - block], block, 0)
        for block in range(1, top_block)
    ]
    for at in range(0, len(slots), 2):
        pair = slots[at : at + 2]
        for slot, values in zip(pair, third_stage(pair)):
            keep(slot[0], values)

    def last_stage(step, carry):
        for u in range(0, 8, 2):
            pair = []
            for v in range(u, u + 2):
                rows = pl.ds(8 * step + v, half_rows, stride=pitch)
                pair.append(jnp.concatenate([real_ref[rows, :], imag_ref[rows, :]], 0).astype(BF16))
            pair = jnp.concatenate(pair, 1)
            done = jnp.dot(
                last_matrix, jnp.concatenate([pair, pair], 0), preferred_element_type=F32
            )
            for v in range(2):
                rows = pl.ds(8 * step + u + v, half_rows, stride=pitch)
                rows_ref[rows, :] = done[:, v * LANES : (v + 1) * LANES]
        return carry

    lax.fori_loop(0, width // 8, last_stage, 0, unroll=True)
    lines = out_ref.shape[2] // width
    for source in range(devices_seq):
        for line in range(lines):
            first, second = swap_halves(
                *(
                    rows_ref[pl.ds(((2 * source + half) * lines + line) * pitch, width), :]
                    for half in range(2)
                )
            )
            at = pl.ds(line * width, width)
            out_ref[source, 0, at, :] = first.astype(BF16)
            out_ref[source, 1, at, :] = second.astype(BF16)


def inverse(spectrum, arrived, devices_seq, piece):
    width = spectrum.shape[1] // 2
    half_rows = spectrum.shape[0] - 1
    _, _, matrices, turn = tables(half_rows, width)
    stage = pltpu.VMEM((half_rows * (width + PAD), LANES), F32)
    block = arrived[0].shape[1:]

    def in_hbm(operand):
        return pltpu.with_memory_space_constraint(jnp.asarray(operand), pltpu.HBM)

    def in_vmem(operand):
        return pltpu.with_memory_space_constraint(operand, pltpu.VMEM)

    vmem = pl.BlockSpec(memory_space=pltpu.VMEM)
    specs = [pl.BlockSpec(memory_space=pltpu.SMEM), vmem, vmem] + [
        pl.BlockSpec(memory_space=pltpu.HBM)
    ] * (1 + devices_seq)
    scratch = [
        pltpu.VMEM((devices_seq, *block), BF16),
        pltpu.VMEM(matrices.shape, BF16),
        pltpu.SemaphoreType.DMA,
        pltpu.SemaphoreType.DMA((devices_seq,)),
    ]

    def call(early, more_in, out_shape, more_scratch, aliases):
        used = [d for e in EARLY for d in (e, devices_seq - 1 - e)]
        rows = [
            in_hbm(arrived[d] if d in used or not early else arrived[used[0]])
            for d in range(devices_seq)
        ]
        operands = [lax.axis_index("seq").reshape(1), in_vmem(spectrum), turn, in_hbm(matrices)]
        operands += rows + more_in
        return pl.pallas_call(
            functools.partial(inverse_kernel, devices_seq=devices_seq, early=early),
            out_shape=out_shape,
            in_specs=specs + [vmem] * len(more_in),
            out_specs=[vmem] * len(out_shape),
            scratch_shapes=scratch + more_scratch,
            input_output_aliases={
                len(specs) + at: to for at, to in enumerate(aliases)
            },
            compiler_params=pltpu.CompilerParams(vmem_limit_bytes=20 << 20),
            cost_estimate=pl.CostEstimate(
                flops=LANES * matrices.size * width,
                bytes_accessed=2 * devices_seq * block[0] * block[1],
                transcendentals=0,
            ),
            name="inverse_early" if early else "inverse_late",
        )(*operands)

    real, imag = call(True, [], [stage, stage], [], [])
    return call(
        False,
        [in_vmem(real), in_vmem(imag)],
        [jax.ShapeDtypeStruct((devices_seq, 2, piece, LANES), BF16), stage, stage],
        [pltpu.VMEM((devices_seq, width, LANES), F32), stage],
        [1, 2],
    )[0]


def mix_kernel(conv_ref, signal_ref, gate_ref, out_gate_ref, gain_ref, out_hbm, out_ref, sems):
    rows = signal_ref.shape[0] // 2
    pieces = sems.shape[0]
    wide = signal_ref.shape[1] // pieces

    def leave(piece):
        lanes = pl.ds(piece * wide, wide)
        return pltpu.make_async_copy(out_ref.at[:, lanes], out_hbm.at[:, lanes], sems.at[piece])

    for piece in range(pieces):
        for start in range(piece * wide, (piece + 1) * wide, LANES):
            lanes = pl.ds(start, LANES)
            gain = gain_ref[:, lanes]
            group, seq = divmod(start // HALF, conv_ref.shape[0])
            halves = swap_halves(
                conv_ref[seq, group].astype(F32), conv_ref[seq + 1, group].astype(F32)
            )
            for half, convolved in enumerate(halves):
                at = pl.ds(half * rows, rows)
                gated = signal_ref[at, lanes].astype(F32) * gate_ref[at, lanes].astype(F32)
                gated = gated.astype(BF16).astype(F32)
                mixed = out_gate_ref[at, lanes].astype(F32) * (convolved + gain * gated)
                out_ref[at, lanes] = mixed.astype(BF16)
        leave(piece).start()
    for piece in range(pieces):
        leave(piece).wait()


def mix(conv, signal, input_gate, output_gate, skip_gain):
    return pl.pallas_call(
        mix_kernel,
        out_shape=jax.ShapeDtypeStruct(signal.shape, BF16),
        in_specs=[pl.BlockSpec(memory_space=pltpu.VMEM)] * 5,
        out_specs=pl.BlockSpec(memory_space=pltpu.HBM),
        scratch_shapes=[pltpu.VMEM(signal.shape, BF16), pltpu.SemaphoreType.DMA((PIECES,))],
        compiler_params=pltpu.CompilerParams(vmem_limit_bytes=16 << 20),
        cost_estimate=pl.CostEstimate(
            flops=4 * signal.size, bytes_accessed=10 * signal.size, transcendentals=0
        ),
        name="mix",
    )(conv, signal, input_gate, output_gate, skip_gain[None, :])


def spread_kernels(signal, input_gate, output_gate, filter_spectrum, skip_gain):
    devices_seq = lax.axis_size("seq")
    width = filter_spectrum.shape[2]

    def pairs(values):
        return exchange(values.reshape(-1, *values.shape[2:]), PAIRS).reshape(values.shape)

    got = pairs(pack_input(signal, input_gate, devices_seq))
    packed = pack_filter(filter_spectrum, devices_seq)
    packed = iter(packed)
    arrived = [next(packed)]
    for distance in range(1, devices_seq):
        if distance - 1 in JOINED:
            arrived.append(swap_with(arrived[-1], 1))
        else:
            arrived.append(swap_with(next(packed), distance))
    spectrum = forward(got, devices_seq, width)
    conv = inverse(spectrum, arrived, devices_seq, signal.shape[0] // 2)
    return mix(pairs(conv), signal, input_gate, output_gate, skip_gain)


def angle_table(rows_count, cols_count, length):
    row_index = lax.iota(jnp.int32, rows_count)
    col_index = lax.iota(jnp.int32, cols_count)
    product = row_index[:, None] * col_index[None, :] % length
    angles = product.astype(jnp.float32) * (2.0 * math.pi / length)
    return (jnp.cos(angles), jnp.sin(angles))


def contract_first(matrix, values):
    return jnp.einsum("kn,nbc->kbc", matrix, values, precision=lax.Precision.HIGH)


def contract_second(matrix, values):
    return jnp.einsum("kn,anc->akc", matrix, values, precision=lax.Precision.HIGH)


def convolve(signal_rows, spectra_real, spectra_imag):
    half_rows, width, _ = signal_rows.shape
    full_rows = 2 * half_rows
    length = full_rows * width
    cos_one, sin_one = angle_table(full_rows, half_rows, full_rows)
    cos_two, sin_two = angle_table(width, width, width)
    turn_cos, turn_sin = angle_table(full_rows, width, length)
    turn_cos = turn_cos[:, :, None]
    turn_sin = turn_sin[:, :, None]
    first_real = contract_first(cos_one, signal_rows)
    first_imag = -contract_first(sin_one, signal_rows)
    twist_real = first_real * turn_cos + first_imag * turn_sin
    twist_imag = first_imag * turn_cos - first_real * turn_sin
    spec_real = contract_second(cos_two, twist_real) + contract_second(sin_two, twist_imag)
    spec_imag = contract_second(cos_two, twist_imag) - contract_second(sin_two, twist_real)
    prod_real = spec_real * spectra_real - spec_imag * spectra_imag
    prod_imag = spec_real * spectra_imag + spec_imag * spectra_real
    back_real = contract_second(cos_two, prod_real) - contract_second(sin_two, prod_imag)
    back_imag = contract_second(sin_two, prod_real) + contract_second(cos_two, prod_imag)
    rotated_real = back_real * turn_cos - back_imag * turn_sin
    rotated_imag = back_real * turn_sin + back_imag * turn_cos
    summed = contract_first(cos_one.T, rotated_real) - contract_first(sin_one.T, rotated_imag)
    return summed * (1.0 / length)


def spread_plain(signal, input_gate, output_gate, filter_spectrum, skip_gain):
    tok_rows, channels = signal.shape
    groups = lax.axis_size("groups")
    devices_seq = lax.axis_size("seq")
    parts = groups * devices_seq
    width = channels // parts
    low, high = filter_spectrum.shape[1:3]
    share = low // groups
    gated_input = (input_gate.astype(jnp.float32) * signal.astype(jnp.float32)).astype(jnp.bfloat16)

    sent = gated_input.reshape(tok_rows, parts, width).transpose(1, 0, 2).reshape(parts, -1, 128)
    got = exchange(sent).reshape(groups, devices_seq, tok_rows, width)
    rows = got.transpose(1, 2, 0, 3).reshape(-1, high, groups * width)

    mine = lax.dynamic_slice_in_dim(filter_spectrum, lax.axis_index("groups") * share, share, axis=1)
    mine = mine.astype(jnp.bfloat16).reshape(2, share, high, parts, width)
    mine = mine.transpose(3, 0, 1, 2, 4).reshape(parts, -1, 128)
    spectra = exchange(mine).reshape(groups, devices_seq, 2, share, high, width)
    spectra = spectra.transpose(2, 1, 0, 3, 4, 5).reshape(2, -1, high, 1, width)
    spectra = jnp.broadcast_to(spectra, spectra.shape[:3] + (groups, width))
    spectra = spectra.reshape(2, -1, high, groups * width).astype(jnp.float32)

    conv = convolve(rows.astype(jnp.float32), spectra[0], spectra[1]).astype(jnp.bfloat16)
    conv = conv.reshape(devices_seq, tok_rows, groups, width).transpose(2, 0, 1, 3)
    back = exchange(conv.reshape(parts, -1, 128)).reshape(parts, tok_rows, width)
    convolved = back.transpose(1, 0, 2).reshape(tok_rows, channels).astype(jnp.float32)
    mixed_out = output_gate.astype(jnp.float32) * (
        convolved + skip_gain[None, :] * gated_input.astype(jnp.float32)
    )
    return mixed_out.astype(jnp.bfloat16)


def on_device(signal, input_gate, output_gate, filter_spectrum, skip_gain):
    groups = lax.axis_size("groups")
    devices_seq = lax.axis_size("seq")
    tok_rows, channels = signal.shape
    low, high = filter_spectrum.shape[1:3]
    fits = (
        groups == 2
        and channels == groups * devices_seq * HALF
        and low == 8
        and tok_rows == low * high // 2
        and tok_rows % 32 == 0
        and devices_seq >= 4
        and devices_seq & (devices_seq - 1) == 0
    )
    plan = spread_kernels if fits else spread_plain
    return plan(signal, input_gate, output_gate, filter_spectrum, skip_gain)


def solution(mesh):
    return jax.shard_map(
        on_device,
        mesh=mesh,
        in_specs=(P(EVERY, None), P(EVERY, None), P(EVERY, None), P(None, "seq", None, None), P()),
        out_specs=P(EVERY, None),
        check_vma=False,
    )
```

```python
import functools
import math

import jax
import jax.numpy as jnp
import ml_dtypes
import numpy as np
from jax import lax
from jax.experimental import pallas as pl
from jax.experimental.pallas import tpu as pltpu
from jax.sharding import PartitionSpec as P

EVERY = ("groups", "seq")
PAIRS = ("seq", "groups")
LANES = 128
HALF = LANES // 2
PAD = 8
PIECES = 4
BF16 = jnp.bfloat16
F32 = jnp.float32


def exchange(values, axes=EVERY):
    return lax.all_to_all(values, axes, split_axis=0, concat_axis=0, tiled=True)


def left_lanes(rows):
    return lax.broadcasted_iota(jnp.int32, (rows, LANES), 1) < HALF


def swap_halves(first, second):
    left = left_lanes(first.shape[0])
    return (
        jnp.where(left, first, pltpu.roll(second, HALF, 1)),
        jnp.where(left, pltpu.roll(first, HALF, 1), second),
    )


def hi_lo(matrix):
    high = matrix.astype(ml_dtypes.bfloat16)
    low = (matrix - high.astype(np.float64)).astype(ml_dtypes.bfloat16)
    return high, low


@functools.lru_cache(None)
def tables(half_rows, width):
    full_rows = 2 * half_rows
    length = full_rows * width
    low_index = np.arange(half_rows)
    angle = 2 * np.pi * (np.outer(low_index, low_index) % full_rows) / full_rows
    real_part, imag_part = np.cos(angle), -np.sin(angle)
    imag_part[0] = 1.0 - 2.0 * (low_index % 2)
    first = np.concatenate([real_part, imag_part], 0)
    last = first.T / length
    inner = np.arange(width)
    angle = 2 * np.pi * (np.outer(inner, inner) % width) / width
    cosine, sine = np.cos(angle), np.sin(angle)
    second = np.block([[cosine, sine], [-sine, cosine]])
    third = np.block([[cosine, -sine], [sine, cosine]])
    first_hi, first_lo = hi_lo(first)
    second_hi, second_lo = hi_lo(second)
    third_hi, third_lo = hi_lo(third)
    last_hi, last_lo = hi_lo(last)
    turn = np.zeros((half_rows // 8 + 1, width, LANES), np.float32)
    for block in range(half_rows // 8 + 1):
        angle = 2 * np.pi * np.outer(inner, 8 * block + np.arange(8)) / length
        turn[block, :, :8] = np.cos(angle)
        turn[block, :, 8:16] = np.sin(angle)
    return (
        np.concatenate([first_hi, first_lo], 1),
        np.concatenate([second_hi, second_lo, second_hi], 1),
        np.block([[third_hi, third_lo], [last_hi, last_lo]]),
        turn,
    )


def pack_input_kernel(signal_ref, gate_ref, out_ref):
    rows = signal_ref.shape[0] // 2
    for block in range(signal_ref.shape[1] // LANES):
        lanes = pl.ds(block * LANES, LANES)
        gated = signal_ref[:, lanes].astype(F32) * gate_ref[:, lanes].astype(F32)
        first, second = swap_halves(gated[:rows], gated[rows:])
        out_ref[2 * block, 0] = first.astype(BF16)
        out_ref[2 * block + 1, 0] = second.astype(BF16)


def pack_input(signal, input_gate, devices_seq):
    tok_rows, channels = signal.shape
    wide = channels // 2
    return pl.pallas_call(
        pack_input_kernel,
        out_shape=jax.ShapeDtypeStruct((devices_seq, 2, tok_rows // 2, LANES), BF16),
        grid=(2,),
        in_specs=[pl.BlockSpec((tok_rows, wide), lambda b: (0, b))] * 2,
        out_specs=pl.BlockSpec((devices_seq, 1, tok_rows // 2, LANES), lambda b: (0, b, 0, 0)),
        cost_estimate=pl.CostEstimate(
            flops=signal.size, bytes_accessed=6 * signal.size, transcendentals=0
        ),
        name="pack_input",
    )(signal, input_gate)


def pack_filter_kernel(place_ref, filter_ref, *refs, middle):
    out_refs, chunks_ref = refs[:-1], refs[-1]
    low_count, width = filter_ref.shape[1:3]
    chunks = chunks_ref.shape[0]
    seq = place_ref[1]
    row = lax.broadcasted_iota(jnp.int32, (width, width), 0)
    col = lax.broadcasted_iota(jnp.int32, (width, width), 1)
    for low in range(low_count):
        mirrored = seq * low_count + low > middle
        order = jnp.where(col == jnp.where(mirrored, width - 1 - row, row), 1.0, 0.0).astype(BF16)
        sign = jnp.where(mirrored, -1.0, 1.0).astype(F32)
        for block in range(chunks // 2):
            lanes = pl.ds(block * LANES, LANES)
            both = jnp.concatenate(
                [filter_ref[0, low, :, lanes], filter_ref[1, low, :, lanes]], 1
            ).astype(BF16)
            both = jnp.dot(order, both, preferred_element_type=F32)
            halves = swap_halves(both[:, :LANES], sign * both[:, LANES:])
            rows = pl.ds(low * width, width)
            for half in range(2):
                near = (2 * block + half) ^ (seq % chunks)
                chunks_ref[near, rows, :] = halves[half].astype(BF16)
    for step in range(len(out_refs) // chunks):

        @pl.when(pl.program_id(0) == step)
        def _():
            for near in range(chunks):
                out_refs[chunks * step + near][...] = chunks_ref[near]


def pack_filter(filter_spectrum, devices_seq):
    _, low, width, channels = filter_spectrum.shape
    chunks = 4
    wide = chunks * HALF
    steps = devices_seq // chunks
    size = low * width * channels // 2
    block = (low * width, LANES)

    def lanes_of(step, place):
        return (0, 0, 0, place[0] * steps + ((place[1] // chunks) ^ step))

    return pl.pallas_call(
        functools.partial(pack_filter_kernel, middle=low * devices_seq // 2),
        out_shape=[pltpu.HBM(block, BF16)] * devices_seq,
        grid_spec=pltpu.PrefetchScalarGridSpec(
            num_scalar_prefetch=1,
            grid=(steps,),
            in_specs=[pl.BlockSpec((2, low, width, wide), lanes_of)],
            out_specs=[pl.BlockSpec(block, lambda step, place: (0, 0))] * devices_seq,
            scratch_shapes=[pltpu.VMEM((chunks, *block), BF16)],
        ),
        compiler_params=pltpu.CompilerParams(vmem_limit_bytes=16 << 20),
        cost_estimate=pl.CostEstimate(
            flops=4 * width * size, bytes_accessed=12 * size, transcendentals=0
        ),
        name="pack_filter",
    )(
        jnp.stack([lax.axis_index("groups"), lax.axis_index("seq")]),
        pltpu.with_memory_space_constraint(filter_spectrum, pltpu.HBM),
    )


def early_distances(devices_seq):
    return list(reversed(range(devices_seq // 4, devices_seq // 2)))


def swap_with(values, distance):
    count = lax.axis_size("seq")
    return lax.ppermute(values, "seq", [(i, i ^ distance) for i in range(count)])


def split_bf16(values):
    high = values.astype(BF16)
    return high, (values - high.astype(F32)).astype(BF16)


def forward_kernel(
    got_ref, first_ref, second_ref, turn_ref, out_ref, rows_ref, stage_ref, *, devices_seq
):
    width = turn_ref.shape[1]
    half_rows = out_ref.shape[0] - 1
    full_rows = 2 * half_rows
    pitch = width + PAD
    tall = full_rows + PAD
    lines = got_ref.shape[2] // width
    for source in range(devices_seq):
        for line in range(lines):
            at = pl.ds(line * width, width)
            halves = swap_halves(
                got_ref[source, 0, at, :].astype(F32), got_ref[source, 1, at, :].astype(F32)
            )
            for half in range(2):
                row = (2 * source + half) * lines + line
                rows_ref[pl.ds(row * pitch, width), :] = halves[half]
    first_matrix = first_ref[...]
    second_matrix = second_ref[...]

    def first_stage(step, carry):
        for u in range(0, 8, 2):
            pair = jnp.concatenate(
                [
                    rows_ref[pl.ds(8 * step + u + v, half_rows, stride=pitch), :].astype(BF16)
                    for v in range(2)
                ],
                1,
            )
            pair = jnp.concatenate([pair, pair], 0)
            done = jnp.dot(first_matrix, pair, preferred_element_type=F32)
            for v in range(2):
                at = pl.multiple_of((8 * step + u + v) * tall, PAD)
                stage_ref[pl.ds(at, full_rows), :] = done[:, v * LANES : (v + 1) * LANES]
        return carry

    lax.fori_loop(0, width // 8, first_stage, 0)

    def turned(real, imag, block, u):
        cosine = turn_ref[block, :, u : u + 1]
        sine = turn_ref[block, :, 8 + u : 9 + u]
        if imag is None:
            return jnp.concatenate([real * cosine, -real * sine], 0)
        return jnp.concatenate([real * cosine + imag * sine, imag * cosine - real * sine], 0)

    def transform(values):
        high, low = split_bf16(values)
        return jnp.dot(
            second_matrix, jnp.concatenate([high, high, low], 0), preferred_element_type=F32
        )

    def second_stage(block, carry):
        for u in range(0, 8, 2):
            pair = []
            for v in range(u, u + 2):
                at = 8 * block + v
                real = stage_ref[pl.ds(at, width, stride=tall), :]
                imag = stage_ref[pl.ds(half_rows + at, width, stride=tall), :]
                if v == 0:
                    imag = imag * jnp.where(block == 0, 0.0, 1.0).astype(F32)
                pair.append(turned(real, imag, block, v))
            done = transform(jnp.concatenate(pair, 1))
            for v in range(2):
                out_ref[8 * block + u + v] = done[:, v * LANES : (v + 1) * LANES]
        return carry

    lax.fori_loop(0, half_rows // 8, second_stage, 0)
    real = stage_ref[pl.ds(half_rows, width, stride=tall), :]
    out_ref[half_rows] = transform(turned(real, None, half_rows // 8, 0))


def forward(got, devices_seq, width):
    half_rows = got.size // (LANES * width)
    first, second, _, turn = tables(half_rows, width)
    return pl.pallas_call(
        functools.partial(forward_kernel, devices_seq=devices_seq),
        out_shape=pltpu.VMEM((half_rows + 1, 2 * width, LANES), F32),
        scratch_shapes=[
            pltpu.VMEM((half_rows * (width + PAD), LANES), F32),
            pltpu.VMEM((width * (2 * half_rows + PAD), LANES), F32),
        ],
        compiler_params=pltpu.CompilerParams(vmem_limit_bytes=16 << 20),
        cost_estimate=pl.CostEstimate(
            flops=2 * LANES * (first.size * width + second.size * half_rows),
            bytes_accessed=2 * got.size + 8 * half_rows * width * LANES,
            transcendentals=0,
        ),
        name="forward",
    )(got, first, second, turn)


def inverse_kernel(place_ref, spec_ref, turn_ref, matrices_hbm, *refs, devices_seq, early):
    distances = first = early_distances(devices_seq)
    if not early:
        distances = [d for d in range(devices_seq // 2) if d not in first]
    filter_hbm, refs = refs[:devices_seq], refs[devices_seq:]
    if early:
        real_ref, imag_ref, filter_ref, matrices_ref, matrices_sem, filter_sems = refs
    else:
        (_, _, out_ref, real_ref, imag_ref) = refs[:5]
        filter_ref, matrices_ref, matrices_sem, filter_sems, lead_ref, rows_ref = refs[5:]
    width = turn_ref.shape[1]
    half_rows = spec_ref.shape[0] - 1
    pitch = width + PAD
    per_source = 8
    left = left_lanes(width)
    top_block = half_rows // per_source

    place = place_ref[0]
    upper = place >= top_block

    def block_of(distance):
        source = place ^ distance
        return jnp.where(upper, devices_seq - 1 - source, source)

    def arrival(distance, count=None):
        rows = pl.ds(0, count or filter_ref.shape[1])
        return pltpu.make_async_copy(
            filter_hbm[distance].at[rows],
            filter_ref.at[distance, rows],
            filter_sems.at[distance],
        )

    def pair_of(distance):
        return distance, devices_seq - 1 - distance

    matrices = pltpu.make_async_copy(matrices_hbm, matrices_ref, matrices_sem)
    matrices.start()
    for distance in distances:
        for near in pair_of(distance):
            arrival(near).start()
    if not early:
        for distance in first:
            for near in pair_of(distance):
                arrival(near, width).start()
    matrices.wait()
    third_matrix = matrices_ref[: 2 * width]
    last_matrix = matrices_ref[2 * width :]

    def response_of(distance, at):
        far = devices_seq - 1 - distance
        row = pl.ds(at * width, width)
        mirror = pl.ds((per_source - at) * width, width)
        lower = jnp.where(upper, filter_ref[far, row], filter_ref[distance, row])
        higher = jnp.where(upper, filter_ref[distance, mirror], filter_ref[far, mirror])
        return lower.astype(F32) + higher.astype(F32)

    def filtered(spec, response):
        turned = pltpu.roll(response, HALF, 1)
        real_part = jnp.where(left, response, turned)
        imag_part = jnp.where(left, turned, response)
        real, imag = spec[:width], spec[width:]
        return jnp.concatenate(
            [real * real_part - imag * imag_part, real * imag_part + imag * real_part], 0
        ).astype(BF16)

    def transform(values):
        return jnp.dot(
            third_matrix, jnp.concatenate([values, values], 0), preferred_element_type=F32
        )

    def turned_back(values, block, u):
        cosine = turn_ref[block, :, u : u + 1]
        sine = turn_ref[block, :, 8 + u : 9 + u]
        real, imag = values[:width], values[width:]
        return real * cosine - imag * sine, real * sine + imag * cosine

    def third_stage(slots):
        values = jnp.concatenate(
            [filtered(spec_ref[low], response) for low, response, _, _ in slots], 1
        )
        done = transform(values)
        results = []
        for v, (_, _, block, u) in enumerate(slots):
            results.append(turned_back(done[:, v * LANES : (v + 1) * LANES], block, u))
        return results

    def keep(low, values):
        at = low * pitch if isinstance(low, int) else pl.multiple_of(low * pitch, PAD)
        real_ref[pl.ds(at, width), :] = values[0]
        imag_ref[pl.ds(at, width), :] = values[1]

    for distance in distances:
        block = block_of(distance)
        for near in pair_of(distance):
            arrival(near).wait()
        slots = [
            (per_source * block + v, response_of(distance, v), block, v)
            for v in range(1, per_source)
        ]
        for at in range(0, len(slots), 2):
            pair = slots[at : at + 2]
            for slot, values in zip(pair, third_stage(pair)):
                keep(slot[0], values)
    if early:
        return
    for distance in first:
        for near in pair_of(distance):
            arrival(near, width).wait()
    for distance in range(devices_seq):
        lead_ref[place ^ distance] = filter_ref[distance, :width].astype(F32)
    slots = [(0, lead_ref[0], 0, 0), (half_rows, lead_ref[top_block], top_block, 0)]
    first, middle = third_stage(slots)
    keep(0, (first[0], middle[0]))
    slots = [
        (per_source * block, lead_ref[block] + lead_ref[devices_seq - block], block, 0)
        for block in range(1, top_block)
    ]
    for at in range(0, len(slots), 2):
        pair = slots[at : at + 2]
        for slot, values in zip(pair, third_stage(pair)):
            keep(slot[0], values)

    def last_stage(step, carry):
        for u in range(0, 8, 2):
            pair = []
            for v in range(u, u + 2):
                rows = pl.ds(8 * step + v, half_rows, stride=pitch)
                pair.append(jnp.concatenate([real_ref[rows, :], imag_ref[rows, :]], 0).astype(BF16))
            pair = jnp.concatenate(pair, 1)
            done = jnp.dot(
                last_matrix, jnp.concatenate([pair, pair], 0), preferred_element_type=F32
            )
            for v in range(2):
                rows = pl.ds(8 * step + u + v, half_rows, stride=pitch)
                rows_ref[rows, :] = done[:, v * LANES : (v + 1) * LANES]
        return carry

    lax.fori_loop(0, width // 8, last_stage, 0, unroll=True)
    lines = out_ref.shape[2] // width
    for source in range(devices_seq):
        for line in range(lines):
            first, second = swap_halves(
                *(
                    rows_ref[pl.ds(((2 * source + half) * lines + line) * pitch, width), :]
                    for half in range(2)
                )
            )
            at = pl.ds(line * width, width)
            out_ref[source, 0, at, :] = first.astype(BF16)
            out_ref[source, 1, at, :] = second.astype(BF16)


def inverse(spectrum, arrived, devices_seq, piece):
    width = spectrum.shape[1] // 2
    half_rows = spectrum.shape[0] - 1
    _, _, matrices, turn = tables(half_rows, width)
    stage = pltpu.VMEM((half_rows * (width + PAD), LANES), F32)
    block = arrived[0].shape

    def in_hbm(operand):
        return pltpu.with_memory_space_constraint(jnp.asarray(operand), pltpu.HBM)

    def in_vmem(operand):
        return pltpu.with_memory_space_constraint(operand, pltpu.VMEM)

    vmem = pl.BlockSpec(memory_space=pltpu.VMEM)
    specs = [pl.BlockSpec(memory_space=pltpu.SMEM), vmem, vmem] + [
        pl.BlockSpec(memory_space=pltpu.HBM)
    ] * (1 + devices_seq)
    scratch = [
        pltpu.VMEM((devices_seq, *block), BF16),
        pltpu.VMEM(matrices.shape, BF16),
        pltpu.SemaphoreType.DMA,
        pltpu.SemaphoreType.DMA((devices_seq,)),
    ]

    def call(early, more_in, out_shape, more_scratch, aliases):
        used = [d for e in early_distances(devices_seq) for d in (e, devices_seq - 1 - e)]
        rows = [
            in_hbm(arrived[d] if d in used or not early else arrived[used[0]])
            for d in range(devices_seq)
        ]
        operands = [lax.axis_index("seq").reshape(1), in_vmem(spectrum), turn, in_hbm(matrices)]
        operands += rows + more_in
        return pl.pallas_call(
            functools.partial(inverse_kernel, devices_seq=devices_seq, early=early),
            out_shape=out_shape,
            in_specs=specs + [vmem] * len(more_in),
            out_specs=[vmem] * len(out_shape),
            scratch_shapes=scratch + more_scratch,
            input_output_aliases={
                len(specs) + at: to for at, to in enumerate(aliases)
            },
            compiler_params=pltpu.CompilerParams(vmem_limit_bytes=20 << 20),
            cost_estimate=pl.CostEstimate(
                flops=LANES * matrices.size * width,
                bytes_accessed=2 * devices_seq * block[0] * block[1],
                transcendentals=0,
            ),
            name="inverse_early" if early else "inverse_late",
        )(*operands)

    real, imag = call(True, [], [stage, stage], [], [])
    return call(
        False,
        [in_vmem(real), in_vmem(imag)],
        [jax.ShapeDtypeStruct((devices_seq, 2, piece, LANES), BF16), stage, stage],
        [pltpu.VMEM((devices_seq, width, LANES), F32), stage],
        [1, 2],
    )[0]


def mix_kernel(conv_ref, signal_ref, gate_ref, out_gate_ref, gain_ref, out_hbm, out_ref, sems):
    rows = signal_ref.shape[0] // 2
    pieces = sems.shape[0]
    wide = signal_ref.shape[1] // pieces

    def leave(piece):
        lanes = pl.ds(piece * wide, wide)
        return pltpu.make_async_copy(out_ref.at[:, lanes], out_hbm.at[:, lanes], sems.at[piece])

    for piece in range(pieces):
        for start in range(piece * wide, (piece + 1) * wide, LANES):
            lanes = pl.ds(start, LANES)
            gain = gain_ref[:, lanes]
            group, seq = divmod(start // HALF, conv_ref.shape[0])
            halves = swap_halves(
                conv_ref[seq, group].astype(F32), conv_ref[seq + 1, group].astype(F32)
            )
            for half, convolved in enumerate(halves):
                at = pl.ds(half * rows, rows)
                gated = signal_ref[at, lanes].astype(F32) * gate_ref[at, lanes].astype(F32)
                gated = gated.astype(BF16).astype(F32)
                mixed = out_gate_ref[at, lanes].astype(F32) * (convolved + gain * gated)
                out_ref[at, lanes] = mixed.astype(BF16)
        leave(piece).start()
    for piece in range(pieces):
        leave(piece).wait()


def mix(conv, signal, input_gate, output_gate, skip_gain):
    return pl.pallas_call(
        mix_kernel,
        out_shape=jax.ShapeDtypeStruct(signal.shape, BF16),
        in_specs=[pl.BlockSpec(memory_space=pltpu.VMEM)] * 5,
        out_specs=pl.BlockSpec(memory_space=pltpu.HBM),
        scratch_shapes=[pltpu.VMEM(signal.shape, BF16), pltpu.SemaphoreType.DMA((PIECES,))],
        compiler_params=pltpu.CompilerParams(vmem_limit_bytes=16 << 20),
        cost_estimate=pl.CostEstimate(
            flops=4 * signal.size, bytes_accessed=10 * signal.size, transcendentals=0
        ),
        name="mix",
    )(conv, signal, input_gate, output_gate, skip_gain[None, :])


def spread_kernels(signal, input_gate, output_gate, filter_spectrum, skip_gain):
    devices_seq = lax.axis_size("seq")
    width = filter_spectrum.shape[2]

    def pairs(values):
        return exchange(values.reshape(-1, *values.shape[2:]), PAIRS).reshape(values.shape)

    got = pairs(pack_input(signal, input_gate, devices_seq))
    packed = pack_filter(filter_spectrum, devices_seq)
    arrived = [packed[0]] + [swap_with(packed[d], d) for d in range(1, devices_seq)]
    spectrum = forward(got, devices_seq, width)
    conv = inverse(spectrum, arrived, devices_seq, signal.shape[0] // 2)
    return mix(pairs(conv), signal, input_gate, output_gate, skip_gain)


def angle_table(rows_count, cols_count, length):
    row_index = lax.iota(jnp.int32, rows_count)
    col_index = lax.iota(jnp.int32, cols_count)
    product = row_index[:, None] * col_index[None, :] % length
    angles = product.astype(jnp.float32) * (2.0 * math.pi / length)
    return (jnp.cos(angles), jnp.sin(angles))


def contract_first(matrix, values):
    return jnp.einsum("kn,nbc->kbc", matrix, values, precision=lax.Precision.HIGH)


def contract_second(matrix, values):
    return jnp.einsum("kn,anc->akc", matrix, values, precision=lax.Precision.HIGH)


def convolve(signal_rows, spectra_real, spectra_imag):
    half_rows, width, _ = signal_rows.shape
    full_rows = 2 * half_rows
    length = full_rows * width
    cos_one, sin_one = angle_table(full_rows, half_rows, full_rows)
    cos_two, sin_two = angle_table(width, width, width)
    turn_cos, turn_sin = angle_table(full_rows, width, length)
    turn_cos = turn_cos[:, :, None]
    turn_sin = turn_sin[:, :, None]
    first_real = contract_first(cos_one, signal_rows)
    first_imag = -contract_first(sin_one, signal_rows)
    twist_real = first_real * turn_cos + first_imag * turn_sin
    twist_imag = first_imag * turn_cos - first_real * turn_sin
    spec_real = contract_second(cos_two, twist_real) + contract_second(sin_two, twist_imag)
    spec_imag = contract_second(cos_two, twist_imag) - contract_second(sin_two, twist_real)
    prod_real = spec_real * spectra_real - spec_imag * spectra_imag
    prod_imag = spec_real * spectra_imag + spec_imag * spectra_real
    back_real = contract_second(cos_two, prod_real) - contract_second(sin_two, prod_imag)
    back_imag = contract_second(sin_two, prod_real) + contract_second(cos_two, prod_imag)
    rotated_real = back_real * turn_cos - back_imag * turn_sin
    rotated_imag = back_real * turn_sin + back_imag * turn_cos
    summed = contract_first(cos_one.T, rotated_real) - contract_first(sin_one.T, rotated_imag)
    return summed * (1.0 / length)


def spread_plain(signal, input_gate, output_gate, filter_spectrum, skip_gain):
    tok_rows, channels = signal.shape
    groups = lax.axis_size("groups")
    devices_seq = lax.axis_size("seq")
    parts = groups * devices_seq
    width = channels // parts
    low, high = filter_spectrum.shape[1:3]
    share = low // groups
    gated_input = (input_gate.astype(jnp.float32) * signal.astype(jnp.float32)).astype(jnp.bfloat16)

    sent = gated_input.reshape(tok_rows, parts, width).transpose(1, 0, 2).reshape(parts, -1, 128)
    got = exchange(sent).reshape(groups, devices_seq, tok_rows, width)
    rows = got.transpose(1, 2, 0, 3).reshape(-1, high, groups * width)

    mine = lax.dynamic_slice_in_dim(filter_spectrum, lax.axis_index("groups") * share, share, axis=1)
    mine = mine.astype(jnp.bfloat16).reshape(2, share, high, parts, width)
    mine = mine.transpose(3, 0, 1, 2, 4).reshape(parts, -1, 128)
    spectra = exchange(mine).reshape(groups, devices_seq, 2, share, high, width)
    spectra = spectra.transpose(2, 1, 0, 3, 4, 5).reshape(2, -1, high, 1, width)
    spectra = jnp.broadcast_to(spectra, spectra.shape[:3] + (groups, width))
    spectra = spectra.reshape(2, -1, high, groups * width).astype(jnp.float32)

    conv = convolve(rows.astype(jnp.float32), spectra[0], spectra[1]).astype(jnp.bfloat16)
    conv = conv.reshape(devices_seq, tok_rows, groups, width).transpose(2, 0, 1, 3)
    back = exchange(conv.reshape(parts, -1, 128)).reshape(parts, tok_rows, width)
    convolved = back.transpose(1, 0, 2).reshape(tok_rows, channels).astype(jnp.float32)
    mixed_out = output_gate.astype(jnp.float32) * (
        convolved + skip_gain[None, :] * gated_input.astype(jnp.float32)
    )
    return mixed_out.astype(jnp.bfloat16)


def on_device(signal, input_gate, output_gate, filter_spectrum, skip_gain):
    groups = lax.axis_size("groups")
    devices_seq = lax.axis_size("seq")
    tok_rows, channels = signal.shape
    low, high = filter_spectrum.shape[1:3]
    fits = (
        groups == 2
        and channels == groups * devices_seq * HALF
        and low == 8
        and tok_rows == low * high // 2
        and tok_rows % 32 == 0
        and devices_seq >= 4
        and devices_seq & (devices_seq - 1) == 0
    )
    plan = spread_kernels if fits else spread_plain
    return plan(signal, input_gate, output_gate, filter_spectrum, skip_gain)


def solution(mesh):
    return jax.shard_map(
        on_device,
        mesh=mesh,
        in_specs=(P(EVERY, None), P(EVERY, None), P(EVERY, None), P(None, "seq", None, None), P()),
        out_specs=P(EVERY, None),
        check_vma=False,
    )
```

```python
import functools
import math

import jax
import jax.numpy as jnp
import ml_dtypes
import numpy as np
from jax import lax
from jax.experimental import pallas as pl
from jax.experimental.pallas import tpu as pltpu
from jax.sharding import PartitionSpec as P

EVERY = ("groups", "seq")
PAIRS = ("seq", "groups")
LANES = 128
HALF = LANES // 2
PAD = 8
PIECES = 4
BF16 = jnp.bfloat16
F32 = jnp.float32


def exchange(values, axes=EVERY):
    return lax.all_to_all(values, axes, split_axis=0, concat_axis=0, tiled=True)


def left_lanes(rows):
    return lax.broadcasted_iota(jnp.int32, (rows, LANES), 1) < HALF


def swap_halves(first, second):
    left = left_lanes(first.shape[0])
    return (
        jnp.where(left, first, pltpu.roll(second, HALF, 1)),
        jnp.where(left, pltpu.roll(first, HALF, 1), second),
    )


def hi_lo(matrix):
    high = matrix.astype(ml_dtypes.bfloat16)
    low = (matrix - high.astype(np.float64)).astype(ml_dtypes.bfloat16)
    return high, low


@functools.lru_cache(None)
def tables(half_rows, width):
    full_rows = 2 * half_rows
    length = full_rows * width
    low_index = np.arange(half_rows)
    angle = 2 * np.pi * (np.outer(low_index, low_index) % full_rows) / full_rows
    real_part, imag_part = np.cos(angle), -np.sin(angle)
    imag_part[0] = 1.0 - 2.0 * (low_index % 2)
    first = np.concatenate([real_part, imag_part], 0)
    last = first.T / length
    inner = np.arange(width)
    angle = 2 * np.pi * (np.outer(inner, inner) % width) / width
    cosine, sine = np.cos(angle), np.sin(angle)
    second = np.block([[cosine, sine], [-sine, cosine]])
    third = np.block([[cosine, -sine], [sine, cosine]])
    first_hi, first_lo = hi_lo(first)
    second_hi, second_lo = hi_lo(second)
    third_hi, third_lo = hi_lo(third)
    last_hi, last_lo = hi_lo(last)
    turn = np.zeros((half_rows // 8 + 1, width, LANES), np.float32)
    for block in range(half_rows // 8 + 1):
        angle = 2 * np.pi * np.outer(inner, 8 * block + np.arange(8)) / length
        turn[block, :, :8] = np.cos(angle)
        turn[block, :, 8:16] = np.sin(angle)
    return (
        np.concatenate([first_hi, first_lo], 1),
        np.concatenate([second_hi, second_lo, second_hi], 1),
        np.block([[third_hi, third_lo], [last_hi, last_lo]]),
        turn,
    )


def pack_input_kernel(signal_ref, gate_ref, out_ref):
    rows = signal_ref.shape[0] // 2
    for block in range(signal_ref.shape[1] // LANES):
        lanes = pl.ds(block * LANES, LANES)
        gated = signal_ref[:, lanes].astype(F32) * gate_ref[:, lanes].astype(F32)
        first, second = swap_halves(gated[:rows], gated[rows:])
        out_ref[2 * block, 0] = first.astype(BF16)
        out_ref[2 * block + 1, 0] = second.astype(BF16)


def pack_input(signal, input_gate, devices_seq):
    tok_rows, channels = signal.shape
    wide = channels // 2
    return pl.pallas_call(
        pack_input_kernel,
        out_shape=jax.ShapeDtypeStruct((devices_seq, 2, tok_rows // 2, LANES), BF16),
        grid=(2,),
        in_specs=[pl.BlockSpec((tok_rows, wide), lambda b: (0, b))] * 2,
        out_specs=pl.BlockSpec((devices_seq, 1, tok_rows // 2, LANES), lambda b: (0, b, 0, 0)),
        cost_estimate=pl.CostEstimate(
            flops=signal.size, bytes_accessed=6 * signal.size, transcendentals=0
        ),
        name="pack_input",
    )(signal, input_gate)


def pack_filter_kernel(place_ref, filter_ref, *refs, middle):
    out_refs, chunks_ref = refs[:-1], refs[-1]
    low_count, width = filter_ref.shape[1:3]
    chunks = chunks_ref.shape[0]
    seq = place_ref[1]
    row = lax.broadcasted_iota(jnp.int32, (width, width), 0)
    col = lax.broadcasted_iota(jnp.int32, (width, width), 1)
    for low in range(low_count):
        mirrored = seq * low_count + low > middle
        order = jnp.where(col == jnp.where(mirrored, width - 1 - row, row), 1.0, 0.0).astype(BF16)
        sign = jnp.where(mirrored, -1.0, 1.0).astype(F32)
        for block in range(chunks // 2):
            lanes = pl.ds(block * LANES, LANES)
            both = jnp.concatenate(
                [filter_ref[0, low, :, lanes], filter_ref[1, low, :, lanes]], 1
            ).astype(BF16)
            both = jnp.dot(order, both, preferred_element_type=F32)
            halves = swap_halves(both[:, :LANES], sign * both[:, LANES:])
            rows = pl.ds(low * width, width)
            for half in range(2):
                near = (2 * block + half) ^ (seq % chunks)
                chunks_ref[near, rows, :] = halves[half].astype(BF16)
    for step in range(len(out_refs) // chunks):

        @pl.when(pl.program_id(0) == step)
        def _():
            for near in range(chunks):
                out_refs[chunks * step + near][...] = chunks_ref[near]


def pack_filter(filter_spectrum, devices_seq):
    _, low, width, channels = filter_spectrum.shape
    chunks = 4
    wide = chunks * HALF
    steps = devices_seq // chunks
    size = low * width * channels // 2
    block = (low * width, LANES)

    def lanes_of(step, place):
        return (0, 0, 0, place[0] * steps + ((place[1] // chunks) ^ step))

    return pl.pallas_call(
        functools.partial(pack_filter_kernel, middle=low * devices_seq // 2),
        out_shape=[pltpu.HBM(block, BF16)] * devices_seq,
        grid_spec=pltpu.PrefetchScalarGridSpec(
            num_scalar_prefetch=1,
            grid=(steps,),
            in_specs=[pl.BlockSpec((2, low, width, wide), lanes_of)],
            out_specs=[pl.BlockSpec(block, lambda step, place: (0, 0))] * devices_seq,
            scratch_shapes=[pltpu.VMEM((chunks, *block), BF16)],
        ),
        compiler_params=pltpu.CompilerParams(vmem_limit_bytes=16 << 20),
        cost_estimate=pl.CostEstimate(
            flops=4 * width * size, bytes_accessed=12 * size, transcendentals=0
        ),
        name="pack_filter",
    )(
        jnp.stack([lax.axis_index("groups"), lax.axis_index("seq")]),
        pltpu.with_memory_space_constraint(filter_spectrum, pltpu.HBM),
    )


def early_distances(devices_seq):
    return list(reversed(range(devices_seq // 4, devices_seq // 2)))


def swap_with(values, distance):
    count = lax.axis_size("seq")
    return lax.ppermute(values, "seq", [(i, i ^ distance) for i in range(count)])


def split_bf16(values):
    high = values.astype(BF16)
    return high, (values - high.astype(F32)).astype(BF16)


def forward_kernel(
    got_ref, first_ref, second_ref, turn_ref, out_ref, rows_ref, stage_ref, *, devices_seq
):
    width = turn_ref.shape[1]
    half_rows = out_ref.shape[0] - 1
    full_rows = 2 * half_rows
    pitch = width + PAD
    tall = full_rows + PAD
    lines = got_ref.shape[2] // width
    for source in range(devices_seq):
        for line in range(lines):
            at = pl.ds(line * width, width)
            halves = swap_halves(
                got_ref[source, 0, at, :].astype(F32), got_ref[source, 1, at, :].astype(F32)
            )
            for half in range(2):
                row = (2 * source + half) * lines + line
                rows_ref[pl.ds(row * pitch, width), :] = halves[half]
    first_matrix = first_ref[...]
    second_matrix = second_ref[...]

    def first_stage(step, carry):
        for u in range(0, 8, 2):
            pair = jnp.concatenate(
                [
                    rows_ref[pl.ds(8 * step + u + v, half_rows, stride=pitch), :].astype(BF16)
                    for v in range(2)
                ],
                1,
            )
            pair = jnp.concatenate([pair, pair], 0)
            done = jnp.dot(first_matrix, pair, preferred_element_type=F32)
            for v in range(2):
                at = pl.multiple_of((8 * step + u + v) * tall, PAD)
                stage_ref[pl.ds(at, full_rows), :] = done[:, v * LANES : (v + 1) * LANES]
        return carry

    lax.fori_loop(0, width // 8, first_stage, 0)

    def turned(real, imag, block, u):
        cosine = turn_ref[block, :, u : u + 1]
        sine = turn_ref[block, :, 8 + u : 9 + u]
        if imag is None:
            return jnp.concatenate([real * cosine, -real * sine], 0)
        return jnp.concatenate([real * cosine + imag * sine, imag * cosine - real * sine], 0)

    def transform(values):
        high, low = split_bf16(values)
        return jnp.dot(
            second_matrix, jnp.concatenate([high, high, low], 0), preferred_element_type=F32
        )

    def second_stage(block, carry):
        for u in range(0, 8, 2):
            pair = []
            for v in range(u, u + 2):
                at = 8 * block + v
                real = stage_ref[pl.ds(at, width, stride=tall), :]
                imag = stage_ref[pl.ds(half_rows + at, width, stride=tall), :]
                if v == 0:
                    imag = imag * jnp.where(block == 0, 0.0, 1.0).astype(F32)
                pair.append(turned(real, imag, block, v))
            done = transform(jnp.concatenate(pair, 1))
            for v in range(2):
                out_ref[8 * block + u + v] = done[:, v * LANES : (v + 1) * LANES]
        return carry

    lax.fori_loop(0, half_rows // 8, second_stage, 0)
    real = stage_ref[pl.ds(half_rows, width, stride=tall), :]
    out_ref[half_rows] = transform(turned(real, None, half_rows // 8, 0))


def forward(got, devices_seq, width):
    half_rows = got.size // (LANES * width)
    first, second, _, turn = tables(half_rows, width)
    return pl.pallas_call(
        functools.partial(forward_kernel, devices_seq=devices_seq),
        out_shape=pltpu.VMEM((half_rows + 1, 2 * width, LANES), F32),
        scratch_shapes=[
            pltpu.VMEM((half_rows * (width + PAD), LANES), F32),
            pltpu.VMEM((width * (2 * half_rows + PAD), LANES), F32),
        ],
        compiler_params=pltpu.CompilerParams(vmem_limit_bytes=16 << 20),
        cost_estimate=pl.CostEstimate(
            flops=2 * LANES * (first.size * width + second.size * half_rows),
            bytes_accessed=2 * got.size + 8 * half_rows * width * LANES,
            transcendentals=0,
        ),
        name="forward",
    )(got, first, second, turn)


def inverse_kernel(place_ref, spec_ref, turn_ref, matrices_hbm, *refs, devices_seq, early):
    distances = first = early_distances(devices_seq)
    if not early:
        distances = [d for d in range(devices_seq // 2) if d not in first]
    filter_hbm, refs = refs[:devices_seq], refs[devices_seq:]
    if early:
        real_ref, imag_ref, filter_ref, matrices_ref, matrices_sem, filter_sems = refs
    else:
        (_, _, out_ref, real_ref, imag_ref) = refs[:5]
        filter_ref, matrices_ref, matrices_sem, filter_sems, lead_ref, rows_ref = refs[5:]
    width = turn_ref.shape[1]
    half_rows = spec_ref.shape[0] - 1
    pitch = width + PAD
    per_source = 8
    left = left_lanes(width)
    top_block = half_rows // per_source

    place = place_ref[0]
    upper = place >= top_block

    def block_of(distance):
        source = place ^ distance
        return jnp.where(upper, devices_seq - 1 - source, source)

    def arrival(distance, count=None):
        rows = pl.ds(0, count or filter_ref.shape[1])
        return pltpu.make_async_copy(
            filter_hbm[distance].at[rows],
            filter_ref.at[distance, rows],
            filter_sems.at[distance],
        )

    def pair_of(distance):
        return distance, devices_seq - 1 - distance

    matrices = pltpu.make_async_copy(matrices_hbm, matrices_ref, matrices_sem)
    matrices.start()
    for distance in distances:
        for near in pair_of(distance):
            arrival(near).start()
    if not early:
        for distance in first:
            for near in pair_of(distance):
                arrival(near, width).start()
    matrices.wait()
    third_matrix = matrices_ref[: 2 * width]
    last_matrix = matrices_ref[2 * width :]

    def response_of(distance, at):
        far = devices_seq - 1 - distance
        row = pl.ds(at * width, width)
        mirror = pl.ds((per_source - at) * width, width)
        lower = jnp.where(upper, filter_ref[far, row], filter_ref[distance, row])
        higher = jnp.where(upper, filter_ref[distance, mirror], filter_ref[far, mirror])
        return lower.astype(F32) + higher.astype(F32)

    def filtered(spec, response):
        turned = pltpu.roll(response, HALF, 1)
        real_part = jnp.where(left, response, turned)
        imag_part = jnp.where(left, turned, response)
        real, imag = spec[:width], spec[width:]
        return jnp.concatenate(
            [real * real_part - imag * imag_part, real * imag_part + imag * real_part], 0
        ).astype(BF16)

    def transform(values):
        return jnp.dot(
            third_matrix, jnp.concatenate([values, values], 0), preferred_element_type=F32
        )

    def turned_back(values, block, u):
        cosine = turn_ref[block, :, u : u + 1]
        sine = turn_ref[block, :, 8 + u : 9 + u]
        real, imag = values[:width], values[width:]
        return real * cosine - imag * sine, real * sine + imag * cosine

    def third_stage(slots):
        values = jnp.concatenate(
            [filtered(spec_ref[low], response) for low, response, _, _ in slots], 1
        )
        done = transform(values)
        results = []
        for v, (_, _, block, u) in enumerate(slots):
            results.append(turned_back(done[:, v * LANES : (v + 1) * LANES], block, u))
        return results

    def keep(low, values):
        at = low * pitch if isinstance(low, int) else pl.multiple_of(low * pitch, PAD)
        real_ref[pl.ds(at, width), :] = values[0]
        imag_ref[pl.ds(at, width), :] = values[1]

    for at in range(0, len(distances), 2):
        slots = []
        for distance in distances[at : at + 2]:
            block = block_of(distance)
            for near in pair_of(distance):
                arrival(near).wait()
            slots += [
                (per_source * block + v, response_of(distance, v), block, v)
                for v in range(1, per_source)
            ]
        for first_slot in range(0, len(slots), 2):
            pair = slots[first_slot : first_slot + 2]
            for slot, values in zip(pair, third_stage(pair)):
                keep(slot[0], values)
    if early:
        return
    for distance in first:
        for near in pair_of(distance):
            arrival(near, width).wait()
    for distance in range(devices_seq):
        lead_ref[place ^ distance] = filter_ref[distance, :width].astype(F32)
    slots = [(0, lead_ref[0], 0, 0), (half_rows, lead_ref[top_block], top_block, 0)]
    first, middle = third_stage(slots)
    keep(0, (first[0], middle[0]))
    slots = [
        (per_source * block, lead_ref[block] + lead_ref[devices_seq - block], block, 0)
        for block in range(1, top_block)
    ]
    for at in range(0, len(slots), 2):
        pair = slots[at : at + 2]
        for slot, values in zip(pair, third_stage(pair)):
            keep(slot[0], values)

    def last_stage(step, carry):
        for u in range(0, 8, 2):
            pair = []
            for v in range(u, u + 2):
                rows = pl.ds(8 * step + v, half_rows, stride=pitch)
                pair.append(jnp.concatenate([real_ref[rows, :], imag_ref[rows, :]], 0).astype(BF16))
            pair = jnp.concatenate(pair, 1)
            done = jnp.dot(
                last_matrix, jnp.concatenate([pair, pair], 0), preferred_element_type=F32
            )
            for v in range(2):
                rows = pl.ds(8 * step + u + v, half_rows, stride=pitch)
                rows_ref[rows, :] = done[:, v * LANES : (v + 1) * LANES]
        return carry

    lax.fori_loop(0, width // 8, last_stage, 0, unroll=True)
    lines = out_ref.shape[2] // width
    for source in range(devices_seq):
        for line in range(lines):
            first, second = swap_halves(
                *(
                    rows_ref[pl.ds(((2 * source + half) * lines + line) * pitch, width), :]
                    for half in range(2)
                )
            )
            at = pl.ds(line * width, width)
            out_ref[source, 0, at, :] = first.astype(BF16)
            out_ref[source, 1, at, :] = second.astype(BF16)


def inverse(spectrum, arrived, devices_seq, piece):
    width = spectrum.shape[1] // 2
    half_rows = spectrum.shape[0] - 1
    _, _, matrices, turn = tables(half_rows, width)
    stage = pltpu.VMEM((half_rows * (width + PAD), LANES), F32)
    block = arrived[0].shape

    def in_hbm(operand):
        return pltpu.with_memory_space_constraint(jnp.asarray(operand), pltpu.HBM)

    def in_vmem(operand):
        return pltpu.with_memory_space_constraint(operand, pltpu.VMEM)

    vmem = pl.BlockSpec(memory_space=pltpu.VMEM)
    specs = [pl.BlockSpec(memory_space=pltpu.SMEM), vmem, vmem] + [
        pl.BlockSpec(memory_space=pltpu.HBM)
    ] * (1 + devices_seq)
    scratch = [
        pltpu.VMEM((devices_seq, *block), BF16),
        pltpu.VMEM(matrices.shape, BF16),
        pltpu.SemaphoreType.DMA,
        pltpu.SemaphoreType.DMA((devices_seq,)),
    ]

    def call(early, more_in, out_shape, more_scratch, aliases):
        used = [d for e in early_distances(devices_seq) for d in (e, devices_seq - 1 - e)]
        rows = [
            in_hbm(arrived[d] if d in used or not early else arrived[used[0]])
            for d in range(devices_seq)
        ]
        operands = [lax.axis_index("seq").reshape(1), in_vmem(spectrum), turn, in_hbm(matrices)]
        operands += rows + more_in
        return pl.pallas_call(
            functools.partial(inverse_kernel, devices_seq=devices_seq, early=early),
            out_shape=out_shape,
            in_specs=specs + [vmem] * len(more_in),
            out_specs=[vmem] * len(out_shape),
            scratch_shapes=scratch + more_scratch,
            input_output_aliases={
                len(specs) + at: to for at, to in enumerate(aliases)
            },
            compiler_params=pltpu.CompilerParams(vmem_limit_bytes=20 << 20),
            cost_estimate=pl.CostEstimate(
                flops=LANES * matrices.size * width,
                bytes_accessed=2 * devices_seq * block[0] * block[1],
                transcendentals=0,
            ),
            name="inverse_early" if early else "inverse_late",
        )(*operands)

    real, imag = call(True, [], [stage, stage], [], [])
    return call(
        False,
        [in_vmem(real), in_vmem(imag)],
        [jax.ShapeDtypeStruct((devices_seq, 2, piece, LANES), BF16), stage, stage],
        [pltpu.VMEM((devices_seq, width, LANES), F32), stage],
        [1, 2],
    )[0]


def mix_kernel(conv_ref, signal_ref, gate_ref, out_gate_ref, gain_ref, out_hbm, out_ref, sems):
    rows = signal_ref.shape[0] // 2
    pieces = sems.shape[0]
    wide = signal_ref.shape[1] // pieces

    def leave(piece):
        lanes = pl.ds(piece * wide, wide)
        return pltpu.make_async_copy(out_ref.at[:, lanes], out_hbm.at[:, lanes], sems.at[piece])

    for piece in range(pieces):
        for start in range(piece * wide, (piece + 1) * wide, LANES):
            lanes = pl.ds(start, LANES)
            gain = gain_ref[:, lanes]
            group, seq = divmod(start // HALF, conv_ref.shape[0])
            halves = swap_halves(
                conv_ref[seq, group].astype(F32), conv_ref[seq + 1, group].astype(F32)
            )
            for half, convolved in enumerate(halves):
                at = pl.ds(half * rows, rows)
                gated = signal_ref[at, lanes].astype(F32) * gate_ref[at, lanes].astype(F32)
                gated = gated.astype(BF16).astype(F32)
                mixed = out_gate_ref[at, lanes].astype(F32) * (convolved + gain * gated)
                out_ref[at, lanes] = mixed.astype(BF16)
        leave(piece).start()
    for piece in range(pieces):
        leave(piece).wait()


def mix(conv, signal, input_gate, output_gate, skip_gain):
    return pl.pallas_call(
        mix_kernel,
        out_shape=jax.ShapeDtypeStruct(signal.shape, BF16),
        in_specs=[pl.BlockSpec(memory_space=pltpu.VMEM)] * 5,
        out_specs=pl.BlockSpec(memory_space=pltpu.HBM),
        scratch_shapes=[pltpu.VMEM(signal.shape, BF16), pltpu.SemaphoreType.DMA((PIECES,))],
        compiler_params=pltpu.CompilerParams(vmem_limit_bytes=16 << 20),
        cost_estimate=pl.CostEstimate(
            flops=4 * signal.size, bytes_accessed=10 * signal.size, transcendentals=0
        ),
        name="mix",
    )(conv, signal, input_gate, output_gate, skip_gain[None, :])


def spread_kernels(signal, input_gate, output_gate, filter_spectrum, skip_gain):
    devices_seq = lax.axis_size("seq")
    width = filter_spectrum.shape[2]

    def pairs(values):
        return exchange(values.reshape(-1, *values.shape[2:]), PAIRS).reshape(values.shape)

    got = pairs(pack_input(signal, input_gate, devices_seq))
    packed = pack_filter(filter_spectrum, devices_seq)
    arrived = [packed[0]] + [swap_with(packed[d], d) for d in range(1, devices_seq)]
    spectrum = forward(got, devices_seq, width)
    conv = inverse(spectrum, arrived, devices_seq, signal.shape[0] // 2)
    return mix(pairs(conv), signal, input_gate, output_gate, skip_gain)


def angle_table(rows_count, cols_count, length):
    row_index = lax.iota(jnp.int32, rows_count)
    col_index = lax.iota(jnp.int32, cols_count)
    product = row_index[:, None] * col_index[None, :] % length
    angles = product.astype(jnp.float32) * (2.0 * math.pi / length)
    return (jnp.cos(angles), jnp.sin(angles))


def contract_first(matrix, values):
    return jnp.einsum("kn,nbc->kbc", matrix, values, precision=lax.Precision.HIGH)


def contract_second(matrix, values):
    return jnp.einsum("kn,anc->akc", matrix, values, precision=lax.Precision.HIGH)


def convolve(signal_rows, spectra_real, spectra_imag):
    half_rows, width, _ = signal_rows.shape
    full_rows = 2 * half_rows
    length = full_rows * width
    cos_one, sin_one = angle_table(full_rows, half_rows, full_rows)
    cos_two, sin_two = angle_table(width, width, width)
    turn_cos, turn_sin = angle_table(full_rows, width, length)
    turn_cos = turn_cos[:, :, None]
    turn_sin = turn_sin[:, :, None]
    first_real = contract_first(cos_one, signal_rows)
    first_imag = -contract_first(sin_one, signal_rows)
    twist_real = first_real * turn_cos + first_imag * turn_sin
    twist_imag = first_imag * turn_cos - first_real * turn_sin
    spec_real = contract_second(cos_two, twist_real) + contract_second(sin_two, twist_imag)
    spec_imag = contract_second(cos_two, twist_imag) - contract_second(sin_two, twist_real)
    prod_real = spec_real * spectra_real - spec_imag * spectra_imag
    prod_imag = spec_real * spectra_imag + spec_imag * spectra_real
    back_real = contract_second(cos_two, prod_real) - contract_second(sin_two, prod_imag)
    back_imag = contract_second(sin_two, prod_real) + contract_second(cos_two, prod_imag)
    rotated_real = back_real * turn_cos - back_imag * turn_sin
    rotated_imag = back_real * turn_sin + back_imag * turn_cos
    summed = contract_first(cos_one.T, rotated_real) - contract_first(sin_one.T, rotated_imag)
    return summed * (1.0 / length)


def spread_plain(signal, input_gate, output_gate, filter_spectrum, skip_gain):
    tok_rows, channels = signal.shape
    groups = lax.axis_size("groups")
    devices_seq = lax.axis_size("seq")
    parts = groups * devices_seq
    width = channels // parts
    low, high = filter_spectrum.shape[1:3]
    share = low // groups
    gated_input = (input_gate.astype(jnp.float32) * signal.astype(jnp.float32)).astype(jnp.bfloat16)

    sent = gated_input.reshape(tok_rows, parts, width).transpose(1, 0, 2).reshape(parts, -1, 128)
    got = exchange(sent).reshape(groups, devices_seq, tok_rows, width)
    rows = got.transpose(1, 2, 0, 3).reshape(-1, high, groups * width)

    mine = lax.dynamic_slice_in_dim(filter_spectrum, lax.axis_index("groups") * share, share, axis=1)
    mine = mine.astype(jnp.bfloat16).reshape(2, share, high, parts, width)
    mine = mine.transpose(3, 0, 1, 2, 4).reshape(parts, -1, 128)
    spectra = exchange(mine).reshape(groups, devices_seq, 2, share, high, width)
    spectra = spectra.transpose(2, 1, 0, 3, 4, 5).reshape(2, -1, high, 1, width)
    spectra = jnp.broadcast_to(spectra, spectra.shape[:3] + (groups, width))
    spectra = spectra.reshape(2, -1, high, groups * width).astype(jnp.float32)

    conv = convolve(rows.astype(jnp.float32), spectra[0], spectra[1]).astype(jnp.bfloat16)
    conv = conv.reshape(devices_seq, tok_rows, groups, width).transpose(2, 0, 1, 3)
    back = exchange(conv.reshape(parts, -1, 128)).reshape(parts, tok_rows, width)
    convolved = back.transpose(1, 0, 2).reshape(tok_rows, channels).astype(jnp.float32)
    mixed_out = output_gate.astype(jnp.float32) * (
        convolved + skip_gain[None, :] * gated_input.astype(jnp.float32)
    )
    return mixed_out.astype(jnp.bfloat16)


def on_device(signal, input_gate, output_gate, filter_spectrum, skip_gain):
    groups = lax.axis_size("groups")
    devices_seq = lax.axis_size("seq")
    tok_rows, channels = signal.shape
    low, high = filter_spectrum.shape[1:3]
    fits = (
        groups == 2
        and channels == groups * devices_seq * HALF
        and low == 8
        and tok_rows == low * high // 2
        and tok_rows % 32 == 0
        and devices_seq >= 4
        and devices_seq & (devices_seq - 1) == 0
    )
    plan = spread_kernels if fits else spread_plain
    return plan(signal, input_gate, output_gate, filter_spectrum, skip_gain)


def solution(mesh):
    return jax.shard_map(
        on_device,
        mesh=mesh,
        in_specs=(P(EVERY, None), P(EVERY, None), P(EVERY, None), P(None, "seq", None, None), P()),
        out_specs=P(EVERY, None),
        check_vma=False,
    )
```
